256 devices in a mesh: group: 4 (over y), dev: 64 (over z, x, core).
Axes of the slice: x: 4, y: 4, z: 8, core: 2. Of those that a mesh axis runs over, the one named last changes fastest.
Arguments:
- source_emb: float32 [2048, 128, 128], P(('group', 'dev')), may hold values from -6 to 6
- target_emb: float32 [8192, 128, 128], P(('group', 'dev')), may hold values from -6 to 6
- source_mass: float32 [2048, 128], P(('group', 'dev')), may hold values from 0.5 to 2
- target_mass: float32 [8192, 128], P(('group', 'dev')), may hold values from 0.5 to 2
- cand_device: int32 [2048, 7], P(('group', 'dev')), may hold values from 0 to 63, all different within a row; in each aligned block of 8 rows (0 to 7, 8 to 15, ...) at most 2 rows name the same one
- cand_block: int32 [2048, 8], P(('group', 'dev')), may hold values from 0 to 31
Outputs:
- src_scale: float32 [2048, 128], P(('group', 'dev'))
- tgt_scale: float32 [8192, 128], P(('group', 'dev'))
The draws below stay inside these ranges and needn't reach their ends.
Inputs may be any that keep to these rules, and one draw needn't show every extreme that they name: `cand_device`: the seven devices named by one source block are distinct; among the 8 source blocks of one device, no device is named more than 2 times, and some device is named exactly 2 times.
All inputs are finite; a program needn't handle non-finite values.
Results may differ from the reference program's by a relative error of at most 0.0001.
Values sent between devices are 32-bit elements; how exact they have to be, the bound alone decides.
A program may use at most 64 MiB of HBM per device.

```python
import math
import jax
import jax.numpy as jnp
import numpy as np
from jax import lax

SB_DEV = 8
TB_DEV = 32
NODE_GROUP_SIZE = 128
FEATURE_LENGTH = 128
ITERS = 2
CAP = 2
NSB = 2048
NTB = 8192
N_GROUP = 4
N_DEV = 64


def touch_ends(result, own_key, least, high):
    longest = result.shape.index(max(result.shape))
    spots = []
    for shift in (0, 1):
        where = [jax.random.randint(jax.random.fold_in(own_key, axis), (), 0, length) for axis, length in enumerate(result.shape)]
        where[longest] = (where[longest] + shift) % result.shape[longest]
        spots.append(tuple(where))
    return result.at[spots[0]].set(least).at[spots[1]].set(high)


def block_levels(key, dims, split, least, top_value):
    def one(axis_at, shards_of):
        draws = jax.random.uniform(jax.random.fold_in(jax.random.fold_in(key, 6), axis_at), (shards_of,), jnp.float32, least / len(split), top_value / len(split))
        return jnp.repeat(jnp.exp(draws), dims[axis_at] // shards_of).reshape((-1,) + (1,) * (len(dims) - axis_at - 1))

    gain = one(*split[0])
    for cut in split[1:]:
        gain = gain * one(*cut)
    return gain


def shared_out(key, own, number, rows, count, top, reach, skew):
    sequence = jax.random.permutation(key, count)
    crowded, common = shares(count, rows * top, reach, skew, True), shares(count, rows * top, reach, skew, False)
    places = jnp.arange(count)

    def named(tallies, rotation):
        used = int((tallies > 0).sum())
        fixed = max(1, used // 4)
        moved = fixed + (places - fixed + rotation * (used - fixed)) % max(1, count - fixed)
        return jnp.zeros((count,), jnp.int32).at[sequence[jnp.where(places < fixed, places, moved)]].set(jnp.asarray(tallies, jnp.int32))

    tallies = jnp.where(number % 4 == 0, named(crowded, number // 4), named(common, number - number // 4 - 1))
    mixed = jax.random.permutation(jax.random.fold_in(own, 3), count)
    giver, receiver = mixed[0:count // 2 * 2:2], mixed[1:count // 2 * 2:2]
    slack = jnp.minimum(tallies[giver] - 1, reach - tallies[receiver]) // 2
    slack = jnp.where((giver == sequence[0]) | (receiver == sequence[0]) | (tallies[receiver] == 0), 0, jnp.maximum(slack, 0))
    moved = jax.random.randint(jax.random.fold_in(own, 4), (count // 2,), 0, 1 << 20) % (slack + 1)
    tallies = tallies.at[giver].add(-moved).at[receiver].add(moved)
    labels = jnp.searchsorted(jnp.cumsum(tallies), jnp.arange(rows * top), side="right").astype(jnp.int32)
    listing = labels.reshape(top, rows).T
    listing = listing[jax.random.permutation(jax.random.fold_in(own, 1), rows)]
    rotation = jax.random.randint(jax.random.fold_in(own, 2), (rows, 1), 0, top)
    return jnp.take_along_axis(listing, (jnp.arange(top)[None, :] + rotation) % top, axis=1)


def shares(number_of, total, reach, lean, full):
    weights = [(1 << 20) // math.isqrt(standing ** lean) + 1 for standing in range(1, number_of + 1)]
    largest = reach if full else min(reach, max(-(-total // number_of), total * weights[0] // sum(weights)))
    least = 1 if total - largest >= number_of - 1 else 0
    holding, surplus = [largest] + [least] * (number_of - 1), total - largest - least * (number_of - 1)
    while surplus > 0:
        free = [i for i in range(1, number_of) if holding[i] < largest] or [i for i in range(1, number_of) if holding[i] < reach]
        pool, remaining = sum([weights[i] for i in free]), surplus
        for i in free:
            extra = min(reach - holding[i], max(1, remaining * weights[i] // pool), surplus)
            holding[i] = holding[i] + extra
            surplus = surplus - extra
    return np.array(holding)


def gaussian(key, extent, deviation, bound, cuts=(), kind=jnp.bfloat16):
    level = block_levels(key, extent, cuts, -0.22, 0.18) if cuts else 1.0
    result = jax.random.normal(key, extent, jnp.float32) * deviation * level
    return jnp.minimum(jnp.maximum(result, -bound), bound).astype(kind)


def setup_inputs(seed: int = 0) -> dict:
    splits = jax.random.split(jax.random.key(seed), 7)
    source_emb = gaussian(splits[0], (NSB, NODE_GROUP_SIZE, FEATURE_LENGTH), 1.0, 6.0, ((0, 256),), jnp.float32)
    target_emb = gaussian(splits[1], (NTB, NODE_GROUP_SIZE, FEATURE_LENGTH), 1.0, 6.0, ((0, 256),), jnp.float32)
    source_mass = jnp.clip(jnp.exp(math.log(2.0) - 1.3862944 * jax.random.uniform(splits[2], (NSB, NODE_GROUP_SIZE), jnp.float32) ** block_levels(splits[2], (NSB, NODE_GROUP_SIZE), ((0, 256),), -0.2, 0.2)), 0.5, 2.0)
    target_mass = jnp.clip(jnp.exp(math.log(2.0) - 1.3862944 * jax.random.uniform(splits[3], (NTB, NODE_GROUP_SIZE), jnp.float32) ** block_levels(splits[3], (NTB, NODE_GROUP_SIZE), ((0, 256),), -0.2, 0.2)), 0.5, 2.0)
    cand_device_keys = jax.random.split(jax.random.fold_in(splits[4], 1), NSB // SB_DEV)
    cand_device_turns = jax.random.permutation(jax.random.fold_in(splits[4], 3), NSB // SB_DEV)
    cand_device = jax.vmap(lambda own, number: shared_out(jax.random.fold_in(splits[4], 2), own, number, SB_DEV, N_DEV, 7, CAP, 2))(cand_device_keys, cand_device_turns).reshape((NSB, 7))
    cand_block = touch_ends(jax.random.randint(splits[5], (NSB, 8), 0, TB_DEV), jax.random.fold_in(splits[5], 1), 0, TB_DEV - 1).astype(jnp.int32)
    return {"source_emb": source_emb, "target_emb": target_emb, "source_mass": source_mass, "target_mass": target_mass, "cand_device": cand_device, "cand_block": cand_block}


entropic_regularizer = 0.1
dustbin = 0.5
epsilon = 1e-06

def unit_rows(emb):
    return emb * lax.rsqrt(lax.optimization_barrier(jnp.mean(emb * emb, axis=-1, keepdims=True)) + epsilon)

def target_ids(cand_device, cand_block):
    src_index = jnp.arange(cand_device.shape[0], dtype=jnp.int32)
    flat_dev = src_index // SB_DEV
    cluster_label = flat_dev // N_DEV
    dev_index = flat_dev % N_DEV
    near_ids = (cluster_label[:, None] * N_DEV + cand_device) * TB_DEV + cand_block[:, :7]
    far_ids = ((cluster_label + 1) % N_GROUP * N_DEV + dev_index) * TB_DEV + cand_block[:, 7]
    return jnp.concatenate([near_ids, far_ids[:, None]], axis=1).astype(jnp.int32)

def kernel_tile(left_node_group, tgt_blocks):
    alignment_affinity = jnp.einsum('bd,kjd->kbj', left_node_group, tgt_blocks, precision=lax.Precision.HIGHEST)
    return jnp.exp(alignment_affinity * (1.0 / (FEATURE_LENGTH * entropic_regularizer))) / (8.0 * NODE_GROUP_SIZE)

def reference(source_emb, target_emb, source_mass, target_mass, cand_device, cand_block):
    src_unit = unit_rows(source_emb)
    tgt_unit = unit_rows(target_emb)
    cand_ids = target_ids(cand_device, cand_block)
    tgt_scale = jnp.ones_like(target_mass)
    src_scale = jnp.ones_like(source_mass)
    for sweep in range(ITERS):

        def rows_of(packed, tgt_scale=tgt_scale):
            left_node_group, id_block = packed
            kernel = kernel_tile(left_node_group, tgt_unit[id_block])
            return jnp.einsum('kbj,kj->b', kernel, tgt_scale[id_block], precision=lax.Precision.HIGHEST)
        row_sums = lax.map(rows_of, (src_unit, cand_ids))
        src_scale = source_mass / (dustbin + row_sums)

        def cols_of(packed):
            left_node_group, id_block, scale_block = packed
            kernel = kernel_tile(left_node_group, tgt_unit[id_block])
            return jnp.einsum('kbj,b->kj', kernel, scale_block, precision=lax.Precision.HIGHEST)
        col_parts = lax.map(cols_of, (src_unit, cand_ids, src_scale))
        col_sums = jax.ops.segment_sum(col_parts.reshape(-1, NODE_GROUP_SIZE), cand_ids.reshape(-1), num_segments=NTB)
        tgt_scale = target_mass / (dustbin + col_sums)
    return (src_scale, tgt_scale)
```

```python
import functools

import jax
import jax.numpy as jnp
from jax import lax
from jax.experimental import pallas as pl
from jax.experimental.pallas import tpu as pltpu
from jax.sharding import PartitionSpec as P

MESH = pl.DeviceIdType.MESH
N = 128
NX = 4
NEAR = 7
CAP = 2
ITERS = 2
EMPTY = -64
CHUNK = 8
DUSTBIN = 0.5
EPSILON = 1e-6
GAIN = 1.0 / (N * 0.1)
SHARE = 1.0 / (8.0 * N)

F32, BF16, I32 = jnp.float32, jnp.bfloat16, jnp.int32


def nt(a, b):
    return lax.dot_general(a, b, (((1,), (1,)), ((), ())), preferred_element_type=F32)


def nn(a, b):
    return lax.dot_general(a, b, (((1,), (0,)), ((), ())), preferred_element_type=F32)


def halves(v):
    hi = v.astype(BF16).astype(F32)
    return hi, v - hi


def kernel(ng, nz, sb, tb_dev, *refs):
    (semb, temb, smass, tmass, cdev, cblk, src_out, tgt_out,
     s_raw, t_raw, f_raw, s_hi, s_lo, t_hi, t_lo, f_hi, f_lo, k_hi, k_lo, kf_hi, kf_lo,
     tab, tabs, tabf, tabs_sm, tabf_sm,
     rp0, rp1, rpi0, rpi1, rf0, rf1, rfi0, rfi1, so0, so1, ss0, ss1, sf0, sf1,
     co0, co1, ci0, ci1, to, ts, snd, rcv, loc) = refs
    nr = 2 * nz
    hops = nz // 2
    half = sb // 2
    g, d = lax.axis_index("group"), lax.axis_index("dev")
    z, x, c = d // (2 * NX), (d // 2) % NX, d % 2

    def dev(dz, dx, flip):
        zz, xx = lax.rem(z + dz, nz), lax.rem(x + dx, NX)
        return (g, zz * (2 * NX) + xx * 2 + (1 - c if flip else c))

    def rel(dz, flip):
        return (dz % nz) * 2 + flip

    up, down = dev(1, 0, 0), dev(nz - 1, 0, 0)
    right, left = dev(0, 1, 0), dev(0, NX - 1, 0)
    partner = dev(0, 0, 1)
    ahead, behind = (lax.rem(g + 1, ng), d), (lax.rem(g + ng - 1, ng), d)

    count = [0]
    sent = []

    def send(src, dst, to_dev):
        k = count[0]
        count[0] += 1
        copy = pltpu.make_async_remote_copy(
            src_ref=src, dst_ref=dst, send_sem=snd.at[k], recv_sem=rcv.at[k],
            device_id=to_dev, device_id_type=MESH)
        copy.start()
        sent.append(copy)
        return copy

    barrier = pltpu.get_barrier_semaphore()
    greeted = (up, down, right, left, partner, ahead, behind)
    for other in greeted:
        pl.semaphore_signal(barrier, inc=1, device_id=other, device_id_type=MESH)
    own_s = pltpu.make_async_copy(semb, s_raw.at[0], loc.at[0])
    own_t = pltpu.make_async_copy(temb, t_raw.at[0], loc.at[1])
    own_s.start()
    own_t.start()

    lane = lax.broadcasted_iota(I32, (1, N), 1)
    run = jnp.zeros((1, N), I32)
    rows = [jnp.full((1, N), EMPTY, I32) for _ in range(2 * CAP)]
    far = jnp.zeros((1, N), I32)
    for b in range(sb):
        hit = jnp.zeros((1, N), I32)
        which = jnp.zeros((1, N), I32)
        for k in range(NEAR):
            m = cdev[b : b + 1, k : k + 1] == lane
            hit = jnp.where(m, 1, hit)
            which = jnp.where(m, cblk[b : b + 1, k : k + 1], which)
        for u in range(CAP):
            m = (hit == 1) & (run == u)
            rows[u] = jnp.where(m, b, rows[u])
            rows[CAP + u] = jnp.where(m, which, rows[CAP + u])
        run = run + hit
        far = jnp.where(lane == b, cblk[b : b + 1, NEAR : NEAR + 1], far)
    table = jnp.concatenate(rows + [far] + [jnp.zeros((1, N), I32)] * (7 - 2 * CAP), axis=0)
    tab[...] = table
    tabs[0] = table

    pl.semaphore_wait(barrier, len(greeted))

    chunks = tb_dev // CHUNK
    mid = chunks // 2
    t_plus, t_minus = {}, {}
    minus_order = list(range(mid, chunks)) + list(range(mid))
    for i in range(chunks):
        p, m = pl.ds(i * CHUNK, CHUNK), pl.ds(minus_order[i] * CHUNK, CHUNK)
        t_plus[i] = send(temb.at[p], t_raw.at[NX - 1, p], right)
        t_minus[minus_order[i]] = send(temb.at[m], t_raw.at[1, m], left)
    w_far = send(tab, tabf, ahead)
    f_far = send(semb, f_raw, ahead)

    w_mate = {0: send(tab, tabs.at[rel(0, 1)], partner)}
    w_plus = {1: send(tab, tabs.at[rel(-1, 0)], up)}
    w_minus = {1: send(tab, tabs.at[rel(1, 0)], down)}
    for h in range(2, hops + 2):
        if h - 1 in w_plus:
            w_plus[h - 1].wait_recv()
            if h <= hops:
                w_plus[h] = send(tabs.at[rel(1 - h, 0)], tabs.at[rel(-h, 0)], up)
            w_mate[-(h - 1)] = send(tabs.at[rel(1 - h, 0)], tabs.at[rel(1 - h, 1)], partner)
        if h - 1 in w_minus:
            w_minus[h - 1].wait_recv()
            if h <= hops - 1:
                w_minus[h] = send(tabs.at[rel(h - 1, 0)], tabs.at[rel(h, 0)], down)
            w_mate[h - 1] = send(tabs.at[rel(h - 1, 0)], tabs.at[rel(h - 1, 1)], partner)

    s_plus = {1: send(semb, s_raw.at[rel(-1, 0)], up)}
    s_minus = {1: send(semb, s_raw.at[rel(1, 0)], down)}
    s_mate = {0: send(semb, s_raw.at[rel(0, 1)], partner)}

    def normalize(raw, hi, lo, start, size, into):
        def one(i, _):
            v = raw[start + i]
            v = v * lax.rsqrt(jnp.mean(v * v, axis=-1, keepdims=True) + EPSILON)
            h = v.astype(BF16)
            hi[into + i] = h
            lo[into + i] = (v - h.astype(F32)).astype(BF16)
            return 0

        lax.fori_loop(0, size, one, 0)

    def norm_s(dz, flip):
        r = rel(dz, flip)
        normalize(s_raw.at[r], s_hi, s_lo, 0, sb, r * sb)

    def norm_t(t, start, size):
        normalize(t_raw.at[t], t_hi.at[t], t_lo.at[t], start, size, start)

    for w in w_mate.values():
        w.wait_recv()
    tables = pltpu.make_async_copy(tabs, tabs_sm, loc.at[2])
    tables.start()
    own_s.wait()
    norm_s(0, 0)
    own_t.wait()
    norm_t(0, 0, tb_dev)
    relay_plus, relay_minus = {}, {}
    for h in range(1, hops + 1):
        if h <= chunks:
            i, j = h - 1, minus_order[h - 1]
            pi, pj = pl.ds(i * CHUNK, CHUNK), pl.ds(j * CHUNK, CHUNK)
            t_plus[i].wait_recv()
            if i < mid:
                relay_plus[i] = send(t_raw.at[NX - 1, pi], t_raw.at[2, pi], right)
            t_minus[j].wait_recv()
            if j >= mid:
                relay_minus[j] = send(t_raw.at[1, pj], t_raw.at[2, pj], left)
        s_plus[h].wait_recv()
        s_minus[h].wait_recv()
        a, b = rel(-h, 0), rel(h, 0)
        if h + 1 < hops:
            s_plus[h + 1] = send(s_raw.at[a], s_raw.at[rel(-h - 1, 0)], up)
            s_minus[h + 1] = send(s_raw.at[b], s_raw.at[rel(h + 1, 0)], down)
        elif h + 1 == hops:
            lo_half, hi_half = pl.ds(0, half), pl.ds(half, half)
            last = rel(hops, 0)
            s_plus[hops] = send(s_raw.at[a, lo_half], s_raw.at[last, lo_half], up)
            s_minus[hops] = send(s_raw.at[b, hi_half], s_raw.at[last, hi_half], down)
        if h < hops:
            s_mate[-h] = send(s_raw.at[a], s_raw.at[rel(-h, 1)], partner)
            s_mate[h] = send(s_raw.at[b], s_raw.at[rel(h, 1)], partner)
            norm_s(-h, 0)
            norm_s(h, 0)
        else:
            s_mate[h] = send(s_raw.at[a], s_raw.at[rel(h, 1)], partner)
            norm_s(h, 0)
        if h <= chunks:
            norm_t(NX - 1, i * CHUNK, CHUNK)
            norm_t(1, j * CHUNK, CHUNK)
        if h == 1:
            f_far.wait_recv()
            w_far.wait_recv()
            far_table = pltpu.make_async_copy(tabf, tabf_sm, loc.at[3])
            far_table.start()
            normalize(f_raw, f_hi, f_lo, 0, sb, 0)
            tables.wait()
            far_table.wait()
    for dz, copy in s_mate.items():
        copy.wait_recv()
        norm_s(dz, 1)

    sub16 = lax.broadcasted_iota(I32, (16, N), 0)
    sub32 = lax.broadcasted_iota(I32, (tb_dev, N), 0)

    def lane_of(t):
        return z * (2 * NX) + lax.rem(x + t, NX) * 2 + c

    def tile(a_hi, a_lo, b_hi, b_lo):
        dots = nt(a_hi, b_hi) + (nt(a_hi, b_lo) + nt(a_lo, b_hi))
        e = jnp.exp(dots * GAIN) * SHARE
        hi = e.astype(BF16)
        return hi, (e - hi.astype(F32)).astype(BF16)

    def build(t, first):
        at = lane_of(t)

        def body(r, _):
            acc = jnp.zeros((16, N), F32)
            for u in range(CAP):
                b, q = tabs_sm[r, u, at], tabs_sm[r, CAP + u, at]
                s = r * sb + jnp.maximum(b, 0)
                w = jnp.maximum(q, 0)
                hi, lo = tile(s_hi[s], s_lo[s], t_hi[t, w], t_lo[t, w])
                k_hi[r, t * CAP + u] = hi
                k_lo[r, t * CAP + u] = lo
                ones = jnp.where(sub16 == b, 1.0, 0.0).astype(BF16)
                acc = acc + nt(ones, hi) + nt(ones, lo)
            if first:
                rp0[r] = acc[:8]
            else:
                rp0[r] = rp0[r] + acc[:8]
            return 0

        lax.fori_loop(0, nr, body, 0)

    def far_tile(f, acc):
        w = tabf_sm[2 * CAP, f]
        hi, lo = tile(f_hi[f], f_lo[f], t_hi[0, w], t_lo[0, w])
        kf_hi[f] = hi
        kf_lo[f] = lo
        ones = jnp.where(sub16 == f, 1.0, 0.0).astype(BF16)
        return acc + nt(ones, hi) + nt(ones, lo)

    rf0[...] = lax.fori_loop(0, sb, far_tile, jnp.zeros((16, N), F32))[:8]
    build(0, True)
    build(NX - 1, False)
    build(1, False)
    for i in range(mid):
        relay_plus[i].wait_recv()
        norm_t(2, i * CHUNK, CHUNK)
        j = minus_order[i]
        relay_minus[j].wait_recv()
        norm_t(2, j * CHUNK, CHUNK)
    build(2, False)

    others = [(dz, flip) for dz in range(nz) for flip in range(2) if (dz, flip) != (0, 0)]
    across = range(1, NX)

    def spread(r, v, base):
        hi, lo = halves(v)
        return jnp.where(sub16 == r, hi, jnp.where(sub16 == r + base, lo, 0.0)).astype(BF16)

    def rows_pass(rp, rf):
        def body(r, _):
            acc = jnp.zeros((16, N), F32)
            for t in range(NX):
                at = lane_of(t)
                for u in range(CAP):
                    b, q = tabs_sm[r, u, at], tabs_sm[r, CAP + u, at]
                    lhs = spread(b, ts[t, pl.ds(jnp.maximum(q, 0), 1), :], 8)
                    acc = acc + nt(lhs, k_hi[r, t * CAP + u]) + nt(lhs, k_lo[r, t * CAP + u])
            rp[r] = acc[:8] + acc[8:]
            return 0

        lax.fori_loop(0, nr, body, 0)
        acc = jnp.zeros((16, N), F32)
        for f in range(sb):
            lhs = spread(f, ts[0, pl.ds(tabf_sm[2 * CAP, f], 1), :], 8)
            acc = acc + nt(lhs, kf_hi[f]) + nt(lhs, kf_lo[f])
        rf[...] = acc[:8] + acc[8:]

    def cols_pass(ss, sf):
        def one(v, hi, lo, q, acc):
            lhs = spread(0, v, 1)
            o = nn(lhs, hi) + nn(lhs, lo)
            return acc + jnp.where(sub32 == q, o[0:1] + o[1:2], 0.0)

        def body(r, accs):
            accs = list(accs)
            for t in range(NX):
                at = lane_of(t)
                for u in range(CAP):
                    b, q = tabs_sm[r, u, at], tabs_sm[r, CAP + u, at]
                    v = ss[r, pl.ds(jnp.maximum(b, 0), 1), :]
                    accs[t] = one(v, k_hi[r, t * CAP + u], k_lo[r, t * CAP + u], q, accs[t])
            return tuple(accs)

        zero = jnp.zeros((tb_dev, N), F32)
        accs = list(lax.fori_loop(0, nr, body, (zero,) * NX))
        for f in range(sb):
            accs[0] = one(sf[f : f + 1, :], kf_hi[f], kf_lo[f], tabf_sm[2 * CAP, f], accs[0])
        return accs

    for it, (rp, rpi, rf, rfi, so, ss, sf, co, ci) in enumerate((
        (rp0, rpi0, rf0, rfi0, so0, ss0, sf0, co0, ci0),
        (rp1, rpi1, rf1, rfi1, so1, ss1, sf1, co1, ci1),
    )):
        if it > 0:
            rows_pass(rp, rf)
        parts = [send(rf, rfi, behind)]
        for dz, flip in others:
            parts.append(send(rp.at[rel(dz, flip)], rpi.at[rel(-dz, flip)], dev(dz, 0, flip)))
        total = rp[0]
        for p in parts:
            p.wait_recv()
        total = total + rfi[...]
        for dz, flip in others:
            total = total + rpi[rel(dz, flip)]
        scale = smass[...] / (DUSTBIN + total)
        so[...] = scale
        ss[0] = scale
        if it == ITERS - 1:
            src_out[...] = scale
        parts = [send(so, sf, ahead)]
        for dz, flip in others:
            parts.append(send(so, ss.at[rel(-dz, flip)], dev(dz, 0, flip)))
        for p in parts:
            p.wait_recv()
        accs = cols_pass(ss, sf)
        parts = []
        for t in across:
            co[t] = accs[t]
        for t in across:
            parts.append(send(co.at[t], ci.at[NX - t], dev(0, t, 0)))
        total = accs[0]
        for p in parts:
            p.wait_recv()
        for t in across:
            total = total + ci[t]
        scale = tmass[...] / (DUSTBIN + total)
        if it == ITERS - 1:
            tgt_out[...] = scale
        else:
            to[...] = scale
            ts[0] = scale
            parts = [send(to, ts.at[NX - t], dev(0, t, 0)) for t in across]
            for p in parts:
                p.wait_recv()
    for copy in sent:
        copy.wait_send()


def local(ng, nz, semb, temb, smass, tmass, cdev, cblk):
    sb, tb = semb.shape[0], temb.shape[0]
    nr = 2 * nz
    near = NX * CAP
    vm = pltpu.VMEM
    tile = (N, N)
    scratch = [
        vm((nr, sb) + tile, F32), vm((NX, tb) + tile, F32), vm((sb,) + tile, F32),
        vm((nr * sb,) + tile, BF16), vm((nr * sb,) + tile, BF16),
        vm((NX, tb) + tile, BF16), vm((NX, tb) + tile, BF16),
        vm((sb,) + tile, BF16), vm((sb,) + tile, BF16),
        vm((nr, near) + tile, BF16), vm((nr, near) + tile, BF16),
        vm((sb,) + tile, BF16), vm((sb,) + tile, BF16),
        vm((8, N), I32), vm((nr, 8, N), I32), vm((8, N), I32),
        pltpu.SMEM((nr, 8, N), I32), pltpu.SMEM((8, N), I32),
    ]
    scratch += [vm((nr, sb, N), F32)] * 4 + [vm((sb, N), F32)] * 4 + [vm((sb, N), F32)] * 2
    scratch += [vm((nr, sb, N), F32)] * 2 + [vm((sb, N), F32)] * 2
    scratch += [vm((NX, tb, N), F32)] * 4 + [vm((tb, N), F32), vm((NX, tb, N), F32)]
    scratch += [pltpu.SemaphoreType.DMA((128,)), pltpu.SemaphoreType.DMA((128,)), pltpu.SemaphoreType.DMA((4,))]
    any_, vmem = pl.BlockSpec(memory_space=pl.ANY), pl.BlockSpec(memory_space=pltpu.VMEM)
    return pl.pallas_call(
        functools.partial(kernel, ng, nz, sb, tb),
        out_shape=(jax.ShapeDtypeStruct(smass.shape, F32), jax.ShapeDtypeStruct(tmass.shape, F32)),
        in_specs=[any_, any_, vmem, vmem, vmem, vmem],
        out_specs=(vmem, vmem),
        scratch_shapes=scratch,
        compiler_params=pltpu.CompilerParams(
            collective_id=0, has_side_effects=True, vmem_limit_bytes=60 * 1024 * 1024),
        name="sinkhorn",
    )(semb, temb, smass, tmass, cdev, cblk)


def solution(mesh):
    placed = (
        P(("group", "dev"), None, None),
        P(("group", "dev"), None, None),
        P(("group", "dev"), None),
        P(("group", "dev"), None),
        P(("group", "dev"), None),
        P(("group", "dev"), None),
    )
    ng, nz = mesh.shape["group"], mesh.shape["dev"] // (2 * NX)
    return jax.shard_map(
        functools.partial(local, ng, nz),
        mesh=mesh,
        in_specs=placed,
        out_specs=(P(("group", "dev"), None), P(("group", "dev"), None)),
        check_vma=False,
    )
```

```python
import functools

import jax
import jax.numpy as jnp
from jax import lax
from jax.experimental import pallas as pl
from jax.experimental.pallas import tpu as pltpu
from jax.sharding import PartitionSpec as P

MESH = pl.DeviceIdType.MESH
N = 128
NX = 4
NEAR = 7
CAP = 2
ITERS = 2
EMPTY = -64
CHUNK = 8
DUSTBIN = 0.5
EPSILON = 1e-6
GAIN = 1.0 / (N * 0.1)
SHARE = 1.0 / (8.0 * N)

F32, BF16, I32 = jnp.float32, jnp.bfloat16, jnp.int32


def nn(a, b):
    return lax.dot_general(a, b, (((1,), (0,)), ((), ())), preferred_element_type=F32)


def halves(v):
    hi = v.astype(BF16).astype(F32)
    return hi, v - hi


def kernel(ng, nz, sb, tb_dev, *refs):
    (semb, temb, smass, tmass, cdev, cblk, src_out, tgt_out,
     s_raw, t_raw, f_raw, s_hi, s_lo, t_hi, t_lo, f_hi, f_lo, k_row, k_col, kf_row, kf_col,
     tab, tabs, tabf, tabc, tabs_sm, tabf_sm,
     rp0, rp1, rpi0, rpi1, rf0, rf1, rfi0, rfi1, so0, so1, ss0, ss1, sf0, sf1,
     co0, co1, ci0, ci1, to, ts, snd, rcv, loc) = refs
    nr = 2 * nz
    hops = nz // 2
    half = sb // 2
    line = 2 * NX
    g, d = lax.axis_index("group"), lax.axis_index("dev")
    z, x, c = d // line, (d // 2) % NX, d % 2

    def dev(dz, dx, flip):
        zz, xx = lax.rem(z + dz, nz), lax.rem(x + dx, NX)
        return (g, zz * line + xx * 2 + (1 - c if flip else c))

    def rel(dz, flip):
        return (dz % nz) * 2 + flip

    up, down = dev(1, 0, 0), dev(nz - 1, 0, 0)
    right, left = dev(0, 1, 0), dev(0, NX - 1, 0)
    partner = dev(0, 0, 1)
    ahead, behind = (lax.rem(g + 1, ng), d), (lax.rem(g + ng - 1, ng), d)

    count = [0]
    sent = []

    def send(src, dst, to_dev):
        k = count[0]
        count[0] += 1
        copy = pltpu.make_async_remote_copy(
            src_ref=src, dst_ref=dst, send_sem=snd.at[k], recv_sem=rcv.at[k],
            device_id=to_dev, device_id_type=MESH)
        copy.start()
        sent.append(copy)
        return copy

    barrier = pltpu.get_barrier_semaphore()
    greeted = (up, down, right, left, partner, ahead, behind)
    for other in greeted:
        pl.semaphore_signal(barrier, inc=1, device_id=other, device_id_type=MESH)
    own_s = pltpu.make_async_copy(semb, s_raw.at[0], loc.at[0])
    own_t = pltpu.make_async_copy(temb, t_raw.at[0], loc.at[1])
    own_s.start()
    own_t.start()

    lane = lax.broadcasted_iota(I32, (1, N), 1)
    run = jnp.zeros((1, N), I32)
    rows = [jnp.full((1, N), EMPTY, I32) for _ in range(2 * CAP)]
    far = jnp.zeros((1, N), I32)
    for b in range(sb):
        hit = jnp.zeros((1, N), I32)
        which = jnp.zeros((1, N), I32)
        for k in range(NEAR):
            m = cdev[b : b + 1, k : k + 1] == lane
            hit = jnp.where(m, 1, hit)
            which = jnp.where(m, cblk[b : b + 1, k : k + 1], which)
        for u in range(CAP):
            m = (hit == 1) & (run == u)
            rows[u] = jnp.where(m, b, rows[u])
            rows[CAP + u] = jnp.where(m, which, rows[CAP + u])
        run = run + hit
        far = jnp.where(lane == b, cblk[b : b + 1, NEAR : NEAR + 1], far)
    table = jnp.concatenate(rows + [far] + [jnp.zeros((1, N), I32)] * (7 - 2 * CAP), axis=0)
    tab[...] = table
    tabs[0] = table

    pl.semaphore_wait(barrier, len(greeted))

    chunks = tb_dev // CHUNK
    mid = chunks // 2
    minus_order = list(range(mid, chunks)) + list(range(mid))
    w_plus = {1: send(tab, tabs.at[rel(-1, 0)], up)}
    w_minus = {1: send(tab, tabs.at[rel(1, 0)], down)}
    s_plus = {1: send(semb, s_raw.at[rel(-1, 0)], up)}
    s_minus = {1: send(semb, s_raw.at[rel(1, 0)], down)}
    t_plus, t_minus = {}, {}
    for i in range(chunks):
        p, m = pl.ds(i * CHUNK, CHUNK), pl.ds(minus_order[i] * CHUNK, CHUNK)
        t_plus[i] = send(temb.at[p], t_raw.at[NX - 1, p], right)
        t_minus[minus_order[i]] = send(temb.at[m], t_raw.at[1, m], left)
    w_far = send(tab, tabf, ahead)
    f_far = send(semb, f_raw, ahead)
    w_mate = {0: send(tab, tabs.at[rel(0, 1)], partner)}
    s_mate = {0: send(semb, s_raw.at[rel(0, 1)], partner)}

    def normalize(raw, hi, lo, start, size, into, turned):
        def one(i, _):
            for w in range(8):
                k = i * 8 + w
                v = raw[start + k]
                if turned:
                    v = v.T
                axis = 0 if turned else 1
                v = v * lax.rsqrt(jnp.mean(v * v, axis=axis, keepdims=True) + EPSILON)
                h = v.astype(BF16)
                hi[into + k] = h
                lo[into + k] = (v - h.astype(F32)).astype(BF16)
            return 0

        lax.fori_loop(0, size // 8, one, 0)

    def norm_s(dz, flip):
        r = rel(dz, flip)
        normalize(s_raw.at[r], s_hi, s_lo, 0, sb, r * sb, True)

    def norm_t(t, start, size):
        normalize(t_raw.at[t], t_hi.at[t], t_lo.at[t], start, size, start, False)

    own_s.wait()
    norm_s(0, 0)
    own_t.wait()
    norm_t(0, 0, tb_dev)
    relay_plus, relay_minus = {}, {}
    for h in range(1, hops + 1):
        a, b = rel(-h, 0), rel(h, 0)
        w_plus[h].wait_recv()
        if h < hops:
            w_plus[h + 1] = send(tabs.at[a], tabs.at[rel(-h - 1, 0)], up)
        w_mate[-h] = send(tabs.at[a], tabs.at[rel(-h, 1)], partner)
        if h < hops:
            w_minus[h].wait_recv()
            if h + 1 < hops:
                w_minus[h + 1] = send(tabs.at[b], tabs.at[rel(h + 1, 0)], down)
            w_mate[h] = send(tabs.at[b], tabs.at[rel(h, 1)], partner)
        s_plus[h].wait_recv()
        s_minus[h].wait_recv()
        if h + 1 < hops:
            s_plus[h + 1] = send(s_raw.at[a], s_raw.at[rel(-h - 1, 0)], up)
            s_minus[h + 1] = send(s_raw.at[b], s_raw.at[rel(h + 1, 0)], down)
        elif h + 1 == hops:
            lo_half, hi_half = pl.ds(0, half), pl.ds(half, half)
            last = rel(hops, 0)
            s_plus[hops] = send(s_raw.at[a, lo_half], s_raw.at[last, lo_half], up)
            s_minus[hops] = send(s_raw.at[b, hi_half], s_raw.at[last, hi_half], down)
        s_mate[-h] = send(s_raw.at[a], s_raw.at[rel(-h, 1)], partner)
        if h < hops:
            s_mate[h] = send(s_raw.at[b], s_raw.at[rel(h, 1)], partner)
        if h <= chunks:
            i, j = h - 1, minus_order[h - 1]
            pi, pj = pl.ds(i * CHUNK, CHUNK), pl.ds(j * CHUNK, CHUNK)
            t_plus[i].wait_recv()
            if i < mid:
                relay_plus[i] = send(t_raw.at[NX - 1, pi], t_raw.at[2, pi], right)
            t_minus[j].wait_recv()
            if j >= mid:
                relay_minus[j] = send(t_raw.at[1, pj], t_raw.at[2, pj], left)
        norm_s(-h, 0)
        if h < hops:
            norm_s(h, 0)
        if h <= chunks:
            norm_t(NX - 1, i * CHUNK, CHUNK)
            norm_t(1, j * CHUNK, CHUNK)
    for copy in w_mate.values():
        copy.wait_recv()
    lane8 = lax.broadcasted_iota(I32, (8, N), 1)
    compact = jnp.zeros((8, N), I32)
    for r in range(nr):
        moved = pltpu.roll(tabs[r], lax.rem(r * line + N - z * line, N), 1)
        compact = jnp.where(lane8 // line == r, moved, compact)
    tabc[...] = compact
    w_far.wait_recv()
    far_table = pltpu.make_async_copy(tabf, tabf_sm, loc.at[3])
    far_table.start()
    f_far.wait_recv()
    normalize(f_raw, f_hi, f_lo, 0, sb, 0, True)
    tables = pltpu.make_async_copy(tabc, tabs_sm, loc.at[2])
    tables.start()
    for dz, copy in s_mate.items():
        copy.wait_recv()
        norm_s(dz, 1)
    far_table.wait()
    tables.wait()

    sub8 = lax.broadcasted_iota(I32, (8, N), 0)
    sub16 = lax.broadcasted_iota(I32, (16, N), 0)
    sub32 = lax.broadcasted_iota(I32, (tb_dev, N), 0)

    def lane_of(r, t):
        return r * line + lax.rem(x + t, NX) * 2 + c

    def two_terms(v, ref, k):
        hi = v.astype(BF16)
        ref[pl.ds(k * 2 * N, N), :] = hi
        ref[pl.ds(k * 2 * N + N, N), :] = (v - hi.astype(F32)).astype(BF16)

    def tile(b_hi, b_lo, a_hi, a_lo, row, col, k):
        dots = nn(b_hi, a_hi) + (nn(b_lo, a_hi) + nn(b_hi, a_lo))
        e = jnp.exp(dots * GAIN) * SHARE
        two_terms(e, row, k)
        two_terms(e.T, col, k)
        return jnp.sum(e, axis=0, keepdims=True)

    def build(t, first):
        def body(r0, _):
            for rr in range(4):
                r = r0 * 4 + rr
                acc = jnp.zeros((8, N), F32)
                for u in range(CAP):
                    b, q = tabs_sm[u, lane_of(r, t)], tabs_sm[CAP + u, lane_of(r, t)]
                    s = r * sb + jnp.maximum(b, 0)
                    w = jnp.maximum(q, 0)
                    sums = tile(t_hi[t, w], t_lo[t, w], s_hi[s], s_lo[s],
                                k_row.at[r], k_col.at[r], t * CAP + u)
                    acc = acc + jnp.where(sub8 == b, sums, 0.0)
                rp0[r] = acc if first else rp0[r] + acc
            return 0

        lax.fori_loop(0, nr // 4, body, 0)

    def far_tiles(f0, acc):
        for ff in range(4):
            f = f0 * 4 + ff
            w = tabf_sm[2 * CAP, f]
            sums = tile(t_hi[0, w], t_lo[0, w], f_hi[f], f_lo[f], kf_row, kf_col, f)
            acc = acc + jnp.where(sub8 == f, sums, 0.0)
        return acc

    rf0[...] = lax.fori_loop(0, sb // 4, far_tiles, jnp.zeros((8, N), F32))
    build(0, True)
    build(NX - 1, False)
    build(1, False)
    for i in range(mid):
        relay_plus[i].wait_recv()
        norm_t(2, i * CHUNK, CHUNK)
        j = minus_order[i]
        relay_minus[j].wait_recv()
        norm_t(2, j * CHUNK, CHUNK)
    build(2, False)

    others = [(dz, flip) for dz in range(nz) for flip in range(2) if (dz, flip) != (0, 0)]
    others.sort(key=lambda o: -min(o[0], nz - o[0]))
    across = (2, 1, 3)

    def spread(v, r):
        hi, lo = halves(v)
        return jnp.where(sub16 == r, hi, jnp.where(sub16 == r + 8, lo, 0.0)).astype(BF16)

    def product(lhs, tiles):
        o = nn(jnp.concatenate([v for v in lhs for _ in range(2)], axis=1), tiles)
        return o[:8] + o[8:]

    def rows_pass(rp, rf):
        def body(r0, _):
            for rr in range(4):
                r = r0 * 4 + rr
                lhs = []
                for t in range(NX):
                    for u in range(CAP):
                        b, q = tabs_sm[u, lane_of(r, t)], tabs_sm[CAP + u, lane_of(r, t)]
                        lhs.append(spread(ts[t, pl.ds(jnp.maximum(q, 0), 1), :], b))
                rp[r] = product(lhs, k_row[r])
            return 0

        lax.fori_loop(0, nr // 4, body, 0)
        lhs = [spread(ts[0, pl.ds(tabf_sm[2 * CAP, f], 1), :], f) for f in range(sb)]
        rf[...] = product(lhs, kf_row[...])

    def cols_pass(ss, sf):
        def body(r0, accs):
            accs = list(accs)
            for rr in range(4):
                r = r0 * 4 + rr
                lhs = []
                for t in range(NX):
                    for u in range(CAP):
                        b = tabs_sm[u, lane_of(r, t)]
                        lhs.append(spread(ss[r, pl.ds(jnp.maximum(b, 0), 1), :], t * CAP + u))
                o = product(lhs, k_col[r])
                for t in range(NX):
                    for u in range(CAP):
                        k = t * CAP + u
                        q = tabs_sm[CAP + u, lane_of(r, t)]
                        accs[t] = accs[t] + jnp.where(sub32 == q, o[k : k + 1], 0.0)
            return tuple(accs)

        lhs = [spread(sf[f : f + 1, :], f) for f in range(sb)]
        o = product(lhs, kf_col[...])
        first = jnp.zeros((tb_dev, N), F32)
        for f in range(sb):
            first = first + jnp.where(sub32 == tabf_sm[2 * CAP, f], o[f : f + 1], 0.0)
        zero = jnp.zeros((tb_dev, N), F32)
        return lax.fori_loop(0, nr // 4, body, (first, zero, zero, zero))

    for it, (rp, rpi, rf, rfi, so, ss, sf, co, ci) in enumerate((
        (rp0, rpi0, rf0, rfi0, so0, ss0, sf0, co0, ci0),
        (rp1, rpi1, rf1, rfi1, so1, ss1, sf1, co1, ci1),
    )):
        if it > 0:
            rows_pass(rp, rf)
        parts = []
        for dz, flip in others:
            parts.append(send(rp.at[rel(dz, flip)], rpi.at[rel(-dz, flip)], dev(dz, 0, flip)))
        parts.append(send(rf, rfi, behind))
        total = rp[0]
        for p in parts:
            p.wait_recv()
        total = total + rfi[...]
        for dz, flip in others:
            total = total + rpi[rel(dz, flip)]
        scale = smass[...] / (DUSTBIN + total)
        so[...] = scale
        ss[0] = scale
        if it == ITERS - 1:
            src_out[...] = scale
        parts = []
        for dz, flip in others:
            parts.append(send(so, ss.at[rel(-dz, flip)], dev(dz, 0, flip)))
        parts.append(send(so, sf, ahead))
        for p in parts:
            p.wait_recv()
        accs = cols_pass(ss, sf)
        parts = []
        for t in across:
            co[t] = accs[t]
        for t in across:
            parts.append(send(co.at[t], ci.at[NX - t], dev(0, t, 0)))
        total = accs[0]
        for p in parts:
            p.wait_recv()
        for t in across:
            total = total + ci[t]
        scale = tmass[...] / (DUSTBIN + total)
        if it == ITERS - 1:
            tgt_out[...] = scale
        else:
            to[...] = scale
            ts[0] = scale
            parts = [send(to, ts.at[NX - t], dev(0, t, 0)) for t in across]
            for p in parts:
                p.wait_recv()
    for copy in sent:
        copy.wait_send()


def local(ng, nz, semb, temb, smass, tmass, cdev, cblk):
    sb, tb = semb.shape[0], temb.shape[0]
    nr = 2 * nz
    slots = NX * CAP * 2 * N
    vm = pltpu.VMEM
    tile = (N, N)
    scratch = [
        vm((nr, sb) + tile, F32), vm((NX, tb) + tile, F32), vm((sb,) + tile, F32),
        vm((nr * sb,) + tile, BF16), vm((nr * sb,) + tile, BF16),
        vm((NX, tb) + tile, BF16), vm((NX, tb) + tile, BF16),
        vm((sb,) + tile, BF16), vm((sb,) + tile, BF16),
        vm((nr, slots, N), BF16), vm((nr, slots, N), BF16),
        vm((sb * 2 * N, N), BF16), vm((sb * 2 * N, N), BF16),
        vm((8, N), I32), vm((nr, 8, N), I32), vm((8, N), I32), vm((8, N), I32),
        pltpu.SMEM((8, N), I32), pltpu.SMEM((8, N), I32),
    ]
    scratch += [vm((nr, sb, N), F32)] * 4 + [vm((sb, N), F32)] * 4 + [vm((sb, N), F32)] * 2
    scratch += [vm((nr, sb, N), F32)] * 2 + [vm((sb, N), F32)] * 2
    scratch += [vm((NX, tb, N), F32)] * 4 + [vm((tb, N), F32), vm((NX, tb, N), F32)]
    scratch += [pltpu.SemaphoreType.DMA((128,)), pltpu.SemaphoreType.DMA((128,)), pltpu.SemaphoreType.DMA((4,))]
    any_, vmem = pl.BlockSpec(memory_space=pl.ANY), pl.BlockSpec(memory_space=pltpu.VMEM)
    return pl.pallas_call(
        functools.partial(kernel, ng, nz, sb, tb),
        out_shape=(jax.ShapeDtypeStruct(smass.shape, F32), jax.ShapeDtypeStruct(tmass.shape, F32)),
        in_specs=[any_, any_, vmem, vmem, vmem, vmem],
        out_specs=(vmem, vmem),
        scratch_shapes=scratch,
        compiler_params=pltpu.CompilerParams(
            collective_id=0, has_side_effects=True, vmem_limit_bytes=60 * 1024 * 1024),
        name="sinkhorn",
    )(semb, temb, smass, tmass, cdev, cblk)


def solution(mesh):
    placed = (
        P(("group", "dev"), None, None),
        P(("group", "dev"), None, None),
        P(("group", "dev"), None),
        P(("group", "dev"), None),
        P(("group", "dev"), None),
        P(("group", "dev"), None),
    )
    ng, nz = mesh.shape["group"], mesh.shape["dev"] // (2 * NX)
    return jax.shard_map(
        functools.partial(local, ng, nz),
        mesh=mesh,
        in_specs=placed,
        out_specs=(P(("group", "dev"), None), P(("group", "dev"), None)),
        check_vma=False,
    )
```

```python
import functools

import jax
import jax.numpy as jnp
from jax import lax
from jax.experimental import pallas as pl
from jax.experimental.pallas import tpu as pltpu
from jax.sharding import PartitionSpec as P

MESH = pl.DeviceIdType.MESH
N = 128
NX = 4
NEAR = 7
CAP = 2
ITERS = 2
EMPTY = -64
CHUNK = 8
COPIES = 45
DUSTBIN = 0.5
EPSILON = 1e-6
GAIN = 1.0 / (N * 0.1)
SHARE = 1.0 / (8.0 * N)

F32, BF16, I32 = jnp.float32, jnp.bfloat16, jnp.int32


def nn(a, b):
    return lax.dot_general(a, b, (((1,), (0,)), ((), ())), preferred_element_type=F32)


def halves(v):
    hi = v.astype(BF16).astype(F32)
    return hi, v - hi


def kernel(ng, nz, sb, tb_dev, *refs):
    (semb, temb, smass_in, tmass_in, cdev_in, cblk_in, out,
     s_raw, t_raw, f_raw, s_hi, s_lo, t_hi, t_lo, f_hi, f_lo, k_row, k_col, kf_row, kf_col,
     tab, tabs, tabf, tabc, tabs_sm, tabf_sm,
     rp0, rp1, rpi0, rpi1, rf0, rf1, rfi0, rfi1, so0, so1, ss0, ss1, ssl, sf0, sf1,
     co0, co1, ci0, ci1, to, ts, smass, tmass, cdev, cblk,
     snd, rcv, rs_snd, rs_rcv, ag_snd, ag_rcv, ex_snd, ex_rcv, loc) = refs
    nr = 2 * nz
    hops = nz // 2
    half = sb // 2
    line = 2 * NX
    g, d = lax.axis_index("group"), lax.axis_index("dev")
    z, x, c = d // line, (d // 2) % NX, d % 2

    def dev(dz, dx, flip):
        zz, xx = lax.rem(z + dz, nz), lax.rem(x + dx, NX)
        return (g, zz * line + xx * 2 + (1 - c if flip else c))

    def rel(dz, flip):
        return (dz % nz) * 2 + flip

    up, down = dev(1, 0, 0), dev(nz - 1, 0, 0)
    right, left = dev(0, 1, 0), dev(0, NX - 1, 0)
    partner = dev(0, 0, 1)
    ahead, behind = (lax.rem(g + 1, ng), d), (lax.rem(g + ng - 1, ng), d)

    count = [0]
    sent = []

    def send(src, dst, to_dev):
        k = count[0]
        count[0] += 1
        copy = pltpu.make_async_remote_copy(
            src_ref=src, dst_ref=dst, send_sem=snd.at[k], recv_sem=rcv.at[k],
            device_id=to_dev, device_id_type=MESH)
        copy.start()
        sent.append(copy)
        return copy

    barrier = pltpu.get_barrier_semaphore()
    greeted = (up, down, right, left, partner, ahead, behind)
    for other in greeted:
        pl.semaphore_signal(barrier, inc=1, device_id=other, device_id_type=MESH)
    own_s = pltpu.make_async_copy(semb, s_raw.at[0], loc.at[0])
    own_t = pltpu.make_async_copy(temb, t_raw.at[0], loc.at[1])
    small = [pltpu.make_async_copy(a, b, loc.at[4 + i]) for i, (a, b) in enumerate(
        ((cdev_in, cdev), (cblk_in, cblk), (smass_in, smass), (tmass_in, tmass)))]
    for copy in small:
        copy.start()
    own_s.start()
    own_t.start()
    for copy in small:
        copy.wait()

    lane = lax.broadcasted_iota(I32, (1, N), 1)
    run = jnp.zeros((1, N), I32)
    rows = [jnp.full((1, N), EMPTY, I32) for _ in range(2 * CAP)]
    far = jnp.zeros((1, N), I32)
    for b in range(sb):
        hit = jnp.zeros((1, N), I32)
        which = jnp.zeros((1, N), I32)
        for k in range(NEAR):
            m = cdev[b : b + 1, k : k + 1] == lane
            hit = jnp.where(m, 1, hit)
            which = jnp.where(m, cblk[b : b + 1, k : k + 1], which)
        for u in range(CAP):
            m = (hit == 1) & (run == u)
            rows[u] = jnp.where(m, b, rows[u])
            rows[CAP + u] = jnp.where(m, which, rows[CAP + u])
        run = run + hit
        far = jnp.where(lane == b, cblk[b : b + 1, NEAR : NEAR + 1], far)
    table = jnp.concatenate(rows + [far] + [jnp.zeros((1, N), I32)] * (7 - 2 * CAP), axis=0)
    tab[...] = table
    tabs[0] = table

    pl.semaphore_wait(barrier, len(greeted))

    chunks = tb_dev // CHUNK
    mid = chunks // 2
    minus_order = list(range(mid, chunks)) + list(range(mid))
    w_plus = {1: send(tab, tabs.at[rel(-1, 0)], up)}
    w_minus = {1: send(tab, tabs.at[rel(1, 0)], down)}
    s_plus = {1: send(semb, s_raw.at[rel(-1, 0)], up)}
    s_minus = {1: send(semb, s_raw.at[rel(1, 0)], down)}
    t_plus, t_minus = {}, {}
    for i in range(chunks):
        p, m = pl.ds(i * CHUNK, CHUNK), pl.ds(minus_order[i] * CHUNK, CHUNK)
        t_plus[i] = send(temb.at[p], t_raw.at[NX - 1, p], right)
        t_minus[minus_order[i]] = send(temb.at[m], t_raw.at[1, m], left)
    w_far = send(tab, tabf, ahead)
    f_far = send(semb, f_raw, ahead)
    w_mate = {0: send(tab, tabs.at[rel(0, 1)], partner)}
    s_mate = {0: send(semb, s_raw.at[rel(0, 1)], partner)}

    def normalize(raw, hi, lo, start, size, into, turned):
        def one(i, _):
            for w in range(8):
                k = i * 8 + w
                v = raw[start + k]
                if turned:
                    v = v.T
                axis = 0 if turned else 1
                v = v * lax.rsqrt(jnp.mean(v * v, axis=axis, keepdims=True) + EPSILON)
                h = v.astype(BF16)
                hi[into + k] = h
                lo[into + k] = (v - h.astype(F32)).astype(BF16)
            return 0

        lax.fori_loop(0, size // 8, one, 0)

    def norm_s(dz, flip):
        r = rel(dz, flip)
        normalize(s_raw.at[r], s_hi, s_lo, 0, sb, r * sb, True)

    def norm_t(t, start, size):
        normalize(t_raw.at[t], t_hi.at[t], t_lo.at[t], start, size, start, False)

    own_s.wait()
    norm_s(0, 0)
    own_t.wait()
    norm_t(0, 0, tb_dev)
    relay_plus, relay_minus = {}, {}
    for h in range(1, hops + 1):
        a, b = rel(-h, 0), rel(h, 0)
        w_plus[h].wait_recv()
        if h < hops:
            w_plus[h + 1] = send(tabs.at[a], tabs.at[rel(-h - 1, 0)], up)
        w_mate[-h] = send(tabs.at[a], tabs.at[rel(-h, 1)], partner)
        if h < hops:
            w_minus[h].wait_recv()
            if h + 1 < hops:
                w_minus[h + 1] = send(tabs.at[b], tabs.at[rel(h + 1, 0)], down)
            w_mate[h] = send(tabs.at[b], tabs.at[rel(h, 1)], partner)
        s_plus[h].wait_recv()
        s_minus[h].wait_recv()
        if h + 1 < hops:
            s_plus[h + 1] = send(s_raw.at[a], s_raw.at[rel(-h - 1, 0)], up)
            s_minus[h + 1] = send(s_raw.at[b], s_raw.at[rel(h + 1, 0)], down)
        elif h + 1 == hops:
            lo_half, hi_half = pl.ds(0, half), pl.ds(half, half)
            last = rel(hops, 0)
            s_plus[hops] = send(s_raw.at[a, lo_half], s_raw.at[last, lo_half], up)
            s_minus[hops] = send(s_raw.at[b, hi_half], s_raw.at[last, hi_half], down)
        s_mate[-h] = send(s_raw.at[a], s_raw.at[rel(-h, 1)], partner)
        if h < hops:
            s_mate[h] = send(s_raw.at[b], s_raw.at[rel(h, 1)], partner)
        if h <= chunks:
            i, j = h - 1, minus_order[h - 1]
            pi, pj = pl.ds(i * CHUNK, CHUNK), pl.ds(j * CHUNK, CHUNK)
            t_plus[i].wait_recv()
            if i < mid:
                relay_plus[i] = send(t_raw.at[NX - 1, pi], t_raw.at[2, pi], right)
            t_minus[j].wait_recv()
            if j >= mid:
                relay_minus[j] = send(t_raw.at[1, pj], t_raw.at[2, pj], left)
        norm_s(-h, 0)
        if h < hops:
            norm_s(h, 0)
        if h <= chunks:
            norm_t(NX - 1, i * CHUNK, CHUNK)
            norm_t(1, j * CHUNK, CHUNK)
    for copy in w_mate.values():
        copy.wait_recv()
    lane8 = lax.broadcasted_iota(I32, (8, N), 1)
    compact = jnp.zeros((8, N), I32)
    for r in range(nr):
        moved = pltpu.roll(tabs[r], lax.rem(r * line + N - z * line, N), 1)
        compact = jnp.where(lane8 // line == r, moved, compact)
    tabc[...] = compact
    w_far.wait_recv()
    far_table = pltpu.make_async_copy(tabf, tabf_sm, loc.at[3])
    far_table.start()
    f_far.wait_recv()
    normalize(f_raw, f_hi, f_lo, 0, sb, 0, True)
    tables = pltpu.make_async_copy(tabc, tabs_sm, loc.at[2])
    tables.start()
    for dz, copy in s_mate.items():
        copy.wait_recv()
        norm_s(dz, 1)
    far_table.wait()
    tables.wait()

    sub8 = lax.broadcasted_iota(I32, (8, N), 0)
    sub16 = lax.broadcasted_iota(I32, (16, N), 0)
    sub32 = lax.broadcasted_iota(I32, (tb_dev, N), 0)

    def lane_of(r, t):
        return r * line + lax.rem(x + t, NX) * 2 + c

    def two_terms(v, ref, k):
        hi = v.astype(BF16)
        ref[pl.ds(k * 2 * N, N), :] = hi
        ref[pl.ds(k * 2 * N + N, N), :] = (v - hi.astype(F32)).astype(BF16)

    def tile(b_hi, b_lo, a_hi, a_lo, row, col, k):
        dots = nn(b_hi, a_hi) + (nn(b_lo, a_hi) + nn(b_hi, a_lo))
        e = jnp.exp(dots * GAIN) * SHARE
        two_terms(e, row, k)
        two_terms(e.T, col, k)
        return jnp.sum(e, axis=0, keepdims=True)

    def group(j):
        near, far = lax.rem(nz - j, nz), j + 1
        return (near, 0), (near, 1), (far, 0), (far, 1)

    def to_line(src, dst, snds, rcvs, dz, flip, whole=False):
        r, back = dz * 2 + flip, lax.rem(nz - dz, nz) * 2 + flip
        return pltpu.make_async_remote_copy(
            src_ref=src if whole else src.at[r], dst_ref=dst.at[back], send_sem=snds.at[r],
            recv_sem=rcvs.at[back], device_id=dev(dz, 0, flip), device_id_type=MESH)

    def from_line(src, dst, snds, rcvs, dz, flip, whole=False):
        r = dz * 2 + flip
        return pltpu.make_async_remote_copy(
            src_ref=src if whole else src.at[r], dst_ref=dst.at[r], send_sem=snds.at[r],
            recv_sem=rcvs.at[r], device_id=dev(dz, 0, flip), device_id_type=MESH)

    def send_rows(rp, rpi, j):
        for i, (dz, flip) in enumerate(group(j)):
            copy = to_line(rp, rpi, rs_snd, rs_rcv, dz, flip)
            if i == 0:
                pl.when(j > 0)(copy.start)
            else:
                copy.start()

    def build(t, first, last=False):
        def body(r0, _):
            j = nz // 2 - 1 - r0
            for dz, flip in group(j):
                r = dz * 2 + flip
                acc = jnp.zeros((8, N), F32)
                for u in range(CAP):
                    b, q = tabs_sm[u, lane_of(r, t)], tabs_sm[CAP + u, lane_of(r, t)]
                    s = r * sb + jnp.maximum(b, 0)
                    w = jnp.maximum(q, 0)
                    sums = tile(t_hi[t, w], t_lo[t, w], s_hi[s], s_lo[s],
                                k_row.at[r], k_col.at[r], t * CAP + u)
                    acc = acc + jnp.where(sub8 == b, sums, 0.0)
                rp0[r] = acc if first else rp0[r] + acc
            if last:
                send_rows(rp0, rpi0, j)
            return 0

        lax.fori_loop(0, nr // 4, body, 0)

    def far_tiles(f0, acc):
        for ff in range(4):
            f = f0 * 4 + ff
            w = tabf_sm[2 * CAP, f]
            sums = tile(t_hi[0, w], t_lo[0, w], f_hi[f], f_lo[f], kf_row, kf_col, f)
            acc = acc + jnp.where(sub8 == f, sums, 0.0)
        return acc

    rf0[...] = lax.fori_loop(0, sb // 4, far_tiles, jnp.zeros((8, N), F32))
    build(0, True)
    build(NX - 1, False)
    build(1, False)
    for i in range(mid):
        relay_plus[i].wait_recv()
        norm_t(2, i * CHUNK, CHUNK)
        j = minus_order[i]
        relay_minus[j].wait_recv()
        norm_t(2, j * CHUNK, CHUNK)
    build(2, False, True)

    others = [(dz, flip) for dz in range(nz) for flip in range(2) if (dz, flip) != (0, 0)]
    others.sort(key=lambda o: -min(o[0], nz - o[0]))
    across = (2, 1, 3)

    def exchange(src, dst, k, to_dev):
        return pltpu.make_async_remote_copy(
            src_ref=src, dst_ref=dst, send_sem=ex_snd.at[k], recv_sem=ex_rcv.at[k],
            device_id=to_dev, device_id_type=MESH)

    def spread(v, r):
        hi, lo = halves(v)
        return jnp.where(sub16 == r, hi, jnp.where(sub16 == r + 8, lo, 0.0)).astype(BF16)

    def product(lhs, tiles):
        o = nn(jnp.concatenate([v for v in lhs for _ in range(2)], axis=1), tiles)
        return o[:8] + o[8:]

    def rows_pass(rp, rpi, rf):
        def body(r0, _):
            j = nz // 2 - 1 - r0
            for dz, flip in group(j):
                r = dz * 2 + flip
                lhs = []
                for t in range(NX):
                    for u in range(CAP):
                        b, q = tabs_sm[u, lane_of(r, t)], tabs_sm[CAP + u, lane_of(r, t)]
                        lhs.append(spread(ts[t, pl.ds(jnp.maximum(q, 0), 1), :], b))
                rp[r] = product(lhs, k_row[r])
            send_rows(rp, rpi, j)
            return 0

        lax.fori_loop(0, nz // 2, body, 0)
        lhs = [spread(ts[0, pl.ds(tabf_sm[2 * CAP, f], 1), :], f) for f in range(sb)]
        rf[...] = product(lhs, kf_row[...])

    def cols_pass(so, ss, sf, far_copy):
        def body(j, accs):
            accs = list(accs)
            for i, (dz, flip) in enumerate(group(j)):
                copy = from_line(so, ss, ag_snd, ag_rcv, dz, flip, True)
                if i == 0:
                    pl.when(j > 0)(copy.wait_recv)
                else:
                    copy.wait_recv()
            for dz, flip in group(j):
                ssl[dz * 2 + flip] = ss[dz * 2 + flip]
            for dz, flip in group(j):
                r = dz * 2 + flip
                lhs = []
                for t in range(NX):
                    for u in range(CAP):
                        b = tabs_sm[u, lane_of(r, t)]
                        lhs.append(spread(ssl[r, pl.ds(jnp.maximum(b, 0), 1), :], t * CAP + u))
                o = product(lhs, k_col[r])
                for t in range(NX):
                    for u in range(CAP):
                        k = t * CAP + u
                        q = tabs_sm[CAP + u, lane_of(r, t)]
                        accs[t] = accs[t] + jnp.where(sub32 == q, o[k : k + 1], 0.0)
            return tuple(accs)

        zero = jnp.zeros((tb_dev, N), F32)
        accs = list(lax.fori_loop(0, nz // 2, body, (zero,) * NX))
        far_copy.wait_recv()
        lhs = [spread(sf[f : f + 1, :], f) for f in range(sb)]
        o = product(lhs, kf_col[...])
        for f in range(sb):
            accs[0] = accs[0] + jnp.where(sub32 == tabf_sm[2 * CAP, f], o[f : f + 1], 0.0)
        return accs

    for it, (rp, rpi, rf, rfi, so, ss, sf, co, ci) in enumerate((
        (rp0, rpi0, rf0, rfi0, so0, ss0, sf0, co0, ci0),
        (rp1, rpi1, rf1, rfi1, so1, ss1, sf1, co1, ci1),
    )):
        last = it == ITERS - 1
        far_rows = exchange(rf, rfi, 0, behind)
        far_scale = exchange(so, sf, 1, ahead)
        if it > 0:
            rows_pass(rp, rpi, rf)
        far_rows.start()
        total = rp[0]
        for dz, flip in others[::-1]:
            from_line(rp, rpi, rs_snd, rs_rcv, dz, flip).wait_recv()
        far_rows.wait_recv()
        total = total + rfi[...]
        for dz, flip in others:
            total = total + rpi[rel(dz, flip)]
        scale = smass[...] / (DUSTBIN + total)
        so[...] = scale
        ss[0] = scale
        if last:
            out[:sb] = scale
        for dz, flip in others:
            to_line(so, ss, ag_snd, ag_rcv, dz, flip, True).start()
        far_scale.start()
        accs = cols_pass(so, ss, sf, far_scale)
        parts = []
        for t in across:
            co[t] = accs[t]
        for t in across:
            copy = exchange(co.at[t], ci.at[NX - t], 1 + t, dev(0, t, 0))
            copy.start()
            parts.append(copy)
        total = accs[0]
        for dz, flip in others:
            to_line(rp, rpi, rs_snd, rs_rcv, dz, flip).wait_send()
            to_line(so, ss, ag_snd, ag_rcv, dz, flip, True).wait_send()
        far_rows.wait_send()
        far_scale.wait_send()
        for p in parts:
            p.wait_recv()
        for t in across:
            total = total + ci[t]
        scale = tmass[...] / (DUSTBIN + total)
        if last:
            out[sb:] = scale
        else:
            to[...] = scale
            ts[0] = scale
            spreads = [exchange(to, ts.at[NX - t], 4 + t, dev(0, t, 0)) for t in across]
            for p in spreads:
                p.start()
            for p in spreads:
                p.wait_recv()
            for p in spreads:
                p.wait_send()
        for p in parts:
            p.wait_send()
    for copy in sent:
        copy.wait_send()
    assert count[0] <= COPIES


def local(ng, nz, semb, temb, smass, tmass, cdev, cblk):
    sb, tb = semb.shape[0], temb.shape[0]
    nr = 2 * nz
    slots = NX * CAP * 2 * N
    vm = pltpu.VMEM
    tile = (N, N)
    scratch = [
        vm((nr, sb) + tile, F32), vm((NX, tb) + tile, F32), vm((sb,) + tile, F32),
        vm((nr * sb,) + tile, BF16), vm((nr * sb,) + tile, BF16),
        vm((NX, tb) + tile, BF16), vm((NX, tb) + tile, BF16),
        vm((sb,) + tile, BF16), vm((sb,) + tile, BF16),
        vm((nr, slots, N), BF16), vm((nr, slots, N), BF16),
        vm((sb * 2 * N, N), BF16), vm((sb * 2 * N, N), BF16),
        vm((8, N), I32), vm((nr, 8, N), I32), vm((8, N), I32), vm((8, N), I32),
        pltpu.SMEM((8, N), I32), pltpu.SMEM((8, N), I32),
    ]
    scratch += [vm((nr, sb, N), F32)] * 4 + [vm((sb, N), F32)] * 4 + [vm((sb, N), F32)] * 2
    scratch += [vm((nr, sb, N), F32)] * 3 + [vm((sb, N), F32)] * 2
    scratch += [vm((NX, tb, N), F32)] * 4 + [vm((tb, N), F32), vm((NX, tb, N), F32)]
    scratch += [vm(a.shape, a.dtype) for a in (smass, tmass, cdev, cblk)]
    dma = pltpu.SemaphoreType.DMA
    scratch += [dma((COPIES,))] * 2 + [dma((nr,))] * 4 + [dma((8,))] * 3
    any_, vmem = pl.BlockSpec(memory_space=pl.ANY), pl.BlockSpec(memory_space=pltpu.VMEM)
    both = pl.pallas_call(
        functools.partial(kernel, ng, nz, sb, tb),
        out_shape=jax.ShapeDtypeStruct((sb + tb, N), F32),
        in_specs=[any_] * 6,
        out_specs=vmem,
        scratch_shapes=scratch,
        compiler_params=pltpu.CompilerParams(
            collective_id=0, has_side_effects=True, vmem_limit_bytes=60 * 1024 * 1024),
        name="sinkhorn",
    )(semb, temb, smass, tmass, cdev, cblk)

    def split(both_ref, src_ref, tgt_ref):
        src_ref[...] = both_ref[:sb]
        tgt_ref[...] = both_ref[sb:]

    return pl.pallas_call(
        split,
        out_shape=(jax.ShapeDtypeStruct(smass.shape, F32), jax.ShapeDtypeStruct(tmass.shape, F32)),
        in_specs=[vmem],
        out_specs=(vmem, vmem),
        name="split",
    )(both)


def solution(mesh):
    placed = (
        P(("group", "dev"), None, None),
        P(("group", "dev"), None, None),
        P(("group", "dev"), None),
        P(("group", "dev"), None),
        P(("group", "dev"), None),
        P(("group", "dev"), None),
    )
    ng, nz = mesh.shape["group"], mesh.shape["dev"] // (2 * NX)
    return jax.shard_map(
        functools.partial(local, ng, nz),
        mesh=mesh,
        in_specs=placed,
        out_specs=(P(("group", "dev"), None), P(("group", "dev"), None)),
        check_vma=False,
    )
```

```python
import functools

import jax
import jax.numpy as jnp
from jax import lax
from jax.experimental import pallas as pl
from jax.experimental.pallas import tpu as pltpu
from jax.sharding import PartitionSpec as P

MESH = pl.DeviceIdType.MESH
N = 128
NX = 4
NEAR = 7
CAP = 2
PAIR = 2
VMEM_BYTES = 62 * 1024 * 1024
ITERS = 2
EMPTY = -64
COPIES = 84
DUSTBIN = 0.5
EPSILON = 1e-6
GAIN = 1.0 / (N * 0.1)
SHARE = 1.0 / (8.0 * N)

F32, BF16, I32 = jnp.float32, jnp.bfloat16, jnp.int32


def nn(a, b):
    return lax.dot_general(a, b, (((1,), (0,)), ((), ())), preferred_element_type=F32)


def halves(v):
    hi = v.astype(BF16).astype(F32)
    return hi, v - hi


def kernel(ng, nz, sb, tb_dev, *refs):
    (semb, temb, smass_in, tmass_in, cdev_in, cblk_in, out,
     s_raw, t_raw, f_raw, s_hi, s_lo, t_hi, t_lo, f_hi, f_lo, k_row, k_col, kf_row, kf_col,
     tab, tabs, tabf, tabc, tabs_sm, tabf_sm,
     rp0, rp1, rpi0, rpi1, ss0, ss1, ssl, rf0, rf1, rfi0, rfi1, so0, so1, sf0, sf1,
     co0, co1, ci0, ci1, ts, smass, tmass, cdev, cblk, tmass_pair,
     snd, rcv, rs_snd, rs_rcv, ag_snd, ag_rcv, ex_snd, ex_rcv, loc) = refs
    nr = 4 * nz
    hops = nz // 2
    half = sb // 2
    quarter = sb // 4
    line = 2 * NX
    near = PAIR * CAP
    g, d = lax.axis_index("group"), lax.axis_index("dev")
    z, x, c = d // line, (d // 2) % NX, d % 2

    def at(zz, xx, cc):
        return (g, zz * line + xx * 2 + cc)

    def dev(dz, flip, bx):
        return at(lax.rem(z + dz, nz), NX - 1 - x if bx else x, 1 - c if flip else c)

    def rel(dz, flip, bx):
        return (dz % nz) * 4 + flip * 2 + bx

    up, down = dev(1, 0, 0), dev(nz - 1, 0, 0)
    partner, mate = dev(0, 1, 0), dev(0, 0, 1)
    pair = at(z, x + 1 - 2 * lax.rem(x, 2), c)
    ahead, behind = (lax.rem(g + 1, ng), d), (lax.rem(g + ng - 1, ng), d)

    count = [0]
    sent = []

    def send(src, dst, to_dev):
        k = count[0]
        count[0] += 1
        copy = pltpu.make_async_remote_copy(
            src_ref=src, dst_ref=dst, send_sem=snd.at[k], recv_sem=rcv.at[k],
            device_id=to_dev, device_id_type=MESH)
        copy.start()
        sent.append(copy)
        return copy

    barrier = pltpu.get_barrier_semaphore()
    greeted = (up, down, mate, pair, partner, ahead, behind)
    for other in greeted:
        pl.semaphore_signal(barrier, inc=1, device_id=other, device_id_type=MESH)
    own_s = pltpu.make_async_copy(semb, s_raw.at[0], loc.at[0])
    own_t = pltpu.make_async_copy(temb, t_raw.at[0], loc.at[1])
    small = [pltpu.make_async_copy(a, b, loc.at[4 + i]) for i, (a, b) in enumerate(
        ((cdev_in, cdev), (cblk_in, cblk), (smass_in, smass), (tmass_in, tmass)))]
    for copy in small:
        copy.start()
    own_s.start()
    own_t.start()
    for copy in small:
        copy.wait()

    lane = lax.broadcasted_iota(I32, (1, N), 1)
    run = jnp.zeros((1, N), I32)
    rows = [jnp.full((1, N), EMPTY, I32) for _ in range(2 * CAP)]
    far = jnp.zeros((1, N), I32)
    for b in range(sb):
        hit = jnp.zeros((1, N), I32)
        which = jnp.zeros((1, N), I32)
        for k in range(NEAR):
            m = cdev[b : b + 1, k : k + 1] == lane
            hit = jnp.where(m, 1, hit)
            which = jnp.where(m, cblk[b : b + 1, k : k + 1], which)
        for u in range(CAP):
            m = (hit == 1) & (run == u)
            rows[u] = jnp.where(m, b, rows[u])
            rows[CAP + u] = jnp.where(m, which, rows[CAP + u])
        run = run + hit
        far = jnp.where(lane == b, cblk[b : b + 1, NEAR : NEAR + 1], far)
    table = jnp.concatenate(rows + [far] + [jnp.zeros((1, N), I32)] * (7 - 2 * CAP), axis=0)
    tab[...] = table
    tabs[0] = table

    pl.semaphore_wait(barrier, len(greeted))

    lo, hi = pl.ds(0, half), pl.ds(half, half)
    pieces = ((0, half), (0, 0), (1, 0))
    z_plus, z_minus = {}, {}

    def piece(dz, p, start=0, size=half):
        bx, first = pieces[p]
        return s_raw.at[rel(dz, 0, bx), pl.ds(first + start, size)]

    w_mate = send(tab, tabs.at[1], mate)
    pre = send(semb.at[lo], s_raw.at[rel(0, 0, 1), lo], mate)
    for p in (0, 1):
        part = semb.at[pl.ds(pieces[p][1], half)]
        z_plus[1, p] = send(part, piece(-1, p), up)
        z_minus[1, p] = send(part, piece(1, p), down)
    post = {0: send(semb.at[hi], s_raw.at[rel(0, 0, 1), hi], mate)}
    t_pair = send(temb, t_raw.at[1], pair)
    mass_pair = send(tmass_in, tmass_pair, pair)
    cores = {0: [send(semb, s_raw.at[rel(0, 1, 0)], partner)]}
    w_far = send(tab, tabf, ahead)
    f_far = send(semb, f_raw, ahead)
    w_plus, w_minus, w_core = {}, {}, {}

    def two(dz, flip):
        return tabs.at[pl.ds(rel(dz, flip, 0), 2)]

    def unit(v, turned):
        if turned:
            v = v.T
        v = v * lax.rsqrt(jnp.mean(v * v, axis=0 if turned else 1, keepdims=True) + EPSILON)
        h = v.astype(BF16)
        return h, (v - h.astype(F32)).astype(BF16)

    def norm_lines(dz):
        def one(i, _):
            r = rel(dz, 0, 0) + i
            for w in range(sb):
                s_hi[r * sb + w], s_lo[r * sb + w] = unit(s_raw[r, w], True)
            return 0

        lax.fori_loop(0, 4, one, 0)

    def norm_t(t):
        def one(i, _):
            for w in range(8):
                t_hi[t, i * 8 + w], t_lo[t, i * 8 + w] = unit(t_raw[t, i * 8 + w], False)
            return 0

        lax.fori_loop(0, tb_dev // 8, one, 0)

    w_mate.wait_recv()
    w_plus[1] = send(two(0, 0), two(-1, 0), up)
    w_minus[1] = send(two(0, 0), two(1, 0), down)
    w_core[0] = send(two(0, 0), two(0, 1), partner)
    pre.wait_recv()
    z_plus[1, 2] = send(piece(0, 2), piece(-1, 2), up)
    z_minus[1, 2] = send(piece(0, 2), piece(1, 2), down)
    cores[0].append(send(piece(0, 2), s_raw.at[rel(0, 1, 1), lo], partner))
    own_t.wait()
    norm_t(0)
    own_s.wait()
    post[0].wait_recv()
    cores[0].append(send(s_raw.at[rel(0, 0, 1), hi], s_raw.at[rel(0, 1, 1), hi], partner))

    sub8 = lax.broadcasted_iota(I32, (8, N), 0)
    sub16 = lax.broadcasted_iota(I32, (16, N), 0)
    sub32 = lax.broadcasted_iota(I32, (tb_dev, N), 0)

    def lane_of(r, t):
        return r * 4 + lax.rem(x + t, 2) * 2 + c

    def two_terms(v, ref, k):
        h = v.astype(BF16)
        ref[pl.ds(k * 2 * N, N), :] = h
        ref[pl.ds(k * 2 * N + N, N), :] = (v - h.astype(F32)).astype(BF16)

    def tile(b_hi, b_lo, a_hi, a_lo, row, col, k):
        dots = nn(b_hi, a_hi) + (nn(b_lo, a_hi) + nn(b_hi, a_lo))
        e = jnp.exp(dots * GAIN) * SHARE
        two_terms(e, row, k)
        two_terms(e.T, col, k)
        return jnp.sum(e, axis=0, keepdims=True)

    def to_line(src, dst, snds, rcvs, dz, flip, bx, whole=False):
        r = dz * 4 + flip * 2 + bx
        back = lax.rem(nz - dz, nz) * 4 + flip * 2 + bx
        return pltpu.make_async_remote_copy(
            src_ref=src if whole else src.at[r], dst_ref=dst.at[back], send_sem=snds.at[r],
            recv_sem=rcvs.at[back], device_id=dev(dz, flip, bx), device_id_type=MESH)

    def from_line(src, dst, snds, rcvs, dz, flip, bx, whole=False):
        r = dz * 4 + flip * 2 + bx
        return pltpu.make_async_remote_copy(
            src_ref=src if whole else src.at[r], dst_ref=dst.at[r], send_sem=snds.at[r],
            recv_sem=rcvs.at[r], device_id=dev(dz, flip, bx), device_id_type=MESH)

    four = tuple((flip, bx) for flip in range(2) for bx in range(2))

    def send_rows(rp, rpi, dz):
        for flip, bx in four:
            copy = to_line(rp, rpi, rs_snd, rs_rcv, dz, flip, bx)
            if (flip, bx) == (0, 0):
                pl.when(dz > 0)(copy.start)
            else:
                copy.start()

    def build(dz):
        for flip in range(2):
            for bx in range(2):
                r = dz * 4 + flip * 2 + bx
                acc = jnp.zeros((8, N), F32)
                for t in range(PAIR):
                    for u in range(CAP):
                        b, q = tabs_sm[u, lane_of(r, t)], tabs_sm[CAP + u, lane_of(r, t)]
                        s, w = r * sb + jnp.maximum(b, 0), jnp.maximum(q, 0)
                        sums = tile(t_hi[t, w], t_lo[t, w], s_hi[s], s_lo[s], k_row.at[dz * 2 + flip],
                                    k_col.at[dz * 2 + flip], bx * near + t * CAP + u)
                        acc = acc + jnp.where(sub8 == b, sums, 0.0)
                rp0[r] = acc
        send_rows(rp0, rpi0, dz)

    def far_tiles(f0, acc):
        for ff in range(4):
            f = f0 * 4 + ff
            w = tabf_sm[2 * CAP, f]
            sums = tile(t_hi[0, w], t_lo[0, w], f_hi[f], f_lo[f], kf_row, kf_col, f)
            acc = acc + jnp.where(sub8 == f, sums, 0.0)
        return acc

    for h in range(1, hops + 1):
        final = h == hops
        ways = ((-h, z_plus, up), (h, z_minus, down))
        w_plus[h].wait_recv()
        if not final:
            w_plus[h + 1] = send(two(-h, 0), two(-h - 1, 0), up)
        w_core[-h] = send(two(-h, 0), two(-h, 1), partner)
        if not final:
            w_minus[h].wait_recv()
            if h + 1 < hops:
                w_minus[h + 1] = send(two(h, 0), two(h + 1, 0), down)
            w_core[h] = send(two(h, 0), two(h, 1), partner)
        for p in range(3):
            bx, first = pieces[p]
            rows = pl.ds(first, half)
            for k, (dz, got, onward) in enumerate(ways):
                got[h, p].wait_recv()
                if h + 1 < hops:
                    got[h + 1, p] = send(piece(dz, p), piece(-h - 1 if k == 0 else h + 1, p), onward)
                elif h + 1 == hops:
                    got[hops, p] = send(piece(dz, p, k * quarter, quarter), piece(hops, p, k * quarter, quarter), onward)
            for dz in (-h, h)[: 1 if final else 2]:
                key = hops if final else dz
                if p == 0:
                    post[key] = send(s_raw.at[rel(dz, 0, 0), hi], s_raw.at[rel(dz, 0, 1), hi], mate)
                cores.setdefault(key, []).append(
                    send(s_raw.at[rel(dz, 0, bx), rows], s_raw.at[rel(dz, 1, bx), rows], partner))
            if p == 1:
                for dz in ((0,) if h == 1 else (1 - h, h - 1)):
                    for copy in cores[dz]:
                        copy.wait_recv()
                    norm_lines(dz)
                if h == 2:
                    f_far.wait_recv()

                    def far_unit(i, _):
                        for w in range(sb):
                            f_hi[w], f_lo[w] = unit(f_raw[w], True)
                        return 0

                    lax.fori_loop(0, 1, far_unit, 0)
                if final:
                    for copy in w_core.values():
                        copy.wait_recv()
                    lane8 = lax.broadcasted_iota(I32, (8, N), 1)
                    compact = jnp.zeros((8, N), I32)
                    for r in range(nr):
                        moved = pltpu.roll(tabs[r], lax.rem(r * 4 + N - z * line - (x // 2) * 4, N), 1)
                        compact = jnp.where(lane8 // 4 == r, moved, compact)
                    tabc[...] = compact
                    w_far.wait_recv()
                    far_table = pltpu.make_async_copy(tabf, tabf_sm, loc.at[3])
                    far_table.start()
                    t_pair.wait_recv()
                    norm_t(1)
                    tables = pltpu.make_async_copy(tabc, tabs_sm, loc.at[2])
                    tables.start()
                    far_table.wait()
                    tables.wait()
                    rf0[...] = lax.fori_loop(0, sb // 4, far_tiles, jnp.zeros((8, N), F32))

                    def builds(i, _):
                        j = (hops * 2 - 1 - i) // 2
                        build(jnp.where(i % 2 == 0, j, lax.rem(nz - j, nz)))
                        return 0

                    lax.fori_loop(0, nz - 1, builds, 0)
        for dz in (-h, h)[: 1 if final else 2]:
            key = hops if final else dz
            post[key].wait_recv()
            cores[key].append(send(s_raw.at[rel(dz, 0, 1), hi], s_raw.at[rel(dz, 1, 1), hi], partner))
    for copy in cores[hops]:
        copy.wait_recv()
    norm_lines(hops)

    def last_build(i, _):
        build(hops + i)
        return 0

    lax.fori_loop(0, 1, last_build, 0)

    others = [(dz,) + o for dz in range(nz) for o in four if (dz,) + o != (0, 0, 0)]
    others.sort(key=lambda o: -min(o[0], nz - o[0]))

    def exchange(src, dst, k, to_dev):
        return pltpu.make_async_remote_copy(
            src_ref=src, dst_ref=dst, send_sem=ex_snd.at[k], recv_sem=ex_rcv.at[k],
            device_id=to_dev, device_id_type=MESH)

    def group(j):
        return lax.rem(nz - j, nz), j + 1

    def spread(v, r):
        h, l = halves(v)
        return jnp.where(sub16 == r, h, jnp.where(sub16 == r + 8, l, 0.0)).astype(BF16)

    def product(lhs, tiles):
        o = nn(jnp.concatenate([v for v in lhs for _ in range(2)], axis=1), tiles)
        return o[:8] + o[8:]

    def rows_pass(rp, rpi, rf):
        def body(r0, _):
            j = hops - 1 - r0
            for dz in group(j):
                for flip, bx in four:
                    r = dz * 4 + flip * 2 + bx
                    lhs = []
                    for t in range(PAIR):
                        for u in range(CAP):
                            b, q = tabs_sm[u, lane_of(r, t)], tabs_sm[CAP + u, lane_of(r, t)]
                            lhs.append(spread(ts[t, pl.ds(jnp.maximum(q, 0), 1), :], b))
                    rp[r] = product(lhs, k_row[dz * 2 + flip, pl.ds(bx * near * 2 * N, near * 2 * N), :])
            for dz in group(j):
                send_rows(rp, rpi, dz)
            return 0

        lax.fori_loop(0, hops, body, 0)
        lhs = [spread(ts[0, pl.ds(tabf_sm[2 * CAP, f], 1), :], f) for f in range(sb)]
        rf[...] = product(lhs, kf_row[...])

    def cols_pass(so, ss, sf, far_copy):
        def body(j, accs):
            accs = list(accs)
            for dz in group(j):
                for flip, bx in four:
                    copy = from_line(so, ss, ag_snd, ag_rcv, dz, flip, bx, True)
                    if (flip, bx) == (0, 0):
                        pl.when(dz > 0)(copy.wait_recv)
                    else:
                        copy.wait_recv()
            for dz in group(j):
                for i in range(4):
                    ssl[dz * 4 + i] = ss[dz * 4 + i]
            for dz in group(j):
                for flip in range(2):
                    lhs = []
                    slots = [(bx, t, u) for bx in range(2) for t in range(PAIR) for u in range(CAP)]
                    for k, (bx, t, u) in enumerate(slots):
                        r = dz * 4 + flip * 2 + bx
                        b = tabs_sm[u, lane_of(r, t)]
                        lhs.append(spread(ssl[r, pl.ds(jnp.maximum(b, 0), 1), :], k))
                    o = product(lhs, k_col[dz * 2 + flip])
                    for k, (bx, t, u) in enumerate(slots):
                        q = tabs_sm[CAP + u, lane_of(dz * 4 + flip * 2 + bx, t)]
                        accs[t] = accs[t] + jnp.where(sub32 == q, o[k : k + 1], 0.0)
            return tuple(accs)

        zero = jnp.zeros((tb_dev, N), F32)
        accs = list(lax.fori_loop(0, hops, body, (zero,) * PAIR))
        far_copy.wait_recv()
        lhs = [spread(sf[f : f + 1, :], f) for f in range(sb)]
        o = product(lhs, kf_col[...])
        for f in range(sb):
            accs[0] = accs[0] + jnp.where(sub32 == tabf_sm[2 * CAP, f], o[f : f + 1], 0.0)
        return accs

    mass_pair.wait_recv()
    for it, (rp, rpi, rf, rfi, so, ss, sf, co, ci) in enumerate((
        (rp0, rpi0, rf0, rfi0, so0, ss0, sf0, co0, ci0),
        (rp1, rpi1, rf1, rfi1, so1, ss1, sf1, co1, ci1),
    )):
        last = it == ITERS - 1
        far_rows = exchange(rf, rfi, 0, behind)
        far_scale = exchange(so, sf, 1, ahead)
        if it > 0:
            rows_pass(rp, rpi, rf)
        far_rows.start()
        total = rp[0]
        for o in others[::-1]:
            from_line(rp, rpi, rs_snd, rs_rcv, *o).wait_recv()
        far_rows.wait_recv()
        total = total + rfi[...]
        for o in others:
            total = total + rpi[rel(*o)]
        scale = smass[...] / (DUSTBIN + total)
        so[...] = scale
        ss[0] = scale
        if last:
            out[:sb] = scale
        for o in others:
            to_line(so, ss, ag_snd, ag_rcv, *o, True).start()
        far_scale.start()
        accs = cols_pass(so, ss, sf, far_scale)
        co[1] = accs[1]
        if last:
            swap = exchange(co.at[1], ci.at[1], 3, pair)
        else:
            co[0] = accs[0]
            swap = exchange(co, ci, 2, pair)
        swap.start()
        for o in others:
            to_line(rp, rpi, rs_snd, rs_rcv, *o).wait_send()
            to_line(so, ss, ag_snd, ag_rcv, *o, True).wait_send()
        far_rows.wait_send()
        far_scale.wait_send()
        swap.wait_recv()
        scale = tmass[...] / (DUSTBIN + (accs[0] + ci[1]))
        if last:
            out[sb:] = scale
        else:
            ts[0] = scale
            ts[1] = tmass_pair[...] / (DUSTBIN + (accs[1] + ci[0]))
        swap.wait_send()
    for copy in sent:
        copy.wait_send()
    assert count[0] == COPIES


def local(ng, nz, semb, temb, smass, tmass, cdev, cblk):
    sb, tb = semb.shape[0], temb.shape[0]
    nr = 4 * nz
    slots = 2 * PAIR * CAP * 2 * N
    vm = pltpu.VMEM
    dma = pltpu.SemaphoreType.DMA
    tile = (N, N)
    blocks = vm((nr, sb, N), F32)
    source, target = vm((sb, N), F32), vm((tb, N), F32)
    pair = vm((PAIR, tb, N), F32)
    scratch = [
        vm((nr, sb) + tile, F32), vm((PAIR, tb) + tile, F32), vm((sb,) + tile, F32),
        vm((nr * sb,) + tile, BF16), vm((nr * sb,) + tile, BF16),
        vm((PAIR, tb) + tile, BF16), vm((PAIR, tb) + tile, BF16),
        vm((sb,) + tile, BF16), vm((sb,) + tile, BF16),
        vm((nr // 2, slots, N), BF16), vm((nr // 2, slots, N), BF16),
        vm((sb * 2 * N, N), BF16), vm((sb * 2 * N, N), BF16),
        vm((8, N), I32), vm((nr, 8, N), I32), vm((8, N), I32), vm((8, N), I32),
        pltpu.SMEM((8, N), I32), pltpu.SMEM((8, N), I32),
    ]
    scratch += [blocks] * 7 + [source] * 8 + [pair] * 5
    scratch += [vm(a.shape, a.dtype) for a in (smass, tmass, cdev, cblk)] + [target]
    scratch += [dma((COPIES,))] * 2 + [dma((nr,))] * 4 + [dma((4,))] * 2 + [dma((8,))]
    any_, vmem = pl.BlockSpec(memory_space=pl.ANY), pl.BlockSpec(memory_space=pltpu.VMEM)
    both = pl.pallas_call(
        functools.partial(kernel, ng, nz, sb, tb),
        out_shape=jax.ShapeDtypeStruct((sb + tb, N), F32),
        in_specs=[any_] * 6,
        out_specs=vmem,
        scratch_shapes=scratch,
        compiler_params=pltpu.CompilerParams(
            collective_id=0, has_side_effects=True, vmem_limit_bytes=VMEM_BYTES),
        name="sinkhorn",
    )(semb, temb, smass, tmass, cdev, cblk)

    def split(both_ref, src_ref, tgt_ref):
        src_ref[...] = both_ref[:sb]
        tgt_ref[...] = both_ref[sb:]

    return pl.pallas_call(
        split,
        out_shape=(jax.ShapeDtypeStruct(smass.shape, F32), jax.ShapeDtypeStruct(tmass.shape, F32)),
        in_specs=[vmem],
        out_specs=(vmem, vmem),
        name="split",
    )(both)


def solution(mesh):
    placed = (
        P(("group", "dev"), None, None),
        P(("group", "dev"), None, None),
        P(("group", "dev"), None),
        P(("group", "dev"), None),
        P(("group", "dev"), None),
        P(("group", "dev"), None),
    )
    ng, nz = mesh.shape["group"], mesh.shape["dev"] // (2 * NX)
    return jax.shard_map(
        functools.partial(local, ng, nz),
        mesh=mesh,
        in_specs=placed,
        out_specs=(P(("group", "dev"), None), P(("group", "dev"), None)),
        check_vma=False,
    )
```

```python
import functools

import jax
import jax.numpy as jnp
from jax import lax
from jax.experimental import pallas as pl
from jax.experimental.pallas import tpu as pltpu
from jax.sharding import PartitionSpec as P

MESH = pl.DeviceIdType.MESH
N = 128
NX = 4
NEAR = 7
CAP = 2
PAIR = 2
VMEM_BYTES = 62 * 1024 * 1024
ITERS = 2
EMPTY = -64
COPIES = 84
DUSTBIN = 0.5
EPSILON = 1e-6
GAIN = 1.0 / (N * 0.1)
SHARE = 1.0 / (8.0 * N)

F32, BF16, I32 = jnp.float32, jnp.bfloat16, jnp.int32


def nn(a, b):
    return lax.dot_general(a, b, (((1,), (0,)), ((), ())), preferred_element_type=F32)


def halves(v):
    hi = v.astype(BF16).astype(F32)
    return hi, v - hi


def kernel(ng, nz, sb, tb_dev, *refs):
    (semb, temb, smass_in, tmass_in, cdev_in, cblk_in, out,
     s_raw, t_raw, f_raw, s_hi, s_lo, t_hi, t_lo, f_hi, f_lo, k_row, k_col, kf_row, kf_col,
     tab, tabs, tabf, tabc, tabs_sm, tabf_sm,
     rp0, rp1, rpi0, rpi1, ss0, ss1, ssl, rf0, rf1, rfi0, rfi1, so0, so1, sf0, sf1,
     co0, co1, ci0, ci1, ts, smass, tmass, cdev, cblk, tmass_pair,
     snd, rcv, rs_snd, rs_rcv, ag_snd, ag_rcv, ex_snd, ex_rcv, loc) = refs
    nr = 4 * nz
    hops = nz // 2
    half = sb // 2
    quarter = sb // 4
    line = 2 * NX
    near = PAIR * CAP
    g, d = lax.axis_index("group"), lax.axis_index("dev")
    z, x, c = d // line, (d // 2) % NX, d % 2

    def at(zz, xx, cc):
        return (g, zz * line + xx * 2 + cc)

    def dev(dz, flip, bx):
        return at(lax.rem(z + dz, nz), NX - 1 - x if bx else x, 1 - c if flip else c)

    def rel(dz, flip, bx):
        return (dz % nz) * 4 + flip * 2 + bx

    up, down = dev(1, 0, 0), dev(nz - 1, 0, 0)
    partner, mate = dev(0, 1, 0), dev(0, 0, 1)
    pair = at(z, x + 1 - 2 * lax.rem(x, 2), c)
    ahead, behind = (lax.rem(g + 1, ng), d), (lax.rem(g + ng - 1, ng), d)

    count = [0]
    sent = []

    def send(src, dst, to_dev):
        k = count[0]
        count[0] += 1
        copy = pltpu.make_async_remote_copy(
            src_ref=src, dst_ref=dst, send_sem=snd.at[k], recv_sem=rcv.at[k],
            device_id=to_dev, device_id_type=MESH)
        copy.start()
        sent.append(copy)
        return copy

    barrier = pltpu.get_barrier_semaphore()
    greeted = (up, down, mate, pair, partner, ahead, behind)
    for other in greeted:
        pl.semaphore_signal(barrier, inc=1, device_id=other, device_id_type=MESH)
    own_s = pltpu.make_async_copy(semb, s_raw.at[0], loc.at[0])
    own_t = pltpu.make_async_copy(temb, t_raw.at[0], loc.at[1])
    small = [pltpu.make_async_copy(a, b, loc.at[4 + i]) for i, (a, b) in enumerate(
        ((cdev_in, cdev), (cblk_in, cblk), (smass_in, smass), (tmass_in, tmass)))]
    for copy in small:
        copy.start()
    own_s.start()
    own_t.start()
    for copy in small:
        copy.wait()

    lane = lax.broadcasted_iota(I32, (1, N), 1)
    run = jnp.zeros((1, N), I32)
    rows = [jnp.full((1, N), EMPTY, I32) for _ in range(2 * CAP)]
    far = jnp.zeros((1, N), I32)
    for b in range(sb):
        hit = jnp.zeros((1, N), I32)
        which = jnp.zeros((1, N), I32)
        for k in range(NEAR):
            m = cdev[b : b + 1, k : k + 1] == lane
            hit = jnp.where(m, 1, hit)
            which = jnp.where(m, cblk[b : b + 1, k : k + 1], which)
        for u in range(CAP):
            m = (hit == 1) & (run == u)
            rows[u] = jnp.where(m, b, rows[u])
            rows[CAP + u] = jnp.where(m, which, rows[CAP + u])
        run = run + hit
        far = jnp.where(lane == b, cblk[b : b + 1, NEAR : NEAR + 1], far)
    table = jnp.concatenate(rows + [far] + [jnp.zeros((1, N), I32)] * (7 - 2 * CAP), axis=0)
    tab[...] = table
    tabs[0] = table

    pl.semaphore_wait(barrier, len(greeted))

    lo, hi = pl.ds(0, half), pl.ds(half, half)
    pieces = ((0, half), (0, 0), (1, 0))
    z_plus, z_minus = {}, {}

    def piece(dz, p, start=0, size=half):
        bx, first = pieces[p]
        return s_raw.at[rel(dz, 0, bx), pl.ds(first + start, size)]

    w_mate = send(tab, tabs.at[1], mate)
    pre = send(semb.at[lo], s_raw.at[rel(0, 0, 1), lo], mate)
    for p in (0, 1):
        part = semb.at[pl.ds(pieces[p][1], half)]
        z_plus[1, p] = send(part, piece(-1, p), up)
        z_minus[1, p] = send(part, piece(1, p), down)
    post = {0: send(semb.at[hi], s_raw.at[rel(0, 0, 1), hi], mate)}
    t_pair = send(temb, t_raw.at[1], pair)
    mass_pair = send(tmass_in, tmass_pair, pair)
    cores = {0: [send(semb, s_raw.at[rel(0, 1, 0)], partner)]}
    w_far = send(tab, tabf, ahead)
    f_far = send(semb, f_raw, ahead)
    w_plus, w_minus, w_core = {}, {}, {}

    def two(dz, flip):
        return tabs.at[pl.ds(rel(dz, flip, 0), 2)]

    def unit(v, turned):
        if turned:
            v = v.T
        v = v * lax.rsqrt(jnp.mean(v * v, axis=0 if turned else 1, keepdims=True) + EPSILON)
        h = v.astype(BF16)
        return h, (v - h.astype(F32)).astype(BF16)

    def norm_lines(dz, bx):
        def one(flip, _):
            r = rel(dz, 0, bx) + flip * 2
            for w in range(sb):
                s_hi[r * sb + w], s_lo[r * sb + w] = unit(s_raw[r, w], True)
            return 0

        lax.fori_loop(0, 2, one, 0)

    def norm_t(t):
        def one(i, _):
            for w in range(8):
                t_hi[t, i * 8 + w], t_lo[t, i * 8 + w] = unit(t_raw[t, i * 8 + w], False)
            return 0

        lax.fori_loop(0, tb_dev // 8, one, 0)

    w_mate.wait_recv()
    w_plus[1] = send(two(0, 0), two(-1, 0), up)
    w_minus[1] = send(two(0, 0), two(1, 0), down)
    w_core[0] = send(two(0, 0), two(0, 1), partner)
    pre.wait_recv()
    z_plus[1, 2] = send(piece(0, 2), piece(-1, 2), up)
    z_minus[1, 2] = send(piece(0, 2), piece(1, 2), down)
    cores[0].append(send(piece(0, 2), s_raw.at[rel(0, 1, 1), lo], partner))
    own_t.wait()
    norm_t(0)
    own_s.wait()
    post[0].wait_recv()
    cores[0].append(send(s_raw.at[rel(0, 0, 1), hi], s_raw.at[rel(0, 1, 1), hi], partner))

    sub8 = lax.broadcasted_iota(I32, (8, N), 0)
    sub16 = lax.broadcasted_iota(I32, (16, N), 0)
    sub32 = lax.broadcasted_iota(I32, (tb_dev, N), 0)

    def lane_of(r, t):
        return r * 4 + lax.rem(x + t, 2) * 2 + c

    def two_terms(v, ref, k):
        h = v.astype(BF16)
        ref[pl.ds(k * 2 * N, N), :] = h
        ref[pl.ds(k * 2 * N + N, N), :] = (v - h.astype(F32)).astype(BF16)

    def tile(b_hi, b_lo, a_hi, a_lo, row, col, k):
        dots = nn(b_hi, a_hi) + (nn(b_lo, a_hi) + nn(b_hi, a_lo))
        e = jnp.exp(dots * GAIN) * SHARE
        two_terms(e, row, k)
        two_terms(e.T, col, k)
        return jnp.sum(e, axis=0, keepdims=True)

    def to_line(src, dst, snds, rcvs, dz, flip, bx, whole=False):
        r = dz * 4 + flip * 2 + bx
        back = lax.rem(nz - dz, nz) * 4 + flip * 2 + bx
        return pltpu.make_async_remote_copy(
            src_ref=src if whole else src.at[r], dst_ref=dst.at[back], send_sem=snds.at[0],
            recv_sem=rcvs.at[back], device_id=dev(dz, flip, bx), device_id_type=MESH)

    def from_line(src, dst, snds, rcvs, dz, flip, bx, whole=False):
        r = dz * 4 + flip * 2 + bx
        return pltpu.make_async_remote_copy(
            src_ref=src if whole else src.at[r], dst_ref=dst.at[r], send_sem=snds.at[0],
            recv_sem=rcvs.at[r], device_id=dev(dz, flip, bx), device_id_type=MESH)

    four = tuple((flip, bx) for flip in range(2) for bx in range(2))

    def send_rows(rp, rpi, dz, bxs=(0, 1)):
        for flip, bx in four:
            if bx in bxs:
                copy = to_line(rp, rpi, rs_snd, rs_rcv, dz, flip, bx)
                if (flip, bx) == (0, 0):
                    pl.when(dz > 0)(copy.start)
                else:
                    copy.start()

    def build(dz, dist, bxs, targets, first, done):
        for flip in range(2):
            for bx in bxs:
                r = dz * 4 + flip * 2 + bx
                acc = jnp.zeros((8, N), F32)
                for t in targets:
                    for u in range(CAP):
                        b, q = tabs_sm[dist, u, lane_of(r, t)], tabs_sm[dist, CAP + u, lane_of(r, t)]
                        s, w = r * sb + jnp.maximum(b, 0), jnp.maximum(q, 0)
                        sums = tile(t_hi[t, w], t_lo[t, w], s_hi[s], s_lo[s], k_row.at[dz * 2 + flip],
                                    k_col.at[dz * 2 + flip], bx * near + t * CAP + u)
                        acc = acc + jnp.where(sub8 == b, sums, 0.0)
                rp0[r] = acc if first else rp0[r] + acc
        if done:
            send_rows(rp0, rpi0, dz, bxs)

    def builds(first_place, places, targets, first, done):
        def one(i, _):
            p = first_place + i
            dist = (p + 1) // 2
            dz = jnp.where(p % 2 == 1, dist, lax.rem(nz - dist, nz))
            build(dz, dist, (0, 1), targets, first, done)
            return 0

        lax.fori_loop(0, places, one, 0)

    def last_build(bx):
        def one(i, _):
            build(hops + i, hops, (bx,), (0, 1), True, True)
            return 0

        lax.fori_loop(0, 1, one, 0)

    lane8 = lax.broadcasted_iota(I32, (8, N), 1)

    def compact(dist):
        places = (0,) if dist == 0 else (hops,) if dist == hops else (-dist, dist)
        part = jnp.zeros((8, N), I32)
        for dz in places:
            w_core[dz].wait_recv()
            for i in range(4):
                r = rel(dz, 0, 0) + i
                moved = pltpu.roll(tabs[r], lax.rem(r * 4 + N - z * line - (x // 2) * 4, N), 1)
                part = jnp.where(lane8 // 4 == r, moved, part)
        tabc[dist] = part

    def table_copy(dist):
        return pltpu.make_async_copy(tabc.at[dist], tabs_sm.at[dist], loc.at[2])

    def far_tiles(f0, acc):
        for ff in range(4):
            f = f0 * 4 + ff
            w = tabf_sm[2 * CAP, f]
            sums = tile(t_hi[0, w], t_lo[0, w], f_hi[f], f_lo[f], kf_row, kf_col, f)
            acc = acc + jnp.where(sub8 == f, sums, 0.0)
        return acc

    for h in range(1, hops + 1):
        final = h == hops
        ways = ((-h, z_plus, up), (h, z_minus, down))
        w_plus[h].wait_recv()
        if not final:
            w_plus[h + 1] = send(two(-h, 0), two(-h - 1, 0), up)
        w_core[hops if final else -h] = send(two(-h, 0), two(-h, 1), partner)
        if not final:
            w_minus[h].wait_recv()
            if h + 1 < hops:
                w_minus[h + 1] = send(two(h, 0), two(h + 1, 0), down)
            w_core[h] = send(two(h, 0), two(h, 1), partner)
        for p in range(3):
            bx, first = pieces[p]
            rows = pl.ds(first, half)
            for k, (dz, got, onward) in enumerate(ways):
                got[h, p].wait_recv()
                if h + 1 < hops:
                    got[h + 1, p] = send(piece(dz, p), piece(-h - 1 if k == 0 else h + 1, p), onward)
                elif h + 1 == hops:
                    got[hops, p] = send(piece(dz, p, k * quarter, quarter), piece(hops, p, k * quarter, quarter), onward)
            for dz in (-h, h)[: 1 if final else 2]:
                key = hops if final else dz
                if p == 0:
                    post[key] = send(s_raw.at[rel(dz, 0, 0), hi], s_raw.at[rel(dz, 0, 1), hi], mate)
                cores.setdefault(key, []).append(
                    send(s_raw.at[rel(dz, 0, bx), rows], s_raw.at[rel(dz, 1, bx), rows], partner))
            if p == (0 if final else 1):
                dist = h - 1
                compact(dist)
                for dz in ((0,) if dist == 0 else (-dist, dist)):
                    for copy in cores[dz]:
                        copy.wait_recv()
                    norm_lines(dz, 0)
                    if dz == (0 if dist == 0 else -dist):
                        table_copy(dist).start()
                    norm_lines(dz, 1)
                table_copy(dist).wait()
                place, places = (0, 1) if dist == 0 else (2 * dist - 1, 2)
                if h < hops - 1:
                    builds(place, places, (0,), True, False)
                if h == 2:
                    w_far.wait_recv()
                    far_table = pltpu.make_async_copy(tabf, tabf_sm, loc.at[3])
                    far_table.start()
                    f_far.wait_recv()

                    def far_unit(i, _):
                        for w in range(sb):
                            f_hi[w], f_lo[w] = unit(f_raw[w], True)
                        return 0

                    lax.fori_loop(0, 1, far_unit, 0)
                    far_table.wait()
                    rf0[...] = lax.fori_loop(0, sb // 4, far_tiles, jnp.zeros((8, N), F32))
                if h == hops - 1:
                    builds(place, places, (0,), True, False)
                    t_pair.wait_recv()
                    norm_t(1)
                    builds(0, place + places, (1,), False, True)
                if final:
                    builds(place, places, (0, 1), True, True)
        if final:
            compact(hops)
            for copy in cores[hops]:
                copy.wait_recv()
            norm_lines(hops, 0)
            table_copy(hops).start()
            table_copy(hops).wait()
            last_build(0)
        for dz in (-h, h)[: 1 if final else 2]:
            key = hops if final else dz
            post[key].wait_recv()
            cores[key].append(send(s_raw.at[rel(dz, 0, 1), hi], s_raw.at[rel(dz, 1, 1), hi], partner))
    cores[hops][-1].wait_recv()
    norm_lines(hops, 1)
    last_build(1)

    others = [(dz,) + o for dz in range(nz) for o in four if (dz,) + o != (0, 0, 0)]
    others.sort(key=lambda o: -min(o[0], nz - o[0]))

    def exchange(src, dst, k, to_dev):
        return pltpu.make_async_remote_copy(
            src_ref=src, dst_ref=dst, send_sem=ex_snd.at[k], recv_sem=ex_rcv.at[k],
            device_id=to_dev, device_id_type=MESH)

    def group(j):
        return (lax.rem(nz - j, nz), j), (j + 1, j + 1)

    def spread(v, r):
        h, l = halves(v)
        return jnp.where(sub16 == r, h, jnp.where(sub16 == r + 8, l, 0.0)).astype(BF16)

    def product(lhs, tiles):
        o = nn(jnp.concatenate([v for v in lhs for _ in range(2)], axis=1), tiles)
        return o[:8] + o[8:]

    def rows_pass(rp, rpi, rf):
        def body(r0, _):
            j = hops - 1 - r0
            for dz, dist in group(j):
                for flip, bx in four:
                    r = dz * 4 + flip * 2 + bx
                    lhs = []
                    for t in range(PAIR):
                        for u in range(CAP):
                            b, q = tabs_sm[dist, u, lane_of(r, t)], tabs_sm[dist, CAP + u, lane_of(r, t)]
                            lhs.append(spread(ts[t, pl.ds(jnp.maximum(q, 0), 1), :], b))
                    rp[r] = product(lhs, k_row[dz * 2 + flip, pl.ds(bx * near * 2 * N, near * 2 * N), :])
            for dz, _ in group(j):
                send_rows(rp, rpi, dz)
            return 0

        lax.fori_loop(0, hops, body, 0)
        lhs = [spread(ts[0, pl.ds(tabf_sm[2 * CAP, f], 1), :], f) for f in range(sb)]
        rf[...] = product(lhs, kf_row[...])

    def cols_pass(so, ss, sf, far_copy):
        def body(j, accs):
            accs = list(accs)
            for dz, _ in group(j):
                for flip, bx in four:
                    copy = from_line(so, ss, ag_snd, ag_rcv, dz, flip, bx, True)
                    if (flip, bx) == (0, 0):
                        pl.when(dz > 0)(copy.wait_recv)
                    else:
                        copy.wait_recv()
            for dz, _ in group(j):
                for i in range(4):
                    ssl[dz * 4 + i] = ss[dz * 4 + i]
            for dz, dist in group(j):
                for flip in range(2):
                    lhs = []
                    slots = [(bx, t, u) for bx in range(2) for t in range(PAIR) for u in range(CAP)]
                    for k, (bx, t, u) in enumerate(slots):
                        r = dz * 4 + flip * 2 + bx
                        b = tabs_sm[dist, u, lane_of(r, t)]
                        lhs.append(spread(ssl[r, pl.ds(jnp.maximum(b, 0), 1), :], k))
                    o = product(lhs, k_col[dz * 2 + flip])
                    for k, (bx, t, u) in enumerate(slots):
                        q = tabs_sm[dist, CAP + u, lane_of(dz * 4 + flip * 2 + bx, t)]
                        accs[t] = accs[t] + jnp.where(sub32 == q, o[k : k + 1], 0.0)
            return tuple(accs)

        zero = jnp.zeros((tb_dev, N), F32)
        accs = list(lax.fori_loop(0, hops, body, (zero,) * PAIR))
        far_copy.wait_recv()
        lhs = [spread(sf[f : f + 1, :], f) for f in range(sb)]
        o = product(lhs, kf_col[...])
        for f in range(sb):
            accs[0] = accs[0] + jnp.where(sub32 == tabf_sm[2 * CAP, f], o[f : f + 1], 0.0)
        return accs

    mass_pair.wait_recv()
    for it, (rp, rpi, rf, rfi, so, ss, sf, co, ci) in enumerate((
        (rp0, rpi0, rf0, rfi0, so0, ss0, sf0, co0, ci0),
        (rp1, rpi1, rf1, rfi1, so1, ss1, sf1, co1, ci1),
    )):
        last = it == ITERS - 1
        far_rows = exchange(rf, rfi, 0, behind)
        far_scale = exchange(so, sf, 1, ahead)
        if it > 0:
            rows_pass(rp, rpi, rf)
        far_rows.start()
        total = rp[0]
        for o in others[::-1]:
            from_line(rp, rpi, rs_snd, rs_rcv, *o).wait_recv()
        far_rows.wait_recv()
        total = total + rfi[...]
        for o in others:
            total = total + rpi[rel(*o)]
        scale = smass[...] / (DUSTBIN + total)
        so[...] = scale
        ss[0] = scale
        if last:
            out[:sb] = scale
        for o in others:
            to_line(so, ss, ag_snd, ag_rcv, *o, True).start()
        far_scale.start()
        accs = cols_pass(so, ss, sf, far_scale)
        co[1] = accs[1]
        if last:
            swap = exchange(co.at[1], ci.at[1], 3, pair)
        else:
            co[0] = accs[0]
            swap = exchange(co, ci, 2, pair)
        swap.start()
        for left, sem in ((rp, rs_snd), (ss, ag_snd)):
            pltpu.make_async_copy(left.at[pl.ds(1, nr - 1)], left.at[pl.ds(1, nr - 1)], sem.at[0]).wait()
        far_rows.wait_send()
        far_scale.wait_send()
        swap.wait_recv()
        scale = tmass[...] / (DUSTBIN + (accs[0] + ci[1]))
        if last:
            out[sb:] = scale
        else:
            ts[0] = scale
            ts[1] = tmass_pair[...] / (DUSTBIN + (accs[1] + ci[0]))
        swap.wait_send()
    for copy in sent:
        copy.wait_send()
    assert count[0] == COPIES


def local(ng, nz, semb, temb, smass, tmass, cdev, cblk):
    sb, tb = semb.shape[0], temb.shape[0]
    nr = 4 * nz
    slots = 2 * PAIR * CAP * 2 * N
    vm = pltpu.VMEM
    dma = pltpu.SemaphoreType.DMA
    tile = (N, N)
    blocks = vm((nr, sb, N), F32)
    source, target = vm((sb, N), F32), vm((tb, N), F32)
    pair = vm((PAIR, tb, N), F32)
    scratch = [
        vm((nr, sb) + tile, F32), vm((PAIR, tb) + tile, F32), vm((sb,) + tile, F32),
        vm((nr * sb,) + tile, BF16), vm((nr * sb,) + tile, BF16),
        vm((PAIR, tb) + tile, BF16), vm((PAIR, tb) + tile, BF16),
        vm((sb,) + tile, BF16), vm((sb,) + tile, BF16),
        vm((nr // 2, slots, N), BF16), vm((nr // 2, slots, N), BF16),
        vm((sb * 2 * N, N), BF16), vm((sb * 2 * N, N), BF16),
        vm((8, N), I32), vm((nr, 8, N), I32), vm((8, N), I32), vm((nz // 2 + 1, 8, N), I32),
        pltpu.SMEM((nz // 2 + 1, 8, N), I32), pltpu.SMEM((8, N), I32),
    ]
    scratch += [blocks] * 7 + [source] * 8 + [pair] * 5
    scratch += [vm(a.shape, a.dtype) for a in (smass, tmass, cdev, cblk)] + [target]
    scratch += [dma((COPIES,))] * 2 + [dma((1,)), dma((nr,)), dma((1,)), dma((nr,))] + [dma((4,))] * 2 + [dma((8,))]
    any_, vmem = pl.BlockSpec(memory_space=pl.ANY), pl.BlockSpec(memory_space=pltpu.VMEM)
    both = pl.pallas_call(
        functools.partial(kernel, ng, nz, sb, tb),
        out_shape=jax.ShapeDtypeStruct((sb + tb, N), F32),
        in_specs=[any_] * 6,
        out_specs=vmem,
        scratch_shapes=scratch,
        compiler_params=pltpu.CompilerParams(
            collective_id=0, has_side_effects=True, vmem_limit_bytes=VMEM_BYTES),
        name="sinkhorn",
    )(semb, temb, smass, tmass, cdev, cblk)

    def split(both_ref, src_ref, tgt_ref):
        src_ref[...] = both_ref[:sb]
        tgt_ref[...] = both_ref[sb:]

    return pl.pallas_call(
        split,
        out_shape=(jax.ShapeDtypeStruct(smass.shape, F32), jax.ShapeDtypeStruct(tmass.shape, F32)),
        in_specs=[vmem],
        out_specs=(vmem, vmem),
        name="split",
    )(both)


def solution(mesh):
    placed = (
        P(("group", "dev"), None, None),
        P(("group", "dev"), None, None),
        P(("group", "dev"), None),
        P(("group", "dev"), None),
        P(("group", "dev"), None),
        P(("group", "dev"), None),
    )
    ng, nz = mesh.shape["group"], mesh.shape["dev"] // (2 * NX)
    return jax.shard_map(
        functools.partial(local, ng, nz),
        mesh=mesh,
        in_specs=placed,
        out_specs=(P(("group", "dev"), None), P(("group", "dev"), None)),
        check_vma=False,
    )
```

```python
import functools

import jax
import jax.numpy as jnp
from jax import lax
from jax.experimental import pallas as pl
from jax.experimental.pallas import tpu as pltpu
from jax.sharding import PartitionSpec as P

MESH = pl.DeviceIdType.MESH
N = 128
NX = 4
NEAR = 7
CAP = 2
TARGETS = 4
VMEM_BYTES = 62 * 1024 * 1024
ITERS = 2
EMPTY = -64
COPIES = 49
DUSTBIN = 0.5
EPSILON = 1e-6
GAIN = 1.0 / (N * 0.1)
SHARE = 1.0 / (8.0 * N)

F32, BF16, I32 = jnp.float32, jnp.bfloat16, jnp.int32


def nn(a, b):
    return lax.dot_general(a, b, (((1,), (0,)), ((), ())), preferred_element_type=F32)


def halves(v):
    hi = v.astype(BF16).astype(F32)
    return hi, v - hi


def kernel(ng, nz, sb, tb_dev, *refs):
    (semb, temb, smass_in, tmass_in, cdev_in, cblk_in, out,
     s_raw, t_raw, f_raw, s_hi, s_lo, t_hi, t_lo, f_hi, f_lo, k_row, k_col, kf_row, kf_col,
     tab, tabs, tabf, tabc, tabs_sm, tabf_sm,
     rp0, rp1, rpi0, rpi1, ss0, ss1, ssl, rf0, rf1, rfi0, rfi1, so0, so1, sf0, sf1,
     co0, co1, ci0, ci1, wo0, wo1, wi0, wi1, ts, smass, cdev, cblk, tmass,
     snd, rcv, rs_snd, rs_rcv, ag_snd, ag_rcv, ex_snd, ex_rcv, loc) = refs
    nr = 2 * nz
    hops = nz // 2
    half = sb // 2
    quarter = sb // 4
    line = 2 * NX
    g, d = lax.axis_index("group"), lax.axis_index("dev")
    z, x, c = d // line, (d // 2) % NX, d % 2

    def at(zz, xx, cc):
        return (g, zz * line + xx * 2 + cc)

    def dev(dz, bx):
        return at(lax.rem(z + dz, nz), NX - 1 - x if bx else x, c)

    def rel(dz, bx):
        return (dz % nz) * 2 + bx

    up, down, mate = dev(1, 0), dev(nz - 1, 0), dev(0, 1)
    partner = at(z, x, 1 - c)
    pair = at(z, x + 1 - 2 * lax.rem(x, 2), c)
    ahead, behind = (lax.rem(g + 1, ng), d), (lax.rem(g + ng - 1, ng), d)

    count = [0]
    sent = []

    def send(src, dst, to_dev):
        k = count[0]
        count[0] += 1
        copy = pltpu.make_async_remote_copy(
            src_ref=src, dst_ref=dst, send_sem=snd.at[k], recv_sem=rcv.at[k],
            device_id=to_dev, device_id_type=MESH)
        copy.start()
        sent.append(copy)
        return copy

    barrier = pltpu.get_barrier_semaphore()
    greeted = (up, down, mate, pair, partner, ahead, behind)
    for other in greeted:
        pl.semaphore_signal(barrier, inc=1, device_id=other, device_id_type=MESH)
    own_s = pltpu.make_async_copy(semb, s_raw.at[0], loc.at[0])
    own_t = pltpu.make_async_copy(temb, t_raw.at[0], loc.at[1])
    small = [pltpu.make_async_copy(a, b, loc.at[4 + i]) for i, (a, b) in enumerate(
        ((cdev_in, cdev), (cblk_in, cblk), (smass_in, smass), (tmass_in, tmass.at[0])))]
    for copy in small:
        copy.start()
    own_s.start()
    own_t.start()
    for copy in small:
        copy.wait()

    lane = lax.broadcasted_iota(I32, (1, N), 1)
    run = jnp.zeros((1, N), I32)
    rows = [jnp.full((1, N), EMPTY, I32) for _ in range(2 * CAP)]
    far = jnp.zeros((1, N), I32)
    for b in range(sb):
        hit = jnp.zeros((1, N), I32)
        which = jnp.zeros((1, N), I32)
        for k in range(NEAR):
            m = cdev[b : b + 1, k : k + 1] == lane
            hit = jnp.where(m, 1, hit)
            which = jnp.where(m, cblk[b : b + 1, k : k + 1], which)
        for u in range(CAP):
            m = (hit == 1) & (run == u)
            rows[u] = jnp.where(m, b, rows[u])
            rows[CAP + u] = jnp.where(m, which, rows[CAP + u])
        run = run + hit
        far = jnp.where(lane == b, cblk[b : b + 1, NEAR : NEAR + 1], far)
    table = jnp.concatenate(rows + [far] + [jnp.zeros((1, N), I32)] * (7 - 2 * CAP), axis=0)
    tab[...] = table
    tabs[0] = table

    pl.semaphore_wait(barrier, len(greeted))

    lo, hi = pl.ds(0, half), pl.ds(half, half)
    pieces = ((0, half), (0, 0), (1, 0))
    z_plus, z_minus = {}, {}

    def piece(dz, p, start=0, size=half):
        bx, first = pieces[p]
        return s_raw.at[rel(dz, bx), pl.ds(first + start, size)]

    w_mate = send(tab, tabs.at[1], mate)
    pre = send(semb.at[lo], s_raw.at[rel(0, 1), lo], mate)
    for p in (0, 1):
        part = semb.at[pl.ds(pieces[p][1], half)]
        z_plus[1, p] = send(part, piece(-1, p), up)
        z_minus[1, p] = send(part, piece(1, p), down)
    post = {0: send(semb.at[hi], s_raw.at[rel(0, 1), hi], mate)}
    t_pair = send(temb, t_raw.at[1], pair)
    mass_pair = send(tmass_in, tmass.at[1], pair)
    t_core = send(temb, t_raw.at[2], partner)
    mass_core = send(tmass_in, tmass.at[2], partner)
    w_far = send(tab, tabf, ahead)
    f_far = send(semb, f_raw, ahead)
    w_plus, w_minus = {}, {}

    def two(dz):
        return tabs.at[pl.ds(rel(dz, 0), 2)]

    def place(p):
        dist = (p + 1) // 2
        return jnp.where(p % 2 == 1, dist, lax.rem(nz - dist, nz)), dist

    def unit(v, turned):
        if turned:
            v = v.T
        v = v * lax.rsqrt(jnp.mean(v * v, axis=0 if turned else 1, keepdims=True) + EPSILON)
        h = v.astype(BF16)
        return h, (v - h.astype(F32)).astype(BF16)

    def norm_lines(first_line, lines):
        def one(i, _):
            dz, _dist = place((first_line + i) // 2)
            r = dz * 2 + (first_line + i) % 2
            for w in range(sb):
                s_hi[r * sb + w], s_lo[r * sb + w] = unit(s_raw[r, w], True)
            return 0

        lax.fori_loop(0, lines, one, 0)

    def norm_t(t):
        def one(i, _):
            for w in range(8):
                t_hi[t, i * 8 + w], t_lo[t, i * 8 + w] = unit(t_raw[t, i * 8 + w], False)
            return 0

        lax.fori_loop(0, tb_dev // 8, one, 0)

    w_mate.wait_recv()
    w_plus[1] = send(two(0), two(-1), up)
    w_minus[1] = send(two(0), two(1), down)
    pre.wait_recv()
    z_plus[1, 2] = send(piece(0, 2), piece(-1, 2), up)
    z_minus[1, 2] = send(piece(0, 2), piece(1, 2), down)
    own_t.wait()
    norm_t(0)
    t_core.wait_recv()
    norm_t(2)
    own_s.wait()
    post[0].wait_recv()

    sub8 = lax.broadcasted_iota(I32, (8, N), 0)
    sub16 = lax.broadcasted_iota(I32, (16, N), 0)
    sub32 = lax.broadcasted_iota(I32, (tb_dev, N), 0)

    def lane_of(r, t):
        return r * 4 + lax.rem(x + t, 2) * 2 + (c if t < 2 else 1 - c)

    def two_terms(v, ref, k):
        h = v.astype(BF16)
        ref[pl.ds(k * 2 * N, N), :] = h
        ref[pl.ds(k * 2 * N + N, N), :] = (v - h.astype(F32)).astype(BF16)

    def tile(b_hi, b_lo, a_hi, a_lo, row, col, k):
        dots = nn(b_hi, a_hi) + (nn(b_lo, a_hi) + nn(b_hi, a_lo))
        e = jnp.exp(dots * GAIN) * SHARE
        two_terms(e, row, k)
        two_terms(e.T, col, k)
        return jnp.sum(e, axis=0, keepdims=True)

    def to_line(src, dst, snds, rcvs, dz, bx, whole=False):
        r, back = dz * 2 + bx, lax.rem(nz - dz, nz) * 2 + bx
        return pltpu.make_async_remote_copy(
            src_ref=src if whole else src.at[r], dst_ref=dst.at[back], send_sem=snds.at[0],
            recv_sem=rcvs.at[back], device_id=dev(dz, bx), device_id_type=MESH)

    def from_line(src, dst, snds, rcvs, dz, bx, whole=False):
        r = dz * 2 + bx
        return pltpu.make_async_remote_copy(
            src_ref=src if whole else src.at[r], dst_ref=dst.at[r], send_sem=snds.at[0],
            recv_sem=rcvs.at[r], device_id=dev(dz, bx), device_id_type=MESH)

    def send_rows(rp, rpi, dz, bxs=(0, 1)):
        for bx in bxs:
            copy = to_line(rp, rpi, rs_snd, rs_rcv, dz, bx)
            if bx == 0:
                pl.when(dz > 0)(copy.start)
            else:
                copy.start()

    def build(dz, dist, bxs, targets, first, done):
        for bx in bxs:
            r = dz * 2 + bx
            acc = jnp.zeros((8, N), F32)
            for t in targets:
                for u in range(CAP):
                    b, q = tabs_sm[dist, u, lane_of(r, t)], tabs_sm[dist, CAP + u, lane_of(r, t)]
                    s, w = r * sb + jnp.maximum(b, 0), jnp.maximum(q, 0)
                    sums = tile(t_hi[t, w], t_lo[t, w], s_hi[s], s_lo[s], k_row.at[r], k_col.at[r], t * CAP + u)
                    acc = acc + jnp.where(sub8 == b, sums, 0.0)
            rp0[r] = acc if first else rp0[r] + acc
        if done:
            send_rows(rp0, rpi0, dz, bxs)

    def builds(first_place, places, targets, first, done):
        def one(i, _):
            dz, dist = place(first_place + i)
            build(dz, dist, (0, 1), targets, first, done)
            return 0

        lax.fori_loop(0, places, one, 0)

    def last_build(bx):
        def one(i, _):
            build(hops + i, hops, (bx,), range(TARGETS), True, True)
            return 0

        lax.fori_loop(0, 1, one, 0)

    lane8 = lax.broadcasted_iota(I32, (8, N), 1)

    def compact(dist):
        part = jnp.zeros((8, N), I32)
        for dz in (0,) if dist == 0 else (hops,) if dist == hops else (-dist, dist):
            for bx in range(2):
                r = rel(dz, bx)
                moved = pltpu.roll(tabs[r], lax.rem(r * 4 + N - z * line - (x // 2) * 4, N), 1)
                part = jnp.where(lane8 // 4 == r, moved, part)
        tabc[dist] = part

    def table_copy(dist):
        return pltpu.make_async_copy(tabc.at[dist], tabs_sm.at[dist], loc.at[2])

    def far_tiles(f0, acc):
        for ff in range(4):
            f = f0 * 4 + ff
            w = tabf_sm[2 * CAP, f]
            sums = tile(t_hi[0, w], t_lo[0, w], f_hi[f], f_lo[f], kf_row, kf_col, f)
            acc = acc + jnp.where(sub8 == f, sums, 0.0)
        return acc

    for h in range(1, hops + 1):
        final = h == hops
        w_plus[h].wait_recv()
        if not final:
            w_plus[h + 1] = send(two(-h), two(-h - 1), up)
            w_minus[h].wait_recv()
            if h + 1 < hops:
                w_minus[h + 1] = send(two(h), two(h + 1), down)
        for p in range(3):
            for k, (dz, got, onward) in enumerate(((-h, z_plus, up), (h, z_minus, down))):
                got[h, p].wait_recv()
                if h + 1 < hops:
                    got[h + 1, p] = send(piece(dz, p), piece(-h - 1 if k == 0 else h + 1, p), onward)
                elif h + 1 == hops:
                    got[hops, p] = send(piece(dz, p, k * quarter, quarter), piece(hops, p, k * quarter, quarter), onward)
            if p == 0:
                for dz in (-h, h)[: 1 if final else 2]:
                    post[dz] = send(s_raw.at[rel(dz, 0), hi], s_raw.at[rel(dz, 1), hi], mate)
            if p == (0 if final else 1):
                dist = h - 1
                first, places = (0, 1) if dist == 0 else (2 * dist - 1, 2)
                compact(dist)
                norm_lines(2 * first, places)
                table_copy(dist).start()
                norm_lines(2 * first + places, places)
                table_copy(dist).wait()
                if not final:
                    builds(first, places, (0, 2), True, False)
                if h == 2:
                    w_far.wait_recv()
                    far_table = pltpu.make_async_copy(tabf, tabf_sm, loc.at[3])
                    far_table.start()
                    f_far.wait_recv()

                    def far_unit(i, _):
                        for w in range(sb):
                            f_hi[w], f_lo[w] = unit(f_raw[w], True)
                        return 0

                    lax.fori_loop(0, 1, far_unit, 0)
                    far_table.wait()
                    rf0[...] = lax.fori_loop(0, sb // 4, far_tiles, jnp.zeros((8, N), F32))
                    mass_pair.wait_recv()
                    mass_diagonal = send(tmass.at[1], tmass.at[3], partner)
                if h == hops - 1:
                    t_pair.wait_recv()
                    t_diagonal = send(t_raw.at[1], t_raw.at[3], partner)
                    norm_t(1)
                    t_diagonal.wait_recv()
                    norm_t(3)
                    builds(0, first + places, (1, 3), False, True)
                if final:
                    builds(first, places, range(TARGETS), True, True)
        if final:
            compact(hops)
            norm_lines(2 * (nz - 1), 1)
            table_copy(hops).start()
            table_copy(hops).wait()
            last_build(0)
        for dz in (-h, h)[: 1 if final else 2]:
            post[dz].wait_recv()
    norm_lines(2 * nz - 1, 1)
    last_build(1)

    others = [(dz, bx) for dz in range(nz) for bx in range(2) if (dz, bx) != (0, 0)]
    others.sort(key=lambda o: -min(o[0], nz - o[0]))

    def exchange(src, dst, k, to_dev):
        return pltpu.make_async_remote_copy(
            src_ref=src, dst_ref=dst, send_sem=ex_snd.at[k], recv_sem=ex_rcv.at[k],
            device_id=to_dev, device_id_type=MESH)

    def group(j):
        return (lax.rem(nz - j, nz), j), (j + 1, j + 1)

    def spread(v, r):
        h, l = halves(v)
        return jnp.where(sub16 == r, h, jnp.where(sub16 == r + 8, l, 0.0)).astype(BF16)

    def product(lhs, tiles):
        o = nn(jnp.concatenate([v for v in lhs for _ in range(2)], axis=1), tiles)
        return o[:8] + o[8:]

    def rows_pass(rp, rpi, rf):
        def body(r0, _):
            j = hops - 1 - r0
            for dz, dist in group(j):
                for bx in range(2):
                    r = dz * 2 + bx
                    lhs = []
                    for t in range(TARGETS):
                        for u in range(CAP):
                            b, q = tabs_sm[dist, u, lane_of(r, t)], tabs_sm[dist, CAP + u, lane_of(r, t)]
                            lhs.append(spread(ts[t, pl.ds(jnp.maximum(q, 0), 1), :], b))
                    rp[r] = product(lhs, k_row[r])
            for dz, _ in group(j):
                send_rows(rp, rpi, dz)
            return 0

        lax.fori_loop(0, hops, body, 0)
        lhs = [spread(ts[0, pl.ds(tabf_sm[2 * CAP, f], 1), :], f) for f in range(sb)]
        rf[...] = product(lhs, kf_row[...])

    def cols_pass(so, ss, sf, far_copy):
        def body(j, accs):
            accs = list(accs)
            for dz, _ in group(j):
                for bx in range(2):
                    copy = from_line(so, ss, ag_snd, ag_rcv, dz, bx, True)
                    if bx == 0:
                        pl.when(dz > 0)(copy.wait_recv)
                    else:
                        copy.wait_recv()
            for dz, _ in group(j):
                for bx in range(2):
                    ssl[dz * 2 + bx] = ss[dz * 2 + bx]
            slots = [(t, u) for t in range(TARGETS) for u in range(CAP)]
            for dz, dist in group(j):
                for bx in range(2):
                    r = dz * 2 + bx
                    lhs = []
                    for k, (t, u) in enumerate(slots):
                        b = tabs_sm[dist, u, lane_of(r, t)]
                        lhs.append(spread(ssl[r, pl.ds(jnp.maximum(b, 0), 1), :], k))
                    o = product(lhs, k_col[r])
                    for k, (t, u) in enumerate(slots):
                        q = tabs_sm[dist, CAP + u, lane_of(r, t)]
                        accs[t] = accs[t] + jnp.where(sub32 == q, o[k : k + 1], 0.0)
            return tuple(accs)

        zero = jnp.zeros((tb_dev, N), F32)
        accs = list(lax.fori_loop(0, hops, body, (zero,) * TARGETS))
        far_copy.wait_recv()
        lhs = [spread(sf[f : f + 1, :], f) for f in range(sb)]
        o = product(lhs, kf_col[...])
        for f in range(sb):
            accs[0] = accs[0] + jnp.where(sub32 == tabf_sm[2 * CAP, f], o[f : f + 1], 0.0)
        return accs

    mass_core.wait_recv()
    mass_diagonal.wait_recv()
    for it, (rp, rpi, rf, rfi, so, ss, sf, co, ci, wo, wi) in enumerate((
        (rp0, rpi0, rf0, rfi0, so0, ss0, sf0, co0, ci0, wo0, wi0),
        (rp1, rpi1, rf1, rfi1, so1, ss1, sf1, co1, ci1, wo1, wi1),
    )):
        last = it == ITERS - 1
        far_rows = exchange(rf, rfi, 0, behind)
        far_scale = exchange(so, sf, 1, ahead)
        if it > 0:
            rows_pass(rp, rpi, rf)
        far_rows.start()
        total = rp[0]
        for o in others[::-1]:
            from_line(rp, rpi, rs_snd, rs_rcv, *o).wait_recv()
        far_rows.wait_recv()
        total = total + rfi[...]
        for o in others:
            total = total + rpi[rel(*o)]
        scale = smass[...] / (DUSTBIN + total)
        so[...] = scale
        ss[0] = scale
        if last:
            out[:sb] = scale
        for o in others:
            to_line(so, ss, ag_snd, ag_rcv, *o, True).start()
        far_scale.start()
        accs = cols_pass(so, ss, sf, far_scale)
        theirs = pl.ds(2, 2) if last else pl.ds(0, TARGETS)
        for t in range(2 if last else 0, TARGETS):
            co[t] = accs[t]
        cores = exchange(co.at[theirs], ci.at[theirs], 2 + 2 * it, partner)
        cores.start()
        for left, sem in ((rp, rs_snd), (ss, ag_snd)):
            pltpu.make_async_copy(left.at[pl.ds(1, nr - 1)], left.at[pl.ds(1, nr - 1)], sem.at[0]).wait()
        far_rows.wait_send()
        far_scale.wait_send()
        cores.wait_recv()
        sums = [accs[t] + ci[t ^ 2] for t in range(2 if last else TARGETS)]
        moving = pl.ds(1, 1) if last else pl.ds(0, TARGETS)
        for t in (1,) if last else range(TARGETS):
            wo[t] = sums[t]
        swap = exchange(wo.at[moving], wi.at[moving], 3 + 2 * it, pair)
        swap.start()
        swap.wait_recv()
        if last:
            out[sb:] = tmass[0] / (DUSTBIN + (sums[0] + wi[1]))
        else:
            for t in range(TARGETS):
                ts[t] = tmass[t] / (DUSTBIN + (sums[t] + wi[t ^ 1]))
        cores.wait_send()
        swap.wait_send()
    for copy in sent:
        copy.wait_send()
    assert count[0] == COPIES


def local(ng, nz, semb, temb, smass, tmass, cdev, cblk):
    sb, tb = semb.shape[0], temb.shape[0]
    nr = 2 * nz
    slots = TARGETS * CAP * 2 * N
    vm = pltpu.VMEM
    dma = pltpu.SemaphoreType.DMA
    tile = (N, N)
    blocks = vm((nr, sb, N), F32)
    source, targets = vm((sb, N), F32), vm((TARGETS, tb, N), F32)
    scratch = [
        vm((nr, sb) + tile, F32), vm((TARGETS, tb) + tile, F32), vm((sb,) + tile, F32),
        vm((nr * sb,) + tile, BF16), vm((nr * sb,) + tile, BF16),
        vm((TARGETS, tb) + tile, BF16), vm((TARGETS, tb) + tile, BF16),
        vm((sb,) + tile, BF16), vm((sb,) + tile, BF16),
        vm((nr, slots, N), BF16), vm((nr, slots, N), BF16),
        vm((sb * 2 * N, N), BF16), vm((sb * 2 * N, N), BF16),
        vm((8, N), I32), vm((nr, 8, N), I32), vm((8, N), I32), vm((nz // 2 + 1, 8, N), I32),
        pltpu.SMEM((nz // 2 + 1, 8, N), I32), pltpu.SMEM((8, N), I32),
    ]
    scratch += [blocks] * 7 + [source] * 8 + [targets] * 9
    scratch += [vm(a.shape, a.dtype) for a in (smass, cdev, cblk)] + [targets]
    scratch += [dma((COPIES,))] * 2 + [dma((1,)), dma((nr,)), dma((1,)), dma((nr,))] + [dma((6,))] * 2 + [dma((8,))]
    any_, vmem = pl.BlockSpec(memory_space=pl.ANY), pl.BlockSpec(memory_space=pltpu.VMEM)
    both = pl.pallas_call(
        functools.partial(kernel, ng, nz, sb, tb),
        out_shape=jax.ShapeDtypeStruct((sb + tb, N), F32),
        in_specs=[any_] * 6,
        out_specs=vmem,
        scratch_shapes=scratch,
        compiler_params=pltpu.CompilerParams(
            collective_id=0, has_side_effects=True, vmem_limit_bytes=VMEM_BYTES),
        name="sinkhorn",
    )(semb, temb, smass, tmass, cdev, cblk)

    def split(both_ref, src_ref, tgt_ref):
        src_ref[...] = both_ref[:sb]
        tgt_ref[...] = both_ref[sb:]

    return pl.pallas_call(
        split,
        out_shape=(jax.ShapeDtypeStruct(smass.shape, F32), jax.ShapeDtypeStruct(tmass.shape, F32)),
        in_specs=[vmem],
        out_specs=(vmem, vmem),
        name="split",
    )(both)


def solution(mesh):
    placed = (
        P(("group", "dev"), None, None),
        P(("group", "dev"), None, None),
        P(("group", "dev"), None),
        P(("group", "dev"), None),
        P(("group", "dev"), None),
        P(("group", "dev"), None),
    )
    ng, nz = mesh.shape["group"], mesh.shape["dev"] // (2 * NX)
    return jax.shard_map(
        functools.partial(local, ng, nz),
        mesh=mesh,
        in_specs=placed,
        out_specs=(P(("group", "dev"), None), P(("group", "dev"), None)),
        check_vma=False,
    )
```

```python
import functools

import jax
import jax.numpy as jnp
from jax import lax
from jax.experimental import pallas as pl
from jax.experimental.pallas import tpu as pltpu
from jax.sharding import PartitionSpec as P

MESH = pl.DeviceIdType.MESH
N = 128
NX = 4
NEAR = 7
CAP = 2
TARGETS = 4
VMEM_BYTES = 62 * 1024 * 1024
ITERS = 2
EMPTY = -64
COPIES = 49
DUSTBIN = 0.5
EPSILON = 1e-6
GAIN = 1.0 / (N * 0.1)
SHARE = 1.0 / (8.0 * N)

F32, BF16, I32 = jnp.float32, jnp.bfloat16, jnp.int32


def nn(a, b):
    return lax.dot_general(a, b, (((1,), (0,)), ((), ())), preferred_element_type=F32)


def halves(v):
    hi = v.astype(BF16).astype(F32)
    return hi, v - hi


def kernel(ng, nz, sb, tb_dev, *refs):
    (semb, temb, smass_in, tmass_in, cdev_in, cblk_in, out,
     s_raw, t_raw, f_raw, s_hi, s_lo, t_hi, t_lo, f_hi, f_lo, k_row, k_col, kf_row, kf_col,
     tab, tabs, tabf, tabc, tabs_sm, tabf_sm,
     rp0, rp1, rpi0, rpi1, ss0, ss1, ssl, rf0, rf1, rfi0, rfi1, so0, so1, sf0, sf1,
     co0, co1, ci0, ci1, wo0, wo1, wi0, wi1, ts, smass, cdev, cblk, tmass,
     snd, rcv, rs_snd, rs_rcv, ag_snd, ag_rcv, ex_snd, ex_rcv, loc) = refs
    nr = 2 * nz
    hops = nz // 2
    half = sb // 2
    quarter = sb // 4
    line = 2 * NX
    g, d = lax.axis_index("group"), lax.axis_index("dev")
    z, x, c = d // line, (d // 2) % NX, d % 2

    def at(zz, xx, cc):
        return (g, zz * line + xx * 2 + cc)

    def dev(dz, bx):
        return at(lax.rem(z + dz, nz), NX - 1 - x if bx else x, c)

    def rel(dz, bx):
        return (dz % nz) * 2 + bx

    up, down, mate = dev(1, 0), dev(nz - 1, 0), dev(0, 1)
    partner = at(z, x, 1 - c)
    pair = at(z, x + 1 - 2 * lax.rem(x, 2), c)
    ahead, behind = (lax.rem(g + 1, ng), d), (lax.rem(g + ng - 1, ng), d)

    count = [0]
    sent = []

    def send(src, dst, to_dev):
        k = count[0]
        count[0] += 1
        copy = pltpu.make_async_remote_copy(
            src_ref=src, dst_ref=dst, send_sem=snd.at[k], recv_sem=rcv.at[k],
            device_id=to_dev, device_id_type=MESH)
        copy.start()
        sent.append(copy)
        return copy

    barrier = pltpu.get_barrier_semaphore()
    greeted = (up, down, mate, pair, partner, ahead, behind)
    for other in greeted:
        pl.semaphore_signal(barrier, inc=1, device_id=other, device_id_type=MESH)
    own_s = pltpu.make_async_copy(semb, s_raw.at[0], loc.at[0])
    own_t = pltpu.make_async_copy(temb, t_raw.at[0], loc.at[1])
    small = [pltpu.make_async_copy(a, b, loc.at[4 + i]) for i, (a, b) in enumerate(
        ((cdev_in, cdev), (cblk_in, cblk), (smass_in, smass), (tmass_in, tmass.at[0])))]
    for copy in small:
        copy.start()
    own_s.start()
    own_t.start()
    for copy in small:
        copy.wait()

    lane = lax.broadcasted_iota(I32, (1, N), 1)
    run = jnp.zeros((1, N), I32)
    rows = [jnp.full((1, N), EMPTY, I32) for _ in range(2 * CAP)]
    far = jnp.zeros((1, N), I32)
    for b in range(sb):
        hit = jnp.zeros((1, N), I32)
        which = jnp.zeros((1, N), I32)
        for k in range(NEAR):
            m = cdev[b : b + 1, k : k + 1] == lane
            hit = jnp.where(m, 1, hit)
            which = jnp.where(m, cblk[b : b + 1, k : k + 1], which)
        for u in range(CAP):
            m = (hit == 1) & (run == u)
            rows[u] = jnp.where(m, b, rows[u])
            rows[CAP + u] = jnp.where(m, which, rows[CAP + u])
        run = run + hit
        far = jnp.where(lane == b, cblk[b : b + 1, NEAR : NEAR + 1], far)
    table = jnp.concatenate(rows + [far] + [jnp.zeros((1, N), I32)] * (7 - 2 * CAP), axis=0)
    tab[...] = table
    tabs[0] = table

    pl.semaphore_wait(barrier, len(greeted))

    lo, hi = pl.ds(0, half), pl.ds(half, half)
    pieces = ((0, half), (0, 0), (1, 0))
    z_plus, z_minus = {}, {}

    def piece(dz, p, start=0, size=half):
        bx, first = pieces[p]
        return s_raw.at[rel(dz, bx), pl.ds(first + start, size)]

    w_mate = send(tab, tabs.at[1], mate)
    pre = send(semb.at[lo], s_raw.at[rel(0, 1), lo], mate)
    for p in (0, 1):
        part = semb.at[pl.ds(pieces[p][1], half)]
        z_plus[1, p] = send(part, piece(-1, p), up)
        z_minus[1, p] = send(part, piece(1, p), down)
    post = {0: send(semb.at[hi], s_raw.at[rel(0, 1), hi], mate)}
    t_pair = send(temb, t_raw.at[1], pair)
    mass_pair = send(tmass_in, tmass.at[1], pair)
    t_core = send(temb, t_raw.at[2], partner)
    mass_core = send(tmass_in, tmass.at[2], partner)
    w_far = send(tab, tabf, ahead)
    f_far = send(semb, f_raw, ahead)
    w_plus, w_minus = {}, {}

    def two(dz):
        return tabs.at[pl.ds(rel(dz, 0), 2)]

    def place(p):
        dist = (p + 1) // 2
        return jnp.where(p % 2 == 1, dist, lax.rem(nz - dist, nz)), dist

    def unit(v, turned):
        if turned:
            v = v.T
        v = v * lax.rsqrt(jnp.mean(v * v, axis=0 if turned else 1, keepdims=True) + EPSILON)
        h = v.astype(BF16)
        return h, (v - h.astype(F32)).astype(BF16)

    def norm_lines(first_line, lines):
        def one(i, _):
            dz, _dist = place((first_line + i) // 2)
            r = dz * 2 + (first_line + i) % 2
            for w in range(sb):
                s_hi[r * sb + w], s_lo[r * sb + w] = unit(s_raw[r, w], True)
            return 0

        lax.fori_loop(0, lines, one, 0)

    def norm_t(t):
        def one(i, _):
            for w in range(8):
                t_hi[t, i * 8 + w], t_lo[t, i * 8 + w] = unit(t_raw[t, i * 8 + w], False)
            return 0

        lax.fori_loop(0, tb_dev // 8, one, 0)

    w_mate.wait_recv()
    w_plus[1] = send(two(0), two(-1), up)
    w_minus[1] = send(two(0), two(1), down)
    pre.wait_recv()
    z_plus[1, 2] = send(piece(0, 2), piece(-1, 2), up)
    z_minus[1, 2] = send(piece(0, 2), piece(1, 2), down)
    own_t.wait()
    norm_t(0)
    t_core.wait_recv()
    norm_t(2)
    own_s.wait()
    post[0].wait_recv()

    sub8 = lax.broadcasted_iota(I32, (8, N), 0)
    sub16 = lax.broadcasted_iota(I32, (16, N), 0)
    sub32 = lax.broadcasted_iota(I32, (tb_dev, N), 0)

    def lane_of(r, t):
        return r * 4 + lax.rem(x + t, 2) * 2 + (c if t < 2 else 1 - c)

    def two_terms(v, ref, k):
        h = v.astype(BF16)
        ref[pl.ds(k * 2 * N, N), :] = h
        ref[pl.ds(k * 2 * N + N, N), :] = (v - h.astype(F32)).astype(BF16)

    def tile(b_hi, b_lo, a_hi, a_lo, row, col, k):
        dots = nn(b_hi, a_hi) + (nn(b_lo, a_hi) + nn(b_hi, a_lo))
        e = jnp.exp(dots * GAIN) * SHARE
        two_terms(e, row, k)
        two_terms(e.T, col, k)
        return jnp.sum(e, axis=0, keepdims=True)

    def to_line(src, dst, snds, rcvs, dz, bx, whole=False):
        r, back = dz * 2 + bx, lax.rem(nz - dz, nz) * 2 + bx
        return pltpu.make_async_remote_copy(
            src_ref=src if whole else src.at[r], dst_ref=dst.at[back], send_sem=snds.at[0],
            recv_sem=rcvs.at[back], device_id=dev(dz, bx), device_id_type=MESH)

    def from_line(src, dst, snds, rcvs, dz, bx, whole=False):
        r = dz * 2 + bx
        return pltpu.make_async_remote_copy(
            src_ref=src if whole else src.at[r], dst_ref=dst.at[r], send_sem=snds.at[0],
            recv_sem=rcvs.at[r], device_id=dev(dz, bx), device_id_type=MESH)

    def send_rows(rp, rpi, dz, bxs=(0, 1)):
        for bx in bxs:
            copy = to_line(rp, rpi, rs_snd, rs_rcv, dz, bx)
            if bx == 0:
                pl.when(dz > 0)(copy.start)
            else:
                copy.start()

    def build(dz, dist, bxs, targets, first, done):
        for bx in bxs:
            r = dz * 2 + bx
            acc = jnp.zeros((8, N), F32)
            for t in targets:
                for u in range(CAP):
                    b, q = tabs_sm[dist, u, lane_of(r, t)], tabs_sm[dist, CAP + u, lane_of(r, t)]
                    s, w = r * sb + jnp.maximum(b, 0), jnp.maximum(q, 0)
                    sums = tile(t_hi[t, w], t_lo[t, w], s_hi[s], s_lo[s], k_row.at[r], k_col.at[r], t * CAP + u)
                    acc = acc + jnp.where(sub8 == b, sums, 0.0)
            rp0[r] = acc if first else rp0[r] + acc
        if done:
            send_rows(rp0, rpi0, dz, bxs)

    def builds(first_place, places, targets, first, done):
        def one(i, _):
            dz, dist = place(first_place + i)
            build(dz, dist, (0, 1), targets, first, done)
            return 0

        lax.fori_loop(0, places, one, 0)

    def last_build(bx):
        def one(i, _):
            build(hops + i, hops, (bx,), range(TARGETS), True, True)
            return 0

        lax.fori_loop(0, 1, one, 0)

    lane8 = lax.broadcasted_iota(I32, (8, N), 1)

    def compact(dist):
        part = jnp.zeros((8, N), I32)
        for dz in (0,) if dist == 0 else (hops,) if dist == hops else (-dist, dist):
            for bx in range(2):
                r = rel(dz, bx)
                moved = pltpu.roll(tabs[r], lax.rem(r * 4 + N - z * line - (x // 2) * 4, N), 1)
                part = jnp.where(lane8 // 4 == r, moved, part)
        tabc[dist] = part

    def table_copy(dist):
        return pltpu.make_async_copy(tabc.at[dist], tabs_sm.at[dist], loc.at[2])

    def far_tiles(f0, acc):
        for ff in range(4):
            f = f0 * 4 + ff
            w = tabf_sm[2 * CAP, f]
            sums = tile(t_hi[0, w], t_lo[0, w], f_hi[f], f_lo[f], kf_row, kf_col, f)
            acc = acc + jnp.where(sub8 == f, sums, 0.0)
        return acc

    for h in range(1, hops + 1):
        final = h == hops
        w_plus[h].wait_recv()
        if not final:
            w_plus[h + 1] = send(two(-h), two(-h - 1), up)
            w_minus[h].wait_recv()
            if h + 1 < hops:
                w_minus[h + 1] = send(two(h), two(h + 1), down)
        for p in range(3):
            for k, (dz, got, onward) in enumerate(((-h, z_plus, up), (h, z_minus, down))):
                got[h, p].wait_recv()
                if h + 2 == hops and p == 2:
                    continue
                if h + 1 < hops:
                    got[h + 1, p] = send(piece(dz, p), piece(-h - 1 if k == 0 else h + 1, p), onward)
                elif h + 1 == hops:
                    got[hops, p] = send(piece(dz, p, k * quarter, quarter), piece(hops, p, k * quarter, quarter), onward)
            if h + 1 == hops and p == 0:
                z_plus[h, 2] = send(piece(1 - h, 2), piece(-h, 2), up)
                z_minus[h, 2] = send(piece(h - 1, 2), piece(h, 2), down)
            if p == 0:
                for dz in (-h, h)[: 1 if final else 2]:
                    post[dz] = send(s_raw.at[rel(dz, 0), hi], s_raw.at[rel(dz, 1), hi], mate)
            if p == (0 if final else 1):
                dist = h - 1
                first, places = (0, 1) if dist == 0 else (2 * dist - 1, 2)
                compact(dist)
                norm_lines(2 * first, places)
                table_copy(dist).start()
                norm_lines(2 * first + places, places)
                table_copy(dist).wait()
                if not final:
                    builds(first, places, (0, 2), True, False)
                if h == 2:
                    w_far.wait_recv()
                    far_table = pltpu.make_async_copy(tabf, tabf_sm, loc.at[3])
                    far_table.start()
                    f_far.wait_recv()

                    def far_unit(i, _):
                        for w in range(sb):
                            f_hi[w], f_lo[w] = unit(f_raw[w], True)
                        return 0

                    lax.fori_loop(0, 1, far_unit, 0)
                    far_table.wait()
                    rf0[...] = lax.fori_loop(0, sb // 4, far_tiles, jnp.zeros((8, N), F32))
                    mass_pair.wait_recv()
                    mass_diagonal = send(tmass.at[1], tmass.at[3], partner)
                if h == hops - 1:
                    t_pair.wait_recv()
                    t_diagonal = send(t_raw.at[1], t_raw.at[3], partner)
                    norm_t(1)
                    t_diagonal.wait_recv()
                    norm_t(3)
                    builds(0, first + places, (1, 3), False, True)
                if final:
                    compact(hops)
                    builds(first, places, range(TARGETS), True, True)
                    table_copy(hops).start()
            if final and p == 1:
                table_copy(hops).wait()
                norm_lines(2 * (nz - 1), 1)
                last_build(0)
        for dz in (-h, h)[: 1 if final else 2]:
            post[dz].wait_recv()
    norm_lines(2 * nz - 1, 1)
    last_build(1)

    others = [(dz, bx) for dz in range(nz) for bx in range(2) if (dz, bx) != (0, 0)]
    others.sort(key=lambda o: -min(o[0], nz - o[0]))

    def exchange(src, dst, k, to_dev):
        return pltpu.make_async_remote_copy(
            src_ref=src, dst_ref=dst, send_sem=ex_snd.at[k], recv_sem=ex_rcv.at[k],
            device_id=to_dev, device_id_type=MESH)

    def group(j):
        return (lax.rem(nz - j, nz), j), (j + 1, j + 1)

    def spread(v, r):
        h, l = halves(v)
        return jnp.where(sub16 == r, h, jnp.where(sub16 == r + 8, l, 0.0)).astype(BF16)

    def product(lhs, tiles):
        o = nn(jnp.concatenate([v for v in lhs for _ in range(2)], axis=1), tiles)
        return o[:8] + o[8:]

    def rows_pass(rp, rpi, rf):
        def body(r0, _):
            j = hops - 1 - r0
            for dz, dist in group(j):
                for bx in range(2):
                    r = dz * 2 + bx
                    lhs = []
                    for t in range(TARGETS):
                        for u in range(CAP):
                            b, q = tabs_sm[dist, u, lane_of(r, t)], tabs_sm[dist, CAP + u, lane_of(r, t)]
                            lhs.append(spread(ts[t, pl.ds(jnp.maximum(q, 0), 1), :], b))
                    rp[r] = product(lhs, k_row[r])
            for dz, _ in group(j):
                send_rows(rp, rpi, dz)
            return 0

        lax.fori_loop(0, hops, body, 0)
        lhs = [spread(ts[0, pl.ds(tabf_sm[2 * CAP, f], 1), :], f) for f in range(sb)]
        rf[...] = product(lhs, kf_row[...])

    def cols_pass(so, ss, sf, far_copy):
        def body(j, accs):
            accs = list(accs)
            for dz, _ in group(j):
                for bx in range(2):
                    copy = from_line(so, ss, ag_snd, ag_rcv, dz, bx, True)
                    if bx == 0:
                        pl.when(dz > 0)(copy.wait_recv)
                    else:
                        copy.wait_recv()
            for dz, _ in group(j):
                for bx in range(2):
                    ssl[dz * 2 + bx] = ss[dz * 2 + bx]
            slots = [(t, u) for t in range(TARGETS) for u in range(CAP)]
            for dz, dist in group(j):
                for bx in range(2):
                    r = dz * 2 + bx
                    lhs = []
                    for k, (t, u) in enumerate(slots):
                        b = tabs_sm[dist, u, lane_of(r, t)]
                        lhs.append(spread(ssl[r, pl.ds(jnp.maximum(b, 0), 1), :], k))
                    o = product(lhs, k_col[r])
                    for k, (t, u) in enumerate(slots):
                        q = tabs_sm[dist, CAP + u, lane_of(r, t)]
                        accs[t] = accs[t] + jnp.where(sub32 == q, o[k : k + 1], 0.0)
            return tuple(accs)

        zero = jnp.zeros((tb_dev, N), F32)
        accs = list(lax.fori_loop(0, hops, body, (zero,) * TARGETS))
        far_copy.wait_recv()
        lhs = [spread(sf[f : f + 1, :], f) for f in range(sb)]
        o = product(lhs, kf_col[...])
        for f in range(sb):
            accs[0] = accs[0] + jnp.where(sub32 == tabf_sm[2 * CAP, f], o[f : f + 1], 0.0)
        return accs

    mass_core.wait_recv()
    mass_diagonal.wait_recv()
    for it, (rp, rpi, rf, rfi, so, ss, sf, co, ci, wo, wi) in enumerate((
        (rp0, rpi0, rf0, rfi0, so0, ss0, sf0, co0, ci0, wo0, wi0),
        (rp1, rpi1, rf1, rfi1, so1, ss1, sf1, co1, ci1, wo1, wi1),
    )):
        last = it == ITERS - 1
        far_rows = exchange(rf, rfi, 0, behind)
        far_scale = exchange(so, sf, 1, ahead)
        if it > 0:
            rows_pass(rp, rpi, rf)
        far_rows.start()
        total = rp[0]
        for o in others[::-1]:
            from_line(rp, rpi, rs_snd, rs_rcv, *o).wait_recv()
        far_rows.wait_recv()
        total = total + rfi[...]
        for o in others:
            total = total + rpi[rel(*o)]
        scale = smass[...] / (DUSTBIN + total)
        so[...] = scale
        ss[0] = scale
        if last:
            out[:sb] = scale
        for o in others:
            to_line(so, ss, ag_snd, ag_rcv, *o, True).start()
        far_scale.start()
        accs = cols_pass(so, ss, sf, far_scale)
        theirs = pl.ds(2, 2) if last else pl.ds(0, TARGETS)
        for t in range(2 if last else 0, TARGETS):
            co[t] = accs[t]
        cores = exchange(co.at[theirs], ci.at[theirs], 2 + 2 * it, partner)
        cores.start()
        for left, sem in ((rp, rs_snd), (ss, ag_snd)):
            pltpu.make_async_copy(left.at[pl.ds(1, nr - 1)], left.at[pl.ds(1, nr - 1)], sem.at[0]).wait()
        far_rows.wait_send()
        far_scale.wait_send()
        cores.wait_recv()
        sums = [accs[t] + ci[t ^ 2] for t in range(2 if last else TARGETS)]
        moving = pl.ds(1, 1) if last else pl.ds(0, TARGETS)
        for t in (1,) if last else range(TARGETS):
            wo[t] = sums[t]
        swap = exchange(wo.at[moving], wi.at[moving], 3 + 2 * it, pair)
        swap.start()
        swap.wait_recv()
        if last:
            out[sb:] = tmass[0] / (DUSTBIN + (sums[0] + wi[1]))
        else:
            for t in range(TARGETS):
                ts[t] = tmass[t] / (DUSTBIN + (sums[t] + wi[t ^ 1]))
        cores.wait_send()
        swap.wait_send()
    for copy in sent:
        copy.wait_send()
    assert count[0] == COPIES


def local(ng, nz, semb, temb, smass, tmass, cdev, cblk):
    sb, tb = semb.shape[0], temb.shape[0]
    nr = 2 * nz
    slots = TARGETS * CAP * 2 * N
    vm = pltpu.VMEM
    dma = pltpu.SemaphoreType.DMA
    tile = (N, N)
    blocks = vm((nr, sb, N), F32)
    source, targets = vm((sb, N), F32), vm((TARGETS, tb, N), F32)
    scratch = [
        vm((nr, sb) + tile, F32), vm((TARGETS, tb) + tile, F32), vm((sb,) + tile, F32),
        vm((nr * sb,) + tile, BF16), vm((nr * sb,) + tile, BF16),
        vm((TARGETS, tb) + tile, BF16), vm((TARGETS, tb) + tile, BF16),
        vm((sb,) + tile, BF16), vm((sb,) + tile, BF16),
        vm((nr, slots, N), BF16), vm((nr, slots, N), BF16),
        vm((sb * 2 * N, N), BF16), vm((sb * 2 * N, N), BF16),
        vm((8, N), I32), vm((nr, 8, N), I32), vm((8, N), I32), vm((nz // 2 + 1, 8, N), I32),
        pltpu.SMEM((nz // 2 + 1, 8, N), I32), pltpu.SMEM((8, N), I32),
    ]
    scratch += [blocks] * 7 + [source] * 8 + [targets] * 9
    scratch += [vm(a.shape, a.dtype) for a in (smass, cdev, cblk)] + [targets]
    scratch += [dma((COPIES,))] * 2 + [dma((1,)), dma((nr,)), dma((1,)), dma((nr,))] + [dma((6,))] * 2 + [dma((8,))]
    any_, vmem = pl.BlockSpec(memory_space=pl.ANY), pl.BlockSpec(memory_space=pltpu.VMEM)
    both = pl.pallas_call(
        functools.partial(kernel, ng, nz, sb, tb),
        out_shape=jax.ShapeDtypeStruct((sb + tb, N), F32),
        in_specs=[any_] * 6,
        out_specs=vmem,
        scratch_shapes=scratch,
        compiler_params=pltpu.CompilerParams(
            collective_id=0, has_side_effects=True, vmem_limit_bytes=VMEM_BYTES),
        name="sinkhorn",
    )(semb, temb, smass, tmass, cdev, cblk)

    def split(both_ref, src_ref, tgt_ref):
        src_ref[...] = both_ref[:sb]
        tgt_ref[...] = both_ref[sb:]

    return pl.pallas_call(
        split,
        out_shape=(jax.ShapeDtypeStruct(smass.shape, F32), jax.ShapeDtypeStruct(tmass.shape, F32)),
        in_specs=[vmem],
        out_specs=(vmem, vmem),
        name="split",
    )(both)


def solution(mesh):
    placed = (
        P(("group", "dev"), None, None),
        P(("group", "dev"), None, None),
        P(("group", "dev"), None),
        P(("group", "dev"), None),
        P(("group", "dev"), None),
        P(("group", "dev"), None),
    )
    ng, nz = mesh.shape["group"], mesh.shape["dev"] // (2 * NX)
    return jax.shard_map(
        functools.partial(local, ng, nz),
        mesh=mesh,
        in_specs=placed,
        out_specs=(P(("group", "dev"), None), P(("group", "dev"), None)),
        check_vma=False,
    )
```

```python
import functools

import jax
import jax.numpy as jnp
from jax import lax
from jax.experimental import pallas as pl
from jax.experimental.pallas import tpu as pltpu
from jax.sharding import PartitionSpec as P

MESH = pl.DeviceIdType.MESH
N = 128
NX = 4
NEAR = 7
CAP = 2
TARGETS = 4
VMEM_BYTES = 62 * 1024 * 1024
ITERS = 2
EMPTY = -64
COPIES = 49
DUSTBIN = 0.5
EPSILON = 1e-6
GAIN = 1.0 / (N * 0.1)
SHARE = 1.0 / (8.0 * N)

F32, BF16, I32 = jnp.float32, jnp.bfloat16, jnp.int32


def nn(a, b):
    return lax.dot_general(a, b, (((1,), (0,)), ((), ())), preferred_element_type=F32)


def halves(v):
    hi = v.astype(BF16).astype(F32)
    return hi, v - hi


def kernel(ng, nz, sb, tb_dev, *refs):
    (semb, temb, smass_in, tmass_in, cdev_in, cblk_in, out,
     s_raw, t_raw, f_raw, s_hi, s_lo, t_hi, t_lo, f_hi, f_lo, k_row, k_col, kf_row, kf_col,
     tab, tabs, tabf, tabc, tabs_sm, tabf_sm,
     rp0, rp1, rpi0, rpi1, ss0, ss1, ssl, rf0, rf1, rfi0, rfi1, so0, so1, sf0, sf1,
     co0, co1, ci0, ci1, wo0, wo1, wi0, wi1, ts, smass, cdev, cblk, tmass,
     snd, rcv, rs_snd, rs_rcv, ag_snd, ag_rcv, ex_snd, ex_rcv, loc) = refs
    nr = 2 * nz
    hops = nz // 2
    half = sb // 2
    quarter = sb // 4
    line = 2 * NX
    g, d = lax.axis_index("group"), lax.axis_index("dev")
    z, x, c = d // line, (d // 2) % NX, d % 2

    def at(zz, xx, cc):
        return (g, zz * line + xx * 2 + cc)

    def dev(dz, bx):
        return at(lax.rem(z + dz, nz), NX - 1 - x if bx else x, c)

    def rel(dz, bx):
        return (dz % nz) * 2 + bx

    up, down, mate = dev(1, 0), dev(nz - 1, 0), dev(0, 1)
    partner = at(z, x, 1 - c)
    pair = at(z, x + 1 - 2 * lax.rem(x, 2), c)
    ahead, behind = (lax.rem(g + 1, ng), d), (lax.rem(g + ng - 1, ng), d)

    count = [0]
    sent = []

    def send(src, dst, to_dev):
        k = count[0]
        count[0] += 1
        copy = pltpu.make_async_remote_copy(
            src_ref=src, dst_ref=dst, send_sem=snd.at[k], recv_sem=rcv.at[k],
            device_id=to_dev, device_id_type=MESH)
        copy.start()
        sent.append(copy)
        return copy

    barrier = pltpu.get_barrier_semaphore()
    greeted = (up, down, mate, pair, partner, ahead, behind)
    for other in greeted:
        pl.semaphore_signal(barrier, inc=1, device_id=other, device_id_type=MESH)
    own_s = pltpu.make_async_copy(semb, s_raw.at[0], loc.at[0])
    own_t = pltpu.make_async_copy(temb, t_raw.at[0], loc.at[1])
    small = [pltpu.make_async_copy(a, b, loc.at[4 + i]) for i, (a, b) in enumerate(
        ((cdev_in, cdev), (cblk_in, cblk), (smass_in, smass), (tmass_in, tmass.at[0])))]
    for copy in small:
        copy.start()
    own_s.start()
    own_t.start()
    for copy in small:
        copy.wait()

    lane = lax.broadcasted_iota(I32, (1, N), 1)
    run = jnp.zeros((1, N), I32)
    rows = [jnp.full((1, N), EMPTY, I32) for _ in range(2 * CAP)]
    far = jnp.zeros((1, N), I32)
    for b in range(sb):
        hit = jnp.zeros((1, N), I32)
        which = jnp.zeros((1, N), I32)
        for k in range(NEAR):
            m = cdev[b : b + 1, k : k + 1] == lane
            hit = jnp.where(m, 1, hit)
            which = jnp.where(m, cblk[b : b + 1, k : k + 1], which)
        for u in range(CAP):
            m = (hit == 1) & (run == u)
            rows[u] = jnp.where(m, b, rows[u])
            rows[CAP + u] = jnp.where(m, which, rows[CAP + u])
        run = run + hit
        far = jnp.where(lane == b, cblk[b : b + 1, NEAR : NEAR + 1], far)
    table = jnp.concatenate(rows + [far] + [jnp.zeros((1, N), I32)] * (7 - 2 * CAP), axis=0)
    tab[...] = table
    tabs[0] = table

    pl.semaphore_wait(barrier, len(greeted))

    lo, hi = pl.ds(0, half), pl.ds(half, half)
    pieces = ((0, half), (0, 0), (1, 0))
    z_plus, z_minus = {}, {}

    def piece(dz, p, start=0, size=half):
        bx, first = pieces[p]
        return s_raw.at[rel(dz, bx), pl.ds(first + start, size)]

    w_mate = send(tab, tabs.at[1], mate)
    pre = send(semb.at[lo], s_raw.at[rel(0, 1), lo], mate)
    for p in (0, 1):
        part = semb.at[pl.ds(pieces[p][1], half)]
        z_plus[1, p] = send(part, piece(-1, p), up)
        z_minus[1, p] = send(part, piece(1, p), down)
    post = {0: send(semb.at[hi], s_raw.at[rel(0, 1), hi], mate)}
    t_pair = send(temb, t_raw.at[1], pair)
    mass_pair = send(tmass_in, tmass.at[1], pair)
    t_core = send(temb, t_raw.at[2], partner)
    mass_core = send(tmass_in, tmass.at[2], partner)
    w_far = send(tab, tabf, ahead)
    f_far = send(semb, f_raw, ahead)
    w_plus, w_minus = {}, {}

    def two(dz):
        return tabs.at[pl.ds(rel(dz, 0), 2)]

    def place(p):
        dist = (p + 1) // 2
        return jnp.where(p % 2 == 1, dist, lax.rem(nz - dist, nz)), dist

    def unit(v, turned):
        if turned:
            v = v.T
        v = v * lax.rsqrt(jnp.mean(v * v, axis=0 if turned else 1, keepdims=True) + EPSILON)
        h = v.astype(BF16)
        return h, (v - h.astype(F32)).astype(BF16)

    def norm_lines(first_line, lines):
        def one(i, _):
            dz, _dist = place((first_line + i) // 2)
            r = dz * 2 + (first_line + i) % 2
            for w in range(sb):
                s_hi[r * sb + w], s_lo[r * sb + w] = unit(s_raw[r, w], True)
            return 0

        lax.fori_loop(0, lines, one, 0)

    def norm_t(t):
        def one(i, _):
            for w in range(8):
                t_hi[t, i * 8 + w], t_lo[t, i * 8 + w] = unit(t_raw[t, i * 8 + w], False)
            return 0

        lax.fori_loop(0, tb_dev // 8, one, 0)

    w_mate.wait_recv()
    w_plus[1] = send(two(0), two(-1), up)
    w_minus[1] = send(two(0), two(1), down)
    pre.wait_recv()
    z_plus[1, 2] = send(piece(0, 2), piece(-1, 2), up)
    z_minus[1, 2] = send(piece(0, 2), piece(1, 2), down)
    own_t.wait()
    norm_t(0)
    t_core.wait_recv()
    norm_t(2)
    own_s.wait()
    post[0].wait_recv()

    sub8 = lax.broadcasted_iota(I32, (8, N), 0)
    sub16 = lax.broadcasted_iota(I32, (16, N), 0)
    sub32 = lax.broadcasted_iota(I32, (tb_dev, N), 0)

    def lane_of(r, t):
        return r * 4 + lax.rem(x + t, 2) * 2 + (c if t < 2 else 1 - c)

    def two_terms(v, ref, k):
        h = v.astype(BF16)
        ref[pl.ds(k * 2 * N, N), :] = h
        ref[pl.ds(k * 2 * N + N, N), :] = (v - h.astype(F32)).astype(BF16)

    def tile(b_hi, b_lo, a_hi, a_lo, row, col, k):
        dots = nn(b_hi, a_hi) + (nn(b_lo, a_hi) + nn(b_hi, a_lo))
        e = jnp.exp(dots * GAIN) * SHARE
        two_terms(e, row, k)
        two_terms(e.T, col, k)
        return jnp.sum(e, axis=0, keepdims=True)

    def to_line(src, dst, snds, rcvs, dz, bx, whole=False):
        r, back = dz * 2 + bx, lax.rem(nz - dz, nz) * 2 + bx
        return pltpu.make_async_remote_copy(
            src_ref=src if whole else src.at[r], dst_ref=dst.at[back], send_sem=snds.at[0],
            recv_sem=rcvs.at[back], device_id=dev(dz, bx), device_id_type=MESH)

    def from_line(src, dst, snds, rcvs, dz, bx, whole=False):
        r = dz * 2 + bx
        return pltpu.make_async_remote_copy(
            src_ref=src if whole else src.at[r], dst_ref=dst.at[r], send_sem=snds.at[0],
            recv_sem=rcvs.at[r], device_id=dev(dz, bx), device_id_type=MESH)

    def send_rows(rp, rpi, dz, bxs=(0, 1)):
        for bx in bxs:
            copy = to_line(rp, rpi, rs_snd, rs_rcv, dz, bx)
            if bx == 0:
                pl.when(dz > 0)(copy.start)
            else:
                copy.start()

    def build(dz, dist, bxs, targets, first, done):
        for bx in bxs:
            r = dz * 2 + bx
            acc = jnp.zeros((8, N), F32)
            for t in targets:
                for u in range(CAP):
                    b, q = tabs_sm[dist, u, lane_of(r, t)], tabs_sm[dist, CAP + u, lane_of(r, t)]
                    s, w = r * sb + jnp.maximum(b, 0), jnp.maximum(q, 0)
                    sums = tile(t_hi[t, w], t_lo[t, w], s_hi[s], s_lo[s], k_row.at[r], k_col.at[r], t * CAP + u)
                    acc = acc + jnp.where(sub8 == b, sums, 0.0)
            rp0[r] = acc if first else rp0[r] + acc
        if done:
            send_rows(rp0, rpi0, dz, bxs)

    def builds(first_place, places, targets, first, done):
        def one(i, _):
            dz, dist = place(first_place + i)
            build(dz, dist, (0, 1), targets, first, done)
            return 0

        lax.fori_loop(0, places, one, 0)

    def last_build(bx):
        def one(i, _):
            build(hops + i, hops, (bx,), range(TARGETS), True, True)
            return 0

        lax.fori_loop(0, 1, one, 0)

    lane8 = lax.broadcasted_iota(I32, (8, N), 1)

    def compact(dist):
        part = jnp.zeros((8, N), I32)
        for dz in (0,) if dist == 0 else (hops,) if dist == hops else (-dist, dist):
            for bx in range(2):
                r = rel(dz, bx)
                moved = pltpu.roll(tabs[r], lax.rem(r * 4 + N - z * line - (x // 2) * 4, N), 1)
                part = jnp.where(lane8 // 4 == r, moved, part)
        tabc[dist] = part

    def table_copy(dist):
        return pltpu.make_async_copy(tabc.at[dist], tabs_sm.at[dist], loc.at[2])

    def far_tiles(f0, acc):
        for ff in range(4):
            f = f0 * 4 + ff
            w = tabf_sm[2 * CAP, f]
            sums = tile(t_hi[0, w], t_lo[0, w], f_hi[f], f_lo[f], kf_row, kf_col, f)
            acc = acc + jnp.where(sub8 == f, sums, 0.0)
        return acc

    def take_tables(h):
        w_plus[h].wait_recv()
        if h < hops:
            w_plus[h + 1] = send(two(-h), two(-h - 1), up)
            w_minus[h].wait_recv()
            if h + 1 < hops:
                w_minus[h + 1] = send(two(h), two(h + 1), down)

    def take(h, p):
        for k, (dz, got, onward) in enumerate(((-h, z_plus, up), (h, z_minus, down))):
            got[h, p].wait_recv()
            if h + 2 == hops and p == 2:
                continue
            if h + 1 < hops:
                got[h + 1, p] = send(piece(dz, p), piece(-h - 1 if k == 0 else h + 1, p), onward)
            elif h + 1 == hops:
                got[hops, p] = send(piece(dz, p, k * quarter, quarter), piece(hops, p, k * quarter, quarter), onward)
        if h + 1 == hops and p == 0:
            z_plus[h, 2] = send(piece(1 - h, 2), piece(-h, 2), up)
            z_minus[h, 2] = send(piece(h - 1, 2), piece(h, 2), down)
        if p == 0:
            for dz in (-h, h)[: 1 if h == hops else 2]:
                post[dz] = send(s_raw.at[rel(dz, 0), hi], s_raw.at[rel(dz, 1), hi], mate)

    def take_post(h):
        for dz in (-h, h)[: 1 if h == hops else 2]:
            post[dz].wait_recv()

    def lines_of(dist):
        return (0, 1) if dist == 0 else (2 * dist - 1, 2)

    def bring(dist):
        first, places = lines_of(dist)
        compact(dist)
        norm_lines(2 * first, places)
        table_copy(dist).start()
        norm_lines(2 * first + places, places)
        table_copy(dist).wait()

    for h in range(1, hops):
        take_tables(h)
        take(h, 0)
        take(h, 1)
        bring(h - 1)
        builds(*lines_of(h - 1), (0, 2), True, False)
        if h == 2:
            w_far.wait_recv()
            far_table = pltpu.make_async_copy(tabf, tabf_sm, loc.at[3])
            far_table.start()
            f_far.wait_recv()

            def far_unit(i, _):
                for w in range(sb):
                    f_hi[w], f_lo[w] = unit(f_raw[w], True)
                return 0

            lax.fori_loop(0, 1, far_unit, 0)
            far_table.wait()
            rf0[...] = lax.fori_loop(0, sb // 4, far_tiles, jnp.zeros((8, N), F32))
            mass_pair.wait_recv()
            mass_diagonal = send(tmass.at[1], tmass.at[3], partner)
        if h < hops - 1:
            take(h, 2)
            take_post(h)
    t_pair.wait_recv()
    t_diagonal = send(t_raw.at[1], t_raw.at[3], partner)
    norm_t(1)
    take_tables(hops)
    take(hops, 0)
    t_diagonal.wait_recv()
    norm_t(3)
    builds(0, 2 * hops - 3, (1, 3), False, True)
    take(hops - 1, 2)
    take_post(hops - 1)
    bring(hops - 1)
    compact(hops)
    builds(*lines_of(hops - 1), range(TARGETS), True, True)
    table_copy(hops).start()
    take(hops, 1)
    table_copy(hops).wait()
    norm_lines(2 * (nz - 1), 1)
    last_build(0)
    take(hops, 2)
    take_post(hops)
    norm_lines(2 * nz - 1, 1)
    last_build(1)

    others = [(dz, bx) for dz in range(nz) for bx in range(2) if (dz, bx) != (0, 0)]
    others.sort(key=lambda o: -min(o[0], nz - o[0]))

    def exchange(src, dst, k, to_dev):
        return pltpu.make_async_remote_copy(
            src_ref=src, dst_ref=dst, send_sem=ex_snd.at[k], recv_sem=ex_rcv.at[k],
            device_id=to_dev, device_id_type=MESH)

    def group(j):
        return (lax.rem(nz - j, nz), j), (j + 1, j + 1)

    def spread(v, r):
        h, l = halves(v)
        return jnp.where(sub16 == r, h, jnp.where(sub16 == r + 8, l, 0.0)).astype(BF16)

    def product(lhs, tiles):
        o = nn(jnp.concatenate([v for v in lhs for _ in range(2)], axis=1), tiles)
        return o[:8] + o[8:]

    def rows_pass(rp, rpi, rf):
        def body(r0, _):
            j = hops - 1 - r0
            for dz, dist in group(j):
                for bx in range(2):
                    r = dz * 2 + bx
                    lhs = []
                    for t in range(TARGETS):
                        for u in range(CAP):
                            b, q = tabs_sm[dist, u, lane_of(r, t)], tabs_sm[dist, CAP + u, lane_of(r, t)]
                            lhs.append(spread(ts[t, pl.ds(jnp.maximum(q, 0), 1), :], b))
                    rp[r] = product(lhs, k_row[r])
            for dz, _ in group(j):
                send_rows(rp, rpi, dz)
            return 0

        lax.fori_loop(0, hops, body, 0)
        lhs = [spread(ts[0, pl.ds(tabf_sm[2 * CAP, f], 1), :], f) for f in range(sb)]
        rf[...] = product(lhs, kf_row[...])

    def cols_pass(so, ss, sf, far_copy):
        def body(j, accs):
            accs = list(accs)
            for dz, _ in group(j):
                for bx in range(2):
                    copy = from_line(so, ss, ag_snd, ag_rcv, dz, bx, True)
                    if bx == 0:
                        pl.when(dz > 0)(copy.wait_recv)
                    else:
                        copy.wait_recv()
            for dz, _ in group(j):
                for bx in range(2):
                    ssl[dz * 2 + bx] = ss[dz * 2 + bx]
            slots = [(t, u) for t in range(TARGETS) for u in range(CAP)]
            for dz, dist in group(j):
                for bx in range(2):
                    r = dz * 2 + bx
                    lhs = []
                    for k, (t, u) in enumerate(slots):
                        b = tabs_sm[dist, u, lane_of(r, t)]
                        lhs.append(spread(ssl[r, pl.ds(jnp.maximum(b, 0), 1), :], k))
                    o = product(lhs, k_col[r])
                    for k, (t, u) in enumerate(slots):
                        q = tabs_sm[dist, CAP + u, lane_of(r, t)]
                        accs[t] = accs[t] + jnp.where(sub32 == q, o[k : k + 1], 0.0)
            return tuple(accs)

        zero = jnp.zeros((tb_dev, N), F32)
        accs = list(lax.fori_loop(0, hops, body, (zero,) * TARGETS))
        far_copy.wait_recv()
        lhs = [spread(sf[f : f + 1, :], f) for f in range(sb)]
        o = product(lhs, kf_col[...])
        for f in range(sb):
            accs[0] = accs[0] + jnp.where(sub32 == tabf_sm[2 * CAP, f], o[f : f + 1], 0.0)
        return accs

    mass_core.wait_recv()
    mass_diagonal.wait_recv()
    for it, (rp, rpi, rf, rfi, so, ss, sf, co, ci, wo, wi) in enumerate((
        (rp0, rpi0, rf0, rfi0, so0, ss0, sf0, co0, ci0, wo0, wi0),
        (rp1, rpi1, rf1, rfi1, so1, ss1, sf1, co1, ci1, wo1, wi1),
    )):
        last = it == ITERS - 1
        far_rows = exchange(rf, rfi, 0, behind)
        far_scale = exchange(so, sf, 1, ahead)
        if it > 0:
            rows_pass(rp, rpi, rf)
        far_rows.start()
        total = rp[0]
        for o in others[::-1]:
            from_line(rp, rpi, rs_snd, rs_rcv, *o).wait_recv()
        far_rows.wait_recv()
        total = total + rfi[...]
        for o in others:
            total = total + rpi[rel(*o)]
        scale = smass[...] / (DUSTBIN + total)
        so[...] = scale
        ss[0] = scale
        if last:
            out[:sb] = scale
        for o in others:
            to_line(so, ss, ag_snd, ag_rcv, *o, True).start()
        far_scale.start()
        accs = cols_pass(so, ss, sf, far_scale)
        theirs = pl.ds(2, 2) if last else pl.ds(0, TARGETS)
        for t in range(2 if last else 0, TARGETS):
            co[t] = accs[t]
        cores = exchange(co.at[theirs], ci.at[theirs], 2 + 2 * it, partner)
        cores.start()
        for left, sem in ((rp, rs_snd), (ss, ag_snd)):
            pltpu.make_async_copy(left.at[pl.ds(1, nr - 1)], left.at[pl.ds(1, nr - 1)], sem.at[0]).wait()
        far_rows.wait_send()
        far_scale.wait_send()
        cores.wait_recv()
        sums = [accs[t] + ci[t ^ 2] for t in range(2 if last else TARGETS)]
        moving = pl.ds(1, 1) if last else pl.ds(0, TARGETS)
        for t in (1,) if last else range(TARGETS):
            wo[t] = sums[t]
        swap = exchange(wo.at[moving], wi.at[moving], 3 + 2 * it, pair)
        swap.start()
        swap.wait_recv()
        if last:
            out[sb:] = tmass[0] / (DUSTBIN + (sums[0] + wi[1]))
        else:
            for t in range(TARGETS):
                ts[t] = tmass[t] / (DUSTBIN + (sums[t] + wi[t ^ 1]))
        cores.wait_send()
        swap.wait_send()
    for copy in sent:
        copy.wait_send()
    assert count[0] == COPIES


def local(ng, nz, semb, temb, smass, tmass, cdev, cblk):
    sb, tb = semb.shape[0], temb.shape[0]
    nr = 2 * nz
    slots = TARGETS * CAP * 2 * N
    vm = pltpu.VMEM
    dma = pltpu.SemaphoreType.DMA
    tile = (N, N)
    blocks = vm((nr, sb, N), F32)
    source, targets = vm((sb, N), F32), vm((TARGETS, tb, N), F32)
    scratch = [
        vm((nr, sb) + tile, F32), vm((TARGETS, tb) + tile, F32), vm((sb,) + tile, F32),
        vm((nr * sb,) + tile, BF16), vm((nr * sb,) + tile, BF16),
        vm((TARGETS, tb) + tile, BF16), vm((TARGETS, tb) + tile, BF16),
        vm((sb,) + tile, BF16), vm((sb,) + tile, BF16),
        vm((nr, slots, N), BF16), vm((nr, slots, N), BF16),
        vm((sb * 2 * N, N), BF16), vm((sb * 2 * N, N), BF16),
        vm((8, N), I32), vm((nr, 8, N), I32), vm((8, N), I32), vm((nz // 2 + 1, 8, N), I32),
        pltpu.SMEM((nz // 2 + 1, 8, N), I32), pltpu.SMEM((8, N), I32),
    ]
    scratch += [blocks] * 7 + [source] * 8 + [targets] * 9
    scratch += [vm(a.shape, a.dtype) for a in (smass, cdev, cblk)] + [targets]
    scratch += [dma((COPIES,))] * 2 + [dma((1,)), dma((nr,)), dma((1,)), dma((nr,))] + [dma((6,))] * 2 + [dma((8,))]
    any_, vmem = pl.BlockSpec(memory_space=pl.ANY), pl.BlockSpec(memory_space=pltpu.VMEM)
    both = pl.pallas_call(
        functools.partial(kernel, ng, nz, sb, tb),
        out_shape=jax.ShapeDtypeStruct((sb + tb, N), F32),
        in_specs=[any_] * 6,
        out_specs=vmem,
        scratch_shapes=scratch,
        compiler_params=pltpu.CompilerParams(
            collective_id=0, has_side_effects=True, vmem_limit_bytes=VMEM_BYTES),
        name="sinkhorn",
    )(semb, temb, smass, tmass, cdev, cblk)

    def split(both_ref, src_ref, tgt_ref):
        src_ref[...] = both_ref[:sb]
        tgt_ref[...] = both_ref[sb:]

    return pl.pallas_call(
        split,
        out_shape=(jax.ShapeDtypeStruct(smass.shape, F32), jax.ShapeDtypeStruct(tmass.shape, F32)),
        in_specs=[vmem],
        out_specs=(vmem, vmem),
        name="split",
    )(both)


def solution(mesh):
    placed = (
        P(("group", "dev"), None, None),
        P(("group", "dev"), None, None),
        P(("group", "dev"), None),
        P(("group", "dev"), None),
        P(("group", "dev"), None),
        P(("group", "dev"), None),
    )
    ng, nz = mesh.shape["group"], mesh.shape["dev"] // (2 * NX)
    return jax.shard_map(
        functools.partial(local, ng, nz),
        mesh=mesh,
        in_specs=placed,
        out_specs=(P(("group", "dev"), None), P(("group", "dev"), None)),
        check_vma=False,
    )
```

```python
import functools

import jax
import jax.numpy as jnp
from jax import lax
from jax.experimental import pallas as pl
from jax.experimental.pallas import tpu as pltpu
from jax.sharding import PartitionSpec as P

MESH = pl.DeviceIdType.MESH
N = 128
NX = 4
NEAR = 7
CAP = 2
TARGETS = 4
VMEM_BYTES = 62 * 1024 * 1024
ITERS = 2
EMPTY = -64
COPIES = 49
DUSTBIN = 0.5
EPSILON = 1e-6
GAIN = 1.0 / (N * 0.1)
SHARE = 1.0 / (8.0 * N)

F32, BF16, I32 = jnp.float32, jnp.bfloat16, jnp.int32


def nn(a, b):
    return lax.dot_general(a, b, (((1,), (0,)), ((), ())), preferred_element_type=F32)


def halves(v):
    hi = v.astype(BF16).astype(F32)
    return hi, v - hi


def kernel(ng, nz, sb, tb_dev, *refs):
    (semb, temb, smass_in, tmass_in, cdev_in, cblk_in, out,
     s_raw, t_raw, f_raw, s_hi, s_lo, t_hi, t_lo, f_hi, f_lo, k_row, k_col, kf_row, kf_col,
     tab, tabs, tabf, tabc, tabs_sm, tabf_sm,
     rp0, rp1, rpi0, rpi1, ss0, ss1, ssl, rf0, rf1, rfi0, rfi1, so0, so1, sf0, sf1,
     co0, co1, ci0, ci1, wo0, wo1, wi0, wi1, ts, smass, cdev, cblk, tmass,
     snd, rcv, rs_snd, rs_rcv, ag_snd, ag_rcv, ex_snd, ex_rcv, loc) = refs
    nr = 2 * nz
    hops = nz // 2
    half = sb // 2
    quarter = sb // 4
    line = 2 * NX
    g, d = lax.axis_index("group"), lax.axis_index("dev")
    z, x, c = d // line, (d // 2) % NX, d % 2

    def at(zz, xx, cc):
        return (g, zz * line + xx * 2 + cc)

    def dev(dz, bx):
        return at(lax.rem(z + dz, nz), NX - 1 - x if bx else x, c)

    def rel(dz, bx):
        return (dz % nz) * 2 + bx

    up, down, mate = dev(1, 0), dev(nz - 1, 0), dev(0, 1)
    partner = at(z, x, 1 - c)
    pair = at(z, x + 1 - 2 * lax.rem(x, 2), c)
    ahead, behind = (lax.rem(g + 1, ng), d), (lax.rem(g + ng - 1, ng), d)

    count = [0]

    def kind(src):
        if src.dtype == I32:
            return 2
        if len(src.shape) == 2:
            return 3
        return 1 if src.shape[0] == tb_dev else 0

    def send(src, dst, to_dev):
        k = count[0]
        count[0] += 1
        copy = pltpu.make_async_remote_copy(
            src_ref=src, dst_ref=dst, send_sem=snd.at[kind(src)], recv_sem=rcv.at[k],
            device_id=to_dev, device_id_type=MESH)
        copy.start()
        return copy

    barrier = pltpu.get_barrier_semaphore()
    greeted = (up, down, mate, pair, partner, ahead, behind)
    for other in greeted:
        pl.semaphore_signal(barrier, inc=1, device_id=other, device_id_type=MESH)
    own_s = pltpu.make_async_copy(semb, s_raw.at[0], loc.at[0])
    own_t = pltpu.make_async_copy(temb, t_raw.at[0], loc.at[1])
    small = [pltpu.make_async_copy(a, b, loc.at[4 + i]) for i, (a, b) in enumerate(
        ((cdev_in, cdev), (cblk_in, cblk), (smass_in, smass), (tmass_in, tmass.at[0])))]
    for copy in small:
        copy.start()
    own_s.start()
    own_t.start()
    for copy in small:
        copy.wait()

    lane = lax.broadcasted_iota(I32, (1, N), 1)
    run = jnp.zeros((1, N), I32)
    rows = [jnp.full((1, N), EMPTY, I32) for _ in range(2 * CAP)]
    far = jnp.zeros((1, N), I32)
    for b in range(sb):
        hit = jnp.zeros((1, N), I32)
        which = jnp.zeros((1, N), I32)
        for k in range(NEAR):
            m = cdev[b : b + 1, k : k + 1] == lane
            hit = jnp.where(m, 1, hit)
            which = jnp.where(m, cblk[b : b + 1, k : k + 1], which)
        for u in range(CAP):
            m = (hit == 1) & (run == u)
            rows[u] = jnp.where(m, b, rows[u])
            rows[CAP + u] = jnp.where(m, which, rows[CAP + u])
        run = run + hit
        far = jnp.where(lane == b, cblk[b : b + 1, NEAR : NEAR + 1], far)
    table = jnp.concatenate(rows + [far] + [jnp.zeros((1, N), I32)] * (7 - 2 * CAP), axis=0)
    tab[...] = table
    tabs[0] = table

    pl.semaphore_wait(barrier, len(greeted))

    lo, hi = pl.ds(0, half), pl.ds(half, half)
    pieces = ((0, half), (0, 0), (1, 0))
    z_plus, z_minus = {}, {}

    def piece(dz, p, start=0, size=half):
        bx, first = pieces[p]
        return s_raw.at[rel(dz, bx), pl.ds(first + start, size)]

    w_mate = send(tab, tabs.at[1], mate)
    pre = send(semb.at[lo], s_raw.at[rel(0, 1), lo], mate)
    for p in (0, 1):
        part = semb.at[pl.ds(pieces[p][1], half)]
        z_plus[1, p] = send(part, piece(-1, p), up)
        z_minus[1, p] = send(part, piece(1, p), down)
    post = {0: send(semb.at[hi], s_raw.at[rel(0, 1), hi], mate)}
    t_pair = send(temb, t_raw.at[1], pair)
    mass_pair = send(tmass_in, tmass.at[1], pair)
    t_core = send(temb, t_raw.at[2], partner)
    mass_core = send(tmass_in, tmass.at[2], partner)
    w_far = send(tab, tabf, ahead)
    f_far = send(semb, f_raw, ahead)
    w_plus, w_minus = {}, {}

    def two(dz):
        return tabs.at[pl.ds(rel(dz, 0), 2)]

    def place(p):
        dist = (p + 1) // 2
        return jnp.where(p % 2 == 1, dist, lax.rem(nz - dist, nz)), dist

    def unit(v, turned):
        if turned:
            v = v.T
        v = v * lax.rsqrt(jnp.mean(v * v, axis=0 if turned else 1, keepdims=True) + EPSILON)
        h = v.astype(BF16)
        return h, (v - h.astype(F32)).astype(BF16)

    def norm_lines(first_line, lines):
        def one(i, _):
            dz, _dist = place((first_line + i) // 2)
            r = dz * 2 + (first_line + i) % 2
            for w in range(sb):
                s_hi[r * sb + w], s_lo[r * sb + w] = unit(s_raw[r, w], True)
            return 0

        lax.fori_loop(0, lines, one, 0)

    def norm_t(t):
        def one(i, _):
            for w in range(8):
                t_hi[t, i * 8 + w], t_lo[t, i * 8 + w] = unit(t_raw[t, i * 8 + w], False)
            return 0

        lax.fori_loop(0, tb_dev // 8, one, 0)

    w_mate.wait_recv()
    w_plus[1] = send(two(0), two(-1), up)
    w_minus[1] = send(two(0), two(1), down)
    pre.wait_recv()
    z_plus[1, 2] = send(piece(0, 2), piece(-1, 2), up)
    z_minus[1, 2] = send(piece(0, 2), piece(1, 2), down)
    own_t.wait()
    norm_t(0)
    t_core.wait_recv()
    norm_t(2)
    own_s.wait()
    post[0].wait_recv()

    sub8 = lax.broadcasted_iota(I32, (8, N), 0)
    sub16 = lax.broadcasted_iota(I32, (16, N), 0)
    sub32 = lax.broadcasted_iota(I32, (tb_dev, N), 0)

    def lane_of(r, t):
        return r * 4 + lax.rem(x + t, 2) * 2 + (c if t < 2 else 1 - c)

    def two_terms(v, ref, k):
        h = v.astype(BF16)
        ref[pl.ds(k * 2 * N, N), :] = h
        ref[pl.ds(k * 2 * N + N, N), :] = (v - h.astype(F32)).astype(BF16)

    def tile(b_hi, b_lo, a_hi, a_lo, row, col, k):
        dots = nn(b_hi, a_hi) + (nn(b_lo, a_hi) + nn(b_hi, a_lo))
        e = jnp.exp(dots * GAIN) * SHARE
        two_terms(e, row, k)
        two_terms(e.T, col, k)
        return jnp.sum(e, axis=0, keepdims=True)

    def to_line(src, dst, snds, rcvs, dz, bx, whole=False):
        r, back = dz * 2 + bx, lax.rem(nz - dz, nz) * 2 + bx
        return pltpu.make_async_remote_copy(
            src_ref=src if whole else src.at[r], dst_ref=dst.at[back], send_sem=snds.at[0],
            recv_sem=rcvs.at[back], device_id=dev(dz, bx), device_id_type=MESH)

    def from_line(src, dst, snds, rcvs, dz, bx, whole=False):
        r = dz * 2 + bx
        return pltpu.make_async_remote_copy(
            src_ref=src if whole else src.at[r], dst_ref=dst.at[r], send_sem=snds.at[0],
            recv_sem=rcvs.at[r], device_id=dev(dz, bx), device_id_type=MESH)

    def send_rows(rp, rpi, dz, bxs=(0, 1)):
        for bx in bxs:
            copy = to_line(rp, rpi, rs_snd, rs_rcv, dz, bx)
            if bx == 0:
                pl.when(dz > 0)(copy.start)
            else:
                copy.start()

    def build(dz, dist, bxs, targets, first, done):
        for bx in bxs:
            r = dz * 2 + bx
            acc = jnp.zeros((8, N), F32)
            for t in targets:
                for u in range(CAP):
                    b, q = tabs_sm[dist, u, lane_of(r, t)], tabs_sm[dist, CAP + u, lane_of(r, t)]
                    s, w = r * sb + jnp.maximum(b, 0), jnp.maximum(q, 0)
                    sums = tile(t_hi[t, w], t_lo[t, w], s_hi[s], s_lo[s], k_row.at[r], k_col.at[r], t * CAP + u)
                    acc = acc + jnp.where(sub8 == b, sums, 0.0)
            rp0[r] = acc if first else rp0[r] + acc
        if done:
            send_rows(rp0, rpi0, dz, bxs)

    def builds(first_place, places, targets, first, done):
        def one(i, _):
            dz, dist = place(first_place + i)
            build(dz, dist, (0, 1), targets, first, done)
            return 0

        lax.fori_loop(0, places, one, 0)

    def last_build(bx):
        def one(i, _):
            build(hops + i, hops, (bx,), range(TARGETS), True, True)
            return 0

        lax.fori_loop(0, 1, one, 0)

    lane8 = lax.broadcasted_iota(I32, (8, N), 1)

    def compact(dist):
        part = jnp.zeros((8, N), I32)
        for dz in (0,) if dist == 0 else (hops,) if dist == hops else (-dist, dist):
            for bx in range(2):
                r = rel(dz, bx)
                moved = pltpu.roll(tabs[r], lax.rem(r * 4 + N - z * line - (x // 2) * 4, N), 1)
                part = jnp.where(lane8 // 4 == r, moved, part)
        tabc[dist] = part

    def table_copy(dist):
        return pltpu.make_async_copy(tabc.at[dist], tabs_sm.at[dist], loc.at[2])

    def far_tiles(f0, acc):
        for ff in range(4):
            f = f0 * 4 + ff
            w = tabf_sm[2 * CAP, f]
            sums = tile(t_hi[0, w], t_lo[0, w], f_hi[f], f_lo[f], kf_row, kf_col, f)
            acc = acc + jnp.where(sub8 == f, sums, 0.0)
        return acc

    def take_tables(h):
        w_plus[h].wait_recv()
        if h < hops:
            w_plus[h + 1] = send(two(-h), two(-h - 1), up)
            w_minus[h].wait_recv()
            if h + 1 < hops:
                w_minus[h + 1] = send(two(h), two(h + 1), down)

    def take(h, p):
        for k, (dz, got, onward) in enumerate(((-h, z_plus, up), (h, z_minus, down))):
            got[h, p].wait_recv()
            if h + 2 == hops and p == 2:
                continue
            if h + 1 < hops:
                got[h + 1, p] = send(piece(dz, p), piece(-h - 1 if k == 0 else h + 1, p), onward)
            elif h + 1 == hops:
                got[hops, p] = send(piece(dz, p, k * quarter, quarter), piece(hops, p, k * quarter, quarter), onward)
        if h + 1 == hops and p == 0:
            z_plus[h, 2] = send(piece(1 - h, 2), piece(-h, 2), up)
            z_minus[h, 2] = send(piece(h - 1, 2), piece(h, 2), down)
        if p == 0:
            for dz in (-h, h)[: 1 if h == hops else 2]:
                post[dz] = send(s_raw.at[rel(dz, 0), hi], s_raw.at[rel(dz, 1), hi], mate)

    def take_post(h):
        for dz in (-h, h)[: 1 if h == hops else 2]:
            post[dz].wait_recv()

    def lines_of(dist):
        return (0, 1) if dist == 0 else (2 * dist - 1, 2)

    def bring(dist):
        first, places = lines_of(dist)
        compact(dist)
        norm_lines(2 * first, places)
        table_copy(dist).start()
        norm_lines(2 * first + places, places)
        table_copy(dist).wait()

    for h in range(1, hops):
        take_tables(h)
        take(h, 0)
        take(h, 1)
        bring(h - 1)
        builds(*lines_of(h - 1), (0, 2), True, False)
        if h == 2:
            w_far.wait_recv()
            far_table = pltpu.make_async_copy(tabf, tabf_sm, loc.at[3])
            far_table.start()
            f_far.wait_recv()

            def far_unit(i, _):
                for w in range(sb):
                    f_hi[w], f_lo[w] = unit(f_raw[w], True)
                return 0

            lax.fori_loop(0, 1, far_unit, 0)
            far_table.wait()
            rf0[...] = lax.fori_loop(0, sb // 4, far_tiles, jnp.zeros((8, N), F32))
            mass_pair.wait_recv()
            mass_diagonal = send(tmass.at[1], tmass.at[3], partner)
        if h < hops - 1:
            take(h, 2)
            take_post(h)
    t_pair.wait_recv()
    t_diagonal = send(t_raw.at[1], t_raw.at[3], partner)
    norm_t(1)
    take_tables(hops)
    take(hops, 0)
    t_diagonal.wait_recv()
    norm_t(3)
    builds(0, 2 * hops - 3, (1, 3), False, True)
    take(hops - 1, 2)
    take_post(hops - 1)
    bring(hops - 1)
    compact(hops)
    builds(*lines_of(hops - 1), range(TARGETS), True, True)
    table_copy(hops).start()
    take(hops, 1)
    table_copy(hops).wait()
    norm_lines(2 * (nz - 1), 1)
    last_build(0)
    take(hops, 2)
    take_post(hops)
    norm_lines(2 * nz - 1, 1)
    last_build(1)

    others = [(dz, bx) for dz in range(nz) for bx in range(2) if (dz, bx) != (0, 0)]
    others.sort(key=lambda o: -min(o[0], nz - o[0]))

    def exchange(src, dst, k, to_dev):
        return pltpu.make_async_remote_copy(
            src_ref=src, dst_ref=dst, send_sem=ex_snd.at[k], recv_sem=ex_rcv.at[k],
            device_id=to_dev, device_id_type=MESH)

    def group(j):
        return (lax.rem(nz - j, nz), j), (j + 1, j + 1)

    def spread(v, r):
        h, l = halves(v)
        return jnp.where(sub16 == r, h, jnp.where(sub16 == r + 8, l, 0.0)).astype(BF16)

    def product(lhs, tiles):
        o = nn(jnp.concatenate([v for v in lhs for _ in range(2)], axis=1), tiles)
        return o[:8] + o[8:]

    def rows_pass(rp, rpi, rf):
        def body(r0, _):
            j = hops - 1 - r0
            for dz, dist in group(j):
                for bx in range(2):
                    r = dz * 2 + bx
                    lhs = []
                    for t in range(TARGETS):
                        for u in range(CAP):
                            b, q = tabs_sm[dist, u, lane_of(r, t)], tabs_sm[dist, CAP + u, lane_of(r, t)]
                            lhs.append(spread(ts[t, pl.ds(jnp.maximum(q, 0), 1), :], b))
                    rp[r] = product(lhs, k_row[r])
            for dz, _ in group(j):
                send_rows(rp, rpi, dz)
            return 0

        lax.fori_loop(0, hops, body, 0)
        lhs = [spread(ts[0, pl.ds(tabf_sm[2 * CAP, f], 1), :], f) for f in range(sb)]
        rf[...] = product(lhs, kf_row[...])

    def cols_pass(so, ss, sf, far_copy):
        def body(j, accs):
            accs = list(accs)
            for dz, _ in group(j):
                for bx in range(2):
                    copy = from_line(so, ss, ag_snd, ag_rcv, dz, bx, True)
                    if bx == 0:
                        pl.when(dz > 0)(copy.wait_recv)
                    else:
                        copy.wait_recv()
            for dz, _ in group(j):
                for bx in range(2):
                    ssl[dz * 2 + bx] = ss[dz * 2 + bx]
            slots = [(t, u) for t in range(TARGETS) for u in range(CAP)]
            for dz, dist in group(j):
                for bx in range(2):
                    r = dz * 2 + bx
                    lhs = []
                    for k, (t, u) in enumerate(slots):
                        b = tabs_sm[dist, u, lane_of(r, t)]
                        lhs.append(spread(ssl[r, pl.ds(jnp.maximum(b, 0), 1), :], k))
                    o = product(lhs, k_col[r])
                    for k, (t, u) in enumerate(slots):
                        q = tabs_sm[dist, CAP + u, lane_of(r, t)]
                        accs[t] = accs[t] + jnp.where(sub32 == q, o[k : k + 1], 0.0)
            return tuple(accs)

        zero = jnp.zeros((tb_dev, N), F32)
        first = zero
        far_copy.wait_recv()
        lhs = [spread(sf[f : f + 1, :], f) for f in range(sb)]
        o = product(lhs, kf_col[...])
        for f in range(sb):
            first = first + jnp.where(sub32 == tabf_sm[2 * CAP, f], o[f : f + 1], 0.0)
        return list(lax.fori_loop(0, hops, body, (first,) + (zero,) * (TARGETS - 1)))

    mass_core.wait_recv()
    mass_diagonal.wait_recv()
    for it, (rp, rpi, rf, rfi, so, ss, sf, co, ci, wo, wi) in enumerate((
        (rp0, rpi0, rf0, rfi0, so0, ss0, sf0, co0, ci0, wo0, wi0),
        (rp1, rpi1, rf1, rfi1, so1, ss1, sf1, co1, ci1, wo1, wi1),
    )):
        last = it == ITERS - 1
        far_rows = exchange(rf, rfi, 0, behind)
        far_scale = exchange(so, sf, 1, ahead)
        if it > 0:
            rows_pass(rp, rpi, rf)
        far_rows.start()
        total = rp[0]
        for o in others[::-1]:
            from_line(rp, rpi, rs_snd, rs_rcv, *o).wait_recv()
        far_rows.wait_recv()
        total = total + rfi[...]
        for o in others:
            total = total + rpi[rel(*o)]
        scale = smass[...] / (DUSTBIN + total)
        so[...] = scale
        ss[0] = scale
        if last:
            out[:sb] = scale
        for o in others:
            to_line(so, ss, ag_snd, ag_rcv, *o, True).start()
        far_scale.start()
        accs = cols_pass(so, ss, sf, far_scale)
        theirs = pl.ds(2, 2) if last else pl.ds(0, TARGETS)
        for t in range(2 if last else 0, TARGETS):
            co[t] = accs[t]
        cores = exchange(co.at[theirs], ci.at[theirs], 2 + 2 * it, partner)
        cores.start()
        for left, sem in ((rp, rs_snd), (ss, ag_snd)):
            pltpu.make_async_copy(left.at[pl.ds(1, nr - 1)], left.at[pl.ds(1, nr - 1)], sem.at[0]).wait()
        far_rows.wait_send()
        far_scale.wait_send()
        cores.wait_recv()
        sums = [accs[t] + ci[t ^ 2] for t in range(2 if last else TARGETS)]
        moving = pl.ds(1, 1) if last else pl.ds(0, TARGETS)
        for t in (1,) if last else range(TARGETS):
            wo[t] = sums[t]
        swap = exchange(wo.at[moving], wi.at[moving], 3 + 2 * it, pair)
        swap.start()
        swap.wait_recv()
        if last:
            out[sb:] = tmass[0] / (DUSTBIN + (sums[0] + wi[1]))
        else:
            for t in range(TARGETS):
                ts[t] = tmass[t] / (DUSTBIN + (sums[t] + wi[t ^ 1]))
        cores.wait_send()
        swap.wait_send()
    others_part = pl.ds(1, TARGETS - 1)
    for k, left in enumerate((s_raw, t_raw.at[others_part], tabs, tmass.at[others_part])):
        pltpu.make_async_copy(left, left, snd.at[k]).wait()
    assert count[0] == COPIES


def local(ng, nz, semb, temb, smass, tmass, cdev, cblk):
    sb, tb = semb.shape[0], temb.shape[0]
    nr = 2 * nz
    slots = TARGETS * CAP * 2 * N
    vm = pltpu.VMEM
    dma = pltpu.SemaphoreType.DMA
    tile = (N, N)
    blocks = vm((nr, sb, N), F32)
    source, targets = vm((sb, N), F32), vm((TARGETS, tb, N), F32)
    scratch = [
        vm((nr, sb) + tile, F32), vm((TARGETS, tb) + tile, F32), vm((sb,) + tile, F32),
        vm((nr * sb,) + tile, BF16), vm((nr * sb,) + tile, BF16),
        vm((TARGETS, tb) + tile, BF16), vm((TARGETS, tb) + tile, BF16),
        vm((sb,) + tile, BF16), vm((sb,) + tile, BF16),
        vm((nr, slots, N), BF16), vm((nr, slots, N), BF16),
        vm((sb * 2 * N, N), BF16), vm((sb * 2 * N, N), BF16),
        vm((8, N), I32), vm((nr, 8, N), I32), vm((8, N), I32), vm((nz // 2 + 1, 8, N), I32),
        pltpu.SMEM((nz // 2 + 1, 8, N), I32), pltpu.SMEM((8, N), I32),
    ]
    scratch += [blocks] * 7 + [source] * 8 + [targets] * 9
    scratch += [vm(a.shape, a.dtype) for a in (smass, cdev, cblk)] + [targets]
    scratch += [dma((4,)), dma((COPIES,)), dma((1,)), dma((nr,)), dma((1,)), dma((nr,))] + [dma((6,))] * 2 + [dma((8,))]
    any_, vmem = pl.BlockSpec(memory_space=pl.ANY), pl.BlockSpec(memory_space=pltpu.VMEM)
    both = pl.pallas_call(
        functools.partial(kernel, ng, nz, sb, tb),
        out_shape=jax.ShapeDtypeStruct((sb + tb, N), F32),
        in_specs=[any_] * 6,
        out_specs=vmem,
        scratch_shapes=scratch,
        compiler_params=pltpu.CompilerParams(
            collective_id=0, has_side_effects=True, vmem_limit_bytes=VMEM_BYTES),
        name="sinkhorn",
    )(semb, temb, smass, tmass, cdev, cblk)

    def split(both_ref, src_ref, tgt_ref):
        src_ref[...] = both_ref[:sb]
        tgt_ref[...] = both_ref[sb:]

    return pl.pallas_call(
        split,
        out_shape=(jax.ShapeDtypeStruct(smass.shape, F32), jax.ShapeDtypeStruct(tmass.shape, F32)),
        in_specs=[vmem],
        out_specs=(vmem, vmem),
        name="split",
    )(both)


def solution(mesh):
    placed = (
        P(("group", "dev"), None, None),
        P(("group", "dev"), None, None),
        P(("group", "dev"), None),
        P(("group", "dev"), None),
        P(("group", "dev"), None),
        P(("group", "dev"), None),
    )
    ng, nz = mesh.shape["group"], mesh.shape["dev"] // (2 * NX)
    return jax.shard_map(
        functools.partial(local, ng, nz),
        mesh=mesh,
        in_specs=placed,
        out_specs=(P(("group", "dev"), None), P(("group", "dev"), None)),
        check_vma=False,
    )
```

```python
import functools

import jax
import jax.numpy as jnp
from jax import lax
from jax.experimental import pallas as pl
from jax.experimental.pallas import tpu as pltpu
from jax.sharding import PartitionSpec as P

MESH = pl.DeviceIdType.MESH
N = 128
NX = 4
NEAR = 7
CAP = 2
TARGETS = 4
VMEM_BYTES = 62 * 1024 * 1024
ITERS = 2
EMPTY = -64
COPIES = 49
DUSTBIN = 0.5
EPSILON = 1e-6
GAIN = 1.0 / (N * 0.1)
SHARE = 1.0 / (8.0 * N)

F32, BF16, I32 = jnp.float32, jnp.bfloat16, jnp.int32


def nn(a, b):
    return lax.dot_general(a, b, (((1,), (0,)), ((), ())), preferred_element_type=F32)


def halves(v):
    hi = v.astype(BF16).astype(F32)
    return hi, v - hi


def kernel(ng, nz, sb, tb_dev, *refs):
    (semb, temb, smass_in, tmass_in, cdev_in, cblk_in, out,
     s_raw, t_raw, f_raw, s_hi, s_lo, t_hi, t_lo, f_hi, f_lo, k_row, k_col, kf_row, kf_col,
     tab, tabs, tabf, tabc, tabs_sm, tabf_sm,
     rp0, rp1, rpi0, rpi1, ss0, ss1, ssl, rf0, rf1, rfi0, rfi1, so0, so1, sf0, sf1,
     co0, co1, ci0, ci1, wo0, wo1, wi0, wi1, ts, smass, cdev, cblk, tmass,
     snd, rcv, rs_snd, rs_rcv, ag_snd, ag_rcv, ex_snd, ex_rcv, loc) = refs
    nr = 2 * nz
    hops = nz // 2
    half = sb // 2
    quarter = sb // 4
    line = 2 * NX
    g, d = lax.axis_index("group"), lax.axis_index("dev")
    z, x, c = d // line, (d // 2) % NX, d % 2

    def at(zz, xx, cc):
        return (g, zz * line + xx * 2 + cc)

    def dev(dz, bx):
        return at(lax.rem(z + dz, nz), NX - 1 - x if bx else x, c)

    def rel(dz, bx):
        return (dz % nz) * 2 + bx

    up, down, mate = dev(1, 0), dev(nz - 1, 0), dev(0, 1)
    partner = at(z, x, 1 - c)
    pair = at(z, x + 1 - 2 * lax.rem(x, 2), c)
    ahead, behind = (lax.rem(g + 1, ng), d), (lax.rem(g + ng - 1, ng), d)

    count = [0]

    def kind(src):
        if src.dtype == I32:
            return 2
        if len(src.shape) == 2:
            return 3
        return 1 if src.shape[0] == tb_dev else 0

    def send(src, dst, to_dev):
        k = count[0]
        count[0] += 1
        copy = pltpu.make_async_remote_copy(
            src_ref=src, dst_ref=dst, send_sem=snd.at[kind(src)], recv_sem=rcv.at[k],
            device_id=to_dev, device_id_type=MESH)
        copy.start()
        return copy

    barrier = pltpu.get_barrier_semaphore()
    greeted = (up, down, mate, pair, partner, ahead, behind)
    for other in greeted:
        pl.semaphore_signal(barrier, inc=1, device_id=other, device_id_type=MESH)
    own_s = pltpu.make_async_copy(semb, s_raw.at[0], loc.at[0])
    own_t = pltpu.make_async_copy(temb, t_raw.at[0], loc.at[1])
    small = [pltpu.make_async_copy(a, b, loc.at[4 + i]) for i, (a, b) in enumerate(
        ((cdev_in, cdev), (cblk_in, cblk), (smass_in, smass), (tmass_in, tmass.at[0])))]
    for copy in small:
        copy.start()
    own_s.start()
    own_t.start()
    for copy in small:
        copy.wait()

    lane = lax.broadcasted_iota(I32, (1, N), 1)
    run = jnp.zeros((1, N), I32)
    rows = [jnp.full((1, N), EMPTY, I32) for _ in range(2 * CAP)]
    far = jnp.zeros((1, N), I32)
    for b in range(sb):
        hit = jnp.zeros((1, N), I32)
        which = jnp.zeros((1, N), I32)
        for k in range(NEAR):
            m = cdev[b : b + 1, k : k + 1] == lane
            hit = jnp.where(m, 1, hit)
            which = jnp.where(m, cblk[b : b + 1, k : k + 1], which)
        for u in range(CAP):
            m = (hit == 1) & (run == u)
            rows[u] = jnp.where(m, b, rows[u])
            rows[CAP + u] = jnp.where(m, which, rows[CAP + u])
        run = run + hit
        far = jnp.where(lane == b, cblk[b : b + 1, NEAR : NEAR + 1], far)
    table = jnp.concatenate(rows + [far] + [jnp.zeros((1, N), I32)] * (7 - 2 * CAP), axis=0)
    tab[...] = table
    tabs[0] = table

    pl.semaphore_wait(barrier, len(greeted))

    lo, hi = pl.ds(0, half), pl.ds(half, half)
    pieces = ((0, half), (0, 0), (1, 0))
    z_plus, z_minus = {}, {}

    def piece(dz, p, start=0, size=half):
        bx, first = pieces[p]
        return s_raw.at[rel(dz, bx), pl.ds(first + start, size)]

    w_mate = send(tab, tabs.at[1], mate)
    pre = send(semb.at[lo], s_raw.at[rel(0, 1), lo], mate)
    for p in (0, 1):
        part = semb.at[pl.ds(pieces[p][1], half)]
        z_plus[1, p] = send(part, piece(-1, p), up)
        z_minus[1, p] = send(part, piece(1, p), down)
    post = {0: send(semb.at[hi], s_raw.at[rel(0, 1), hi], mate)}
    t_pair = send(temb, t_raw.at[1], pair)
    mass_pair = send(tmass_in, tmass.at[1], pair)
    t_core = send(temb, t_raw.at[2], partner)
    mass_core = send(tmass_in, tmass.at[2], partner)
    w_far = send(tab, tabf, ahead)
    f_far = send(semb, f_raw, ahead)
    w_plus, w_minus = {}, {}

    def two(dz):
        return tabs.at[pl.ds(rel(dz, 0), 2)]

    def place(p):
        dist = (p + 1) // 2
        return jnp.where(p % 2 == 1, dist, lax.rem(nz - dist, nz)), dist

    def unit(v, turned):
        if turned:
            v = v.T
        v = v * lax.rsqrt(jnp.mean(v * v, axis=0 if turned else 1, keepdims=True) + EPSILON)
        h = v.astype(BF16)
        return h, (v - h.astype(F32)).astype(BF16)

    def norm_lines(first_line, lines):
        def one(i, _):
            dz, _dist = place((first_line + i) // 2)
            r = dz * 2 + (first_line + i) % 2
            for w in range(sb):
                s_hi[r * sb + w], s_lo[r * sb + w] = unit(s_raw[r, w], True)
            return 0

        lax.fori_loop(0, lines, one, 0)

    def norm_t(t):
        def one(i, _):
            for w in range(8):
                t_hi[t, i * 8 + w], t_lo[t, i * 8 + w] = unit(t_raw[t, i * 8 + w], False)
            return 0

        lax.fori_loop(0, tb_dev // 8, one, 0)

    w_mate.wait_recv()
    w_plus[1] = send(two(0), two(-1), up)
    w_minus[1] = send(two(0), two(1), down)
    pre.wait_recv()
    z_plus[1, 2] = send(piece(0, 2), piece(-1, 2), up)
    z_minus[1, 2] = send(piece(0, 2), piece(1, 2), down)
    own_t.wait()
    norm_t(0)
    t_core.wait_recv()
    norm_t(2)
    own_s.wait()

    sub8 = lax.broadcasted_iota(I32, (8, N), 0)
    sub16 = lax.broadcasted_iota(I32, (16, N), 0)
    sub32 = lax.broadcasted_iota(I32, (tb_dev, N), 0)

    def lane_of(r, t):
        return r * 4 + lax.rem(x + t, 2) * 2 + (c if t < 2 else 1 - c)

    def two_terms(v, ref, k):
        h = v.astype(BF16)
        ref[pl.ds(k * 2 * N, N), :] = h
        ref[pl.ds(k * 2 * N + N, N), :] = (v - h.astype(F32)).astype(BF16)

    def tile(b_hi, b_lo, a_hi, a_lo, row, col, k):
        dots = nn(b_hi, a_hi) + (nn(b_lo, a_hi) + nn(b_hi, a_lo))
        e = jnp.exp(dots * GAIN) * SHARE
        two_terms(e, row, k)
        two_terms(e.T, col, k)
        return jnp.sum(e, axis=0, keepdims=True)

    def to_line(src, dst, snds, rcvs, dz, bx, whole=False):
        r, back = dz * 2 + bx, lax.rem(nz - dz, nz) * 2 + bx
        return pltpu.make_async_remote_copy(
            src_ref=src if whole else src.at[r], dst_ref=dst.at[back], send_sem=snds.at[0],
            recv_sem=rcvs.at[back], device_id=dev(dz, bx), device_id_type=MESH)

    def from_line(src, dst, snds, rcvs, dz, bx, whole=False):
        r = dz * 2 + bx
        return pltpu.make_async_remote_copy(
            src_ref=src if whole else src.at[r], dst_ref=dst.at[r], send_sem=snds.at[0],
            recv_sem=rcvs.at[r], device_id=dev(dz, bx), device_id_type=MESH)

    def send_rows(rp, rpi, dz, bxs=(0, 1)):
        for bx in bxs:
            copy = to_line(rp, rpi, rs_snd, rs_rcv, dz, bx)
            if bx == 0:
                pl.when(dz > 0)(copy.start)
            else:
                copy.start()

    def build(dz, dist, bxs, targets, first, done):
        for bx in bxs:
            r = dz * 2 + bx
            acc = jnp.zeros((8, N), F32)
            for t in targets:
                for u in range(CAP):
                    b, q = tabs_sm[dist, u, lane_of(r, t)], tabs_sm[dist, CAP + u, lane_of(r, t)]
                    s, w = r * sb + jnp.maximum(b, 0), jnp.maximum(q, 0)
                    sums = tile(t_hi[t, w], t_lo[t, w], s_hi[s], s_lo[s], k_row.at[r], k_col.at[r], t * CAP + u)
                    acc = acc + jnp.where(sub8 == b, sums, 0.0)
            rp0[r] = acc if first else rp0[r] + acc
        if done:
            send_rows(rp0, rpi0, dz, bxs)

    def builds(first_place, places, targets, first, done):
        def one(i, _):
            dz, dist = place(first_place + i)
            build(dz, dist, (0, 1), targets, first, done)
            return 0

        lax.fori_loop(0, places, one, 0)

    def last_build(bx):
        def one(i, _):
            build(hops + i, hops, (bx,), range(TARGETS), True, True)
            return 0

        lax.fori_loop(0, 1, one, 0)

    lane8 = lax.broadcasted_iota(I32, (8, N), 1)

    def compact(dist):
        part = jnp.zeros((8, N), I32)
        for dz in (0,) if dist == 0 else (hops,) if dist == hops else (-dist, dist):
            for bx in range(2):
                r = rel(dz, bx)
                moved = pltpu.roll(tabs[r], lax.rem(r * 4 + N - z * line - (x // 2) * 4, N), 1)
                part = jnp.where(lane8 // 4 == r, moved, part)
        tabc[dist] = part

    def table_copy(dist):
        return pltpu.make_async_copy(tabc.at[dist], tabs_sm.at[dist], loc.at[2])

    def far_tiles(f0, acc):
        for ff in range(4):
            f = f0 * 4 + ff
            w = tabf_sm[2 * CAP, f]
            sums = tile(t_hi[0, w], t_lo[0, w], f_hi[f], f_lo[f], kf_row, kf_col, f)
            acc = acc + jnp.where(sub8 == f, sums, 0.0)
        return acc

    def take_tables(h):
        w_plus[h].wait_recv()
        if h < hops:
            w_plus[h + 1] = send(two(-h), two(-h - 1), up)
            w_minus[h].wait_recv()
            if h + 1 < hops:
                w_minus[h + 1] = send(two(h), two(h + 1), down)

    def take(h, p):
        for k, (dz, got, onward) in enumerate(((-h, z_plus, up), (h, z_minus, down))):
            got[h, p].wait_recv()
            if h + 2 == hops and p == 2:
                continue
            if h + 1 < hops:
                got[h + 1, p] = send(piece(dz, p), piece(-h - 1 if k == 0 else h + 1, p), onward)
            elif h + 1 == hops:
                got[hops, p] = send(piece(dz, p, k * quarter, quarter), piece(hops, p, k * quarter, quarter), onward)
        if h + 1 == hops and p == 0:
            z_plus[h, 2] = send(piece(1 - h, 2), piece(-h, 2), up)
            z_minus[h, 2] = send(piece(h - 1, 2), piece(h, 2), down)
        if p == 0:
            for dz in (-h, h)[: 1 if h == hops else 2]:
                post[dz] = send(s_raw.at[rel(dz, 0), hi], s_raw.at[rel(dz, 1), hi], mate)

    def take_post(h):
        for dz in (-h, h)[: 1 if h == hops else 2]:
            post[dz].wait_recv()

    def lines_of(dist):
        return (0, 1) if dist == 0 else (2 * dist - 1, 2)

    def bring(dist):
        first, places = lines_of(dist)
        compact(dist)
        norm_lines(2 * first, places)
        table_copy(dist).start()
        norm_lines(2 * first + places, places)
        table_copy(dist).wait()

    for h in range(1, hops):
        take(h, 0)
        take_tables(h)
        take(h, 1)
        if h == 1:
            post[0].wait_recv()
        bring(h - 1)
        builds(*lines_of(h - 1), (0, 2), True, False)
        if h == 2:
            w_far.wait_recv()
            far_table = pltpu.make_async_copy(tabf, tabf_sm, loc.at[3])
            far_table.start()
            f_far.wait_recv()

            def far_unit(i, _):
                for w in range(sb):
                    f_hi[w], f_lo[w] = unit(f_raw[w], True)
                return 0

            lax.fori_loop(0, 1, far_unit, 0)
            far_table.wait()
            rf0[...] = lax.fori_loop(0, sb // 4, far_tiles, jnp.zeros((8, N), F32))
            mass_pair.wait_recv()
            mass_diagonal = send(tmass.at[1], tmass.at[3], partner)
        if h < hops - 1:
            take(h, 2)
            take_post(h)
    t_pair.wait_recv()
    t_diagonal = send(t_raw.at[1], t_raw.at[3], partner)
    norm_t(1)
    take(hops, 0)
    take_tables(hops)
    t_diagonal.wait_recv()
    norm_t(3)
    builds(0, 2 * hops - 3, (1, 3), False, True)
    take(hops - 1, 2)
    take_post(hops - 1)
    bring(hops - 1)
    compact(hops)
    builds(*lines_of(hops - 1), range(TARGETS), True, True)
    table_copy(hops).start()
    take(hops, 1)
    table_copy(hops).wait()
    norm_lines(2 * (nz - 1), 1)
    last_build(0)
    take(hops, 2)
    take_post(hops)
    norm_lines(2 * nz - 1, 1)
    last_build(1)

    others = [(dz, bx) for dz in range(nz) for bx in range(2) if (dz, bx) != (0, 0)]
    others.sort(key=lambda o: -min(o[0], nz - o[0]))

    def exchange(src, dst, k, to_dev):
        return pltpu.make_async_remote_copy(
            src_ref=src, dst_ref=dst, send_sem=ex_snd.at[k], recv_sem=ex_rcv.at[k],
            device_id=to_dev, device_id_type=MESH)

    def group(j):
        return (lax.rem(nz - j, nz), j), (j + 1, j + 1)

    def spread(v, r):
        h, l = halves(v)
        return jnp.where(sub16 == r, h, jnp.where(sub16 == r + 8, l, 0.0)).astype(BF16)

    def product(lhs, tiles):
        o = nn(jnp.concatenate([v for v in lhs for _ in range(2)], axis=1), tiles)
        return o[:8] + o[8:]

    def rows_pass(rp, rpi, rf):
        def body(r0, _):
            j = hops - 1 - r0
            for dz, dist in group(j):
                for bx in range(2):
                    r = dz * 2 + bx
                    lhs = []
                    for t in range(TARGETS):
                        for u in range(CAP):
                            b, q = tabs_sm[dist, u, lane_of(r, t)], tabs_sm[dist, CAP + u, lane_of(r, t)]
                            lhs.append(spread(ts[t, pl.ds(jnp.maximum(q, 0), 1), :], b))
                    rp[r] = product(lhs, k_row[r])
            for dz, _ in group(j):
                send_rows(rp, rpi, dz)
            return 0

        lax.fori_loop(0, hops, body, 0)
        lhs = [spread(ts[0, pl.ds(tabf_sm[2 * CAP, f], 1), :], f) for f in range(sb)]
        rf[...] = product(lhs, kf_row[...])

    def cols_pass(so, ss, sf, far_copy):
        def body(j, accs):
            accs = list(accs)
            for dz, _ in group(j):
                for bx in range(2):
                    copy = from_line(so, ss, ag_snd, ag_rcv, dz, bx, True)
                    if bx == 0:
                        pl.when(dz > 0)(copy.wait_recv)
                    else:
                        copy.wait_recv()
            for dz, _ in group(j):
                for bx in range(2):
                    ssl[dz * 2 + bx] = ss[dz * 2 + bx]
            slots = [(t, u) for t in range(TARGETS) for u in range(CAP)]
            for dz, dist in group(j):
                for bx in range(2):
                    r = dz * 2 + bx
                    lhs = []
                    for k, (t, u) in enumerate(slots):
                        b = tabs_sm[dist, u, lane_of(r, t)]
                        lhs.append(spread(ssl[r, pl.ds(jnp.maximum(b, 0), 1), :], k))
                    o = product(lhs, k_col[r])
                    for k, (t, u) in enumerate(slots):
                        q = tabs_sm[dist, CAP + u, lane_of(r, t)]
                        accs[t] = accs[t] + jnp.where(sub32 == q, o[k : k + 1], 0.0)
            return tuple(accs)

        zero = jnp.zeros((tb_dev, N), F32)
        first = zero
        far_copy.wait_recv()
        lhs = [spread(sf[f : f + 1, :], f) for f in range(sb)]
        o = product(lhs, kf_col[...])
        for f in range(sb):
            first = first + jnp.where(sub32 == tabf_sm[2 * CAP, f], o[f : f + 1], 0.0)
        return list(lax.fori_loop(0, hops, body, (first,) + (zero,) * (TARGETS - 1)))

    mass_core.wait_recv()
    mass_diagonal.wait_recv()
    for it, (rp, rpi, rf, rfi, so, ss, sf, co, ci, wo, wi) in enumerate((
        (rp0, rpi0, rf0, rfi0, so0, ss0, sf0, co0, ci0, wo0, wi0),
        (rp1, rpi1, rf1, rfi1, so1, ss1, sf1, co1, ci1, wo1, wi1),
    )):
        last = it == ITERS - 1
        far_rows = exchange(rf, rfi, 0, behind)
        far_scale = exchange(so, sf, 1, ahead)
        if it > 0:
            rows_pass(rp, rpi, rf)
        far_rows.start()
        total = rp[0]
        for o in others[::-1]:
            from_line(rp, rpi, rs_snd, rs_rcv, *o).wait_recv()
        far_rows.wait_recv()
        total = total + rfi[...]
        for o in others:
            total = total + rpi[rel(*o)]
        scale = smass[...] / (DUSTBIN + total)
        so[...] = scale
        ss[0] = scale
        if last:
            out[:sb] = scale
        for o in others:
            to_line(so, ss, ag_snd, ag_rcv, *o, True).start()
        far_scale.start()
        accs = cols_pass(so, ss, sf, far_scale)
        theirs = pl.ds(2, 2) if last else pl.ds(0, TARGETS)
        for t in range(2 if last else 0, TARGETS):
            co[t] = accs[t]
        cores = exchange(co.at[theirs], ci.at[theirs], 2 + 2 * it, partner)
        cores.start()
        for left, sem in ((rp, rs_snd), (ss, ag_snd)):
            pltpu.make_async_copy(left.at[pl.ds(1, nr - 1)], left.at[pl.ds(1, nr - 1)], sem.at[0]).wait()
        far_rows.wait_send()
        far_scale.wait_send()
        cores.wait_recv()
        sums = [accs[t] + ci[t ^ 2] for t in range(2 if last else TARGETS)]
        moving = pl.ds(1, 1) if last else pl.ds(0, TARGETS)
        for t in (1,) if last else range(TARGETS):
            wo[t] = sums[t]
        swap = exchange(wo.at[moving], wi.at[moving], 3 + 2 * it, pair)
        swap.start()
        swap.wait_recv()
        if last:
            out[sb:] = tmass[0] / (DUSTBIN + (sums[0] + wi[1]))
        else:
            for t in range(TARGETS):
                ts[t] = tmass[t] / (DUSTBIN + (sums[t] + wi[t ^ 1]))
        cores.wait_send()
        swap.wait_send()
    others_part = pl.ds(1, TARGETS - 1)
    for k, left in enumerate((s_raw, t_raw.at[others_part], tabs, tmass.at[others_part])):
        pltpu.make_async_copy(left, left, snd.at[k]).wait()
    assert count[0] == COPIES


def local(ng, nz, semb, temb, smass, tmass, cdev, cblk):
    sb, tb = semb.shape[0], temb.shape[0]
    nr = 2 * nz
    slots = TARGETS * CAP * 2 * N
    vm = pltpu.VMEM
    dma = pltpu.SemaphoreType.DMA
    tile = (N, N)
    blocks = vm((nr, sb, N), F32)
    source, targets = vm((sb, N), F32), vm((TARGETS, tb, N), F32)
    scratch = [
        vm((nr, sb) + tile, F32), vm((TARGETS, tb) + tile, F32), vm((sb,) + tile, F32),
        vm((nr * sb,) + tile, BF16), vm((nr * sb,) + tile, BF16),
        vm((TARGETS, tb) + tile, BF16), vm((TARGETS, tb) + tile, BF16),
        vm((sb,) + tile, BF16), vm((sb,) + tile, BF16),
        vm((nr, slots, N), BF16), vm((nr, slots, N), BF16),
        vm((sb * 2 * N, N), BF16), vm((sb * 2 * N, N), BF16),
        vm((8, N), I32), vm((nr, 8, N), I32), vm((8, N), I32), vm((nz // 2 + 1, 8, N), I32),
        pltpu.SMEM((nz // 2 + 1, 8, N), I32), pltpu.SMEM((8, N), I32),
    ]
    scratch += [blocks] * 7 + [source] * 8 + [targets] * 9
    scratch += [vm(a.shape, a.dtype) for a in (smass, cdev, cblk)] + [targets]
    scratch += [dma((4,)), dma((COPIES,)), dma((1,)), dma((nr,)), dma((1,)), dma((nr,))] + [dma((6,))] * 2 + [dma((8,))]
    any_, vmem = pl.BlockSpec(memory_space=pl.ANY), pl.BlockSpec(memory_space=pltpu.VMEM)
    both = pl.pallas_call(
        functools.partial(kernel, ng, nz, sb, tb),
        out_shape=jax.ShapeDtypeStruct((sb + tb, N), F32),
        in_specs=[any_] * 6,
        out_specs=vmem,
        scratch_shapes=scratch,
        compiler_params=pltpu.CompilerParams(
            collective_id=0, has_side_effects=True, vmem_limit_bytes=VMEM_BYTES),
        name="sinkhorn",
    )(semb, temb, smass, tmass, cdev, cblk)

    def split(both_ref, src_ref, tgt_ref):
        src_ref[...] = both_ref[:sb]
        tgt_ref[...] = both_ref[sb:]

    return pl.pallas_call(
        split,
        out_shape=(jax.ShapeDtypeStruct(smass.shape, F32), jax.ShapeDtypeStruct(tmass.shape, F32)),
        in_specs=[vmem],
        out_specs=(vmem, vmem),
        name="split",
    )(both)


def solution(mesh):
    placed = (
        P(("group", "dev"), None, None),
        P(("group", "dev"), None, None),
        P(("group", "dev"), None),
        P(("group", "dev"), None),
        P(("group", "dev"), None),
        P(("group", "dev"), None),
    )
    ng, nz = mesh.shape["group"], mesh.shape["dev"] // (2 * NX)
    return jax.shard_map(
        functools.partial(local, ng, nz),
        mesh=mesh,
        in_specs=placed,
        out_specs=(P(("group", "dev"), None), P(("group", "dev"), None)),
        check_vma=False,
    )
```

```python
import functools

import jax
import jax.numpy as jnp
from jax import lax
from jax.experimental import pallas as pl
from jax.experimental.pallas import tpu as pltpu
from jax.sharding import PartitionSpec as P

MESH = pl.DeviceIdType.MESH
N = 128
NX = 4
NEAR = 7
CAP = 2
TARGETS = 4
VMEM_BYTES = 62 * 1024 * 1024
ITERS = 2
EMPTY = -64
COPIES = 49
DUSTBIN = 0.5
EPSILON = 1e-6
GAIN = 1.0 / (N * 0.1)
SHARE = 1.0 / (8.0 * N)

F32, BF16, I32 = jnp.float32, jnp.bfloat16, jnp.int32


def nn(a, b):
    return lax.dot_general(a, b, (((1,), (0,)), ((), ())), preferred_element_type=F32)


def halves(v):
    hi = v.astype(BF16).astype(F32)
    return hi, v - hi


def kernel(ng, nz, sb, tb_dev, *refs):
    (semb, temb, smass_in, tmass_in, cdev_in, cblk_in, out,
     s_raw, t_raw, f_raw, s_hi, s_lo, t_hi, t_lo, f_hi, f_lo, k_row, k_col, kf_row, kf_col,
     tab, tabs, tabf, tabc, tabs_sm, tabf_sm,
     rp0, rp1, rpi0, rpi1, ss0, ss1, ssl, rf0, rf1, rfi0, rfi1, so0, so1, sf0, sf1,
     co0, co1, ci0, ci1, wo0, wo1, wi0, wi1, ts, smass, cdev, cblk, tmass,
     snd, rcv, rs_snd, rs_rcv, ag_snd, ag_rcv, ex_snd, ex_rcv, loc) = refs
    nr = 2 * nz
    hops = nz // 2
    half = sb // 2
    quarter = sb // 4
    line = 2 * NX
    g, d = lax.axis_index("group"), lax.axis_index("dev")
    z, x, c = d // line, (d // 2) % NX, d % 2

    def at(zz, xx, cc):
        return (g, zz * line + xx * 2 + cc)

    def dev(dz, bx):
        return at(lax.rem(z + dz, nz), NX - 1 - x if bx else x, c)

    def rel(dz, bx):
        return (dz % nz) * 2 + bx

    up, down, mate = dev(1, 0), dev(nz - 1, 0), dev(0, 1)
    partner = at(z, x, 1 - c)
    pair = at(z, x + 1 - 2 * lax.rem(x, 2), c)
    ahead, behind = (lax.rem(g + 1, ng), d), (lax.rem(g + ng - 1, ng), d)

    count = [0]

    def kind(src):
        if src.dtype == I32:
            return 2
        if len(src.shape) == 2:
            return 3
        return 1 if src.shape[0] == tb_dev else 0

    def send(src, dst, to_dev):
        k = count[0]
        count[0] += 1
        copy = pltpu.make_async_remote_copy(
            src_ref=src, dst_ref=dst, send_sem=snd.at[kind(src)], recv_sem=rcv.at[k],
            device_id=to_dev, device_id_type=MESH)
        copy.start()
        return copy

    barrier = pltpu.get_barrier_semaphore()
    greeted = (up, down, mate, pair, partner, ahead, behind)
    for other in greeted:
        pl.semaphore_signal(barrier, inc=1, device_id=other, device_id_type=MESH)
    own_s = pltpu.make_async_copy(semb, s_raw.at[0], loc.at[0])
    own_t = pltpu.make_async_copy(temb, t_raw.at[0], loc.at[1])
    small = [pltpu.make_async_copy(a, b, loc.at[4 + i]) for i, (a, b) in enumerate(
        ((cdev_in, cdev), (cblk_in, cblk), (smass_in, smass), (tmass_in, tmass.at[0])))]
    for copy in small:
        copy.start()
    own_s.start()
    own_t.start()
    for copy in small:
        copy.wait()

    lane = lax.broadcasted_iota(I32, (1, N), 1)
    run = jnp.zeros((1, N), I32)
    rows = [jnp.full((1, N), EMPTY, I32) for _ in range(2 * CAP)]
    far = jnp.zeros((1, N), I32)
    for b in range(sb):
        hit = jnp.zeros((1, N), I32)
        which = jnp.zeros((1, N), I32)
        for k in range(NEAR):
            m = cdev[b : b + 1, k : k + 1] == lane
            hit = jnp.where(m, 1, hit)
            which = jnp.where(m, cblk[b : b + 1, k : k + 1], which)
        for u in range(CAP):
            m = (hit == 1) & (run == u)
            rows[u] = jnp.where(m, b, rows[u])
            rows[CAP + u] = jnp.where(m, which, rows[CAP + u])
        run = run + hit
        far = jnp.where(lane == b, cblk[b : b + 1, NEAR : NEAR + 1], far)
    table = jnp.concatenate(rows + [far] + [jnp.zeros((1, N), I32)] * (7 - 2 * CAP), axis=0)
    tab[...] = table
    tabs[0] = table

    pl.semaphore_wait(barrier, len(greeted))

    lo, hi = pl.ds(0, half), pl.ds(half, half)
    pieces = ((0, half), (0, 0), (1, 0))
    z_plus, z_minus = {}, {}

    def piece(dz, p, start=0, size=half):
        bx, first = pieces[p]
        return s_raw.at[rel(dz, bx), pl.ds(first + start, size)]

    w_mate = send(tab, tabs.at[1], mate)
    pre = send(semb.at[lo], s_raw.at[rel(0, 1), lo], mate)
    for p in (0, 1):
        part = semb.at[pl.ds(pieces[p][1], half)]
        z_plus[1, p] = send(part, piece(-1, p), up)
        z_minus[1, p] = send(part, piece(1, p), down)
    post = {0: send(semb.at[hi], s_raw.at[rel(0, 1), hi], mate)}
    t_pair = send(temb, t_raw.at[1], pair)
    mass_pair = send(tmass_in, tmass.at[1], pair)
    t_core = send(temb, t_raw.at[2], partner)
    mass_core = send(tmass_in, tmass.at[2], partner)
    w_far = send(tab, tabf, ahead)
    f_far = send(semb, f_raw, ahead)
    w_plus, w_minus = {}, {}

    def two(dz):
        return tabs.at[pl.ds(rel(dz, 0), 2)]

    def place(p):
        dist = (p + 1) // 2
        return jnp.where(p % 2 == 1, dist, lax.rem(nz - dist, nz)), dist

    def unit(v, turned):
        if turned:
            v = v.T
        v = v * lax.rsqrt(jnp.mean(v * v, axis=0 if turned else 1, keepdims=True) + EPSILON)
        h = v.astype(BF16)
        return h, (v - h.astype(F32)).astype(BF16)

    def norm_lines(first_line, lines):
        def one(i, _):
            dz, _dist = place((first_line + i) // 2)
            r = dz * 2 + (first_line + i) % 2
            for w in range(sb):
                s_hi[r * sb + w], s_lo[r * sb + w] = unit(s_raw[r, w], True)
            return 0

        lax.fori_loop(0, lines, one, 0)

    def norm_t(t):
        def one(i, _):
            for w in range(8):
                t_hi[t, i * 8 + w], t_lo[t, i * 8 + w] = unit(t_raw[t, i * 8 + w], False)
            return 0

        lax.fori_loop(0, tb_dev // 8, one, 0)

    w_mate.wait_recv()
    w_plus[1] = send(two(0), two(-1), up)
    w_minus[1] = send(two(0), two(1), down)
    pre.wait_recv()
    z_plus[1, 2] = send(piece(0, 2), piece(-1, 2), up)
    z_minus[1, 2] = send(piece(0, 2), piece(1, 2), down)
    own_t.wait()
    norm_t(0)
    t_core.wait_recv()
    norm_t(2)
    own_s.wait()
    post[0].wait_recv()

    sub8 = lax.broadcasted_iota(I32, (8, N), 0)
    sub16 = lax.broadcasted_iota(I32, (16, N), 0)
    sub32 = lax.broadcasted_iota(I32, (tb_dev, N), 0)

    def lane_of(r, t):
        return r * 4 + lax.rem(x + t, 2) * 2 + (c if t < 2 else 1 - c)

    def two_terms(v, ref, k):
        h = v.astype(BF16)
        ref[pl.ds(k * 2 * N, N), :] = h
        ref[pl.ds(k * 2 * N + N, N), :] = (v - h.astype(F32)).astype(BF16)

    def tile(b_hi, b_lo, a_hi, a_lo, row, col, k):
        dots = nn(b_hi, a_hi) + (nn(b_lo, a_hi) + nn(b_hi, a_lo))
        e = jnp.exp(dots * GAIN) * SHARE
        two_terms(e, row, k)
        two_terms(e.T, col, k)
        return jnp.sum(e, axis=0, keepdims=True)

    def to_line(src, dst, snds, rcvs, dz, bx, whole=False):
        r, back = dz * 2 + bx, lax.rem(nz - dz, nz) * 2 + bx
        return pltpu.make_async_remote_copy(
            src_ref=src if whole else src.at[r], dst_ref=dst.at[back], send_sem=snds.at[0],
            recv_sem=rcvs.at[back], device_id=dev(dz, bx), device_id_type=MESH)

    def from_line(src, dst, snds, rcvs, dz, bx, whole=False):
        r = dz * 2 + bx
        return pltpu.make_async_remote_copy(
            src_ref=src if whole else src.at[r], dst_ref=dst.at[r], send_sem=snds.at[0],
            recv_sem=rcvs.at[r], device_id=dev(dz, bx), device_id_type=MESH)

    def send_rows(rp, rpi, dz, bxs=(0, 1)):
        for bx in bxs:
            copy = to_line(rp, rpi, rs_snd, rs_rcv, dz, bx)
            if bx == 0:
                pl.when(dz > 0)(copy.start)
            else:
                copy.start()

    def build(dz, dist, bxs, targets, first, done):
        for bx in bxs:
            r = dz * 2 + bx
            acc = jnp.zeros((8, N), F32)
            for t in targets:
                for u in range(CAP):
                    b, q = tabs_sm[dist, u, lane_of(r, t)], tabs_sm[dist, CAP + u, lane_of(r, t)]
                    s, w = r * sb + jnp.maximum(b, 0), jnp.maximum(q, 0)
                    sums = tile(t_hi[t, w], t_lo[t, w], s_hi[s], s_lo[s], k_row.at[r], k_col.at[r], t * CAP + u)
                    acc = acc + jnp.where(sub8 == b, sums, 0.0)
            rp0[r] = acc if first else rp0[r] + acc
        if done:
            send_rows(rp0, rpi0, dz, bxs)

    def builds(first_place, places, targets, first, done):
        def one(i, _):
            dz, dist = place(first_place + i)
            build(dz, dist, (0, 1), targets, first, done)
            return 0

        lax.fori_loop(0, places, one, 0)

    def last_build(bx):
        def one(i, _):
            build(hops + i, hops, (bx,), range(TARGETS), True, True)
            return 0

        lax.fori_loop(0, 1, one, 0)

    lane8 = lax.broadcasted_iota(I32, (8, N), 1)

    def compact(dist):
        part = jnp.zeros((8, N), I32)
        for dz in (0,) if dist == 0 else (hops,) if dist == hops else (-dist, dist):
            for bx in range(2):
                r = rel(dz, bx)
                moved = pltpu.roll(tabs[r], lax.rem(r * 4 + N - z * line - (x // 2) * 4, N), 1)
                part = jnp.where(lane8 // 4 == r, moved, part)
        tabc[dist] = part

    def table_copy(dist):
        return pltpu.make_async_copy(tabc.at[dist], tabs_sm.at[dist], loc.at[2])

    def far_tiles(f0, acc):
        for ff in range(4):
            f = f0 * 4 + ff
            w = tabf_sm[2 * CAP, f]
            sums = tile(t_hi[0, w], t_lo[0, w], f_hi[f], f_lo[f], kf_row, kf_col, f)
            acc = acc + jnp.where(sub8 == f, sums, 0.0)
        return acc

    def take_tables(h):
        w_plus[h].wait_recv()
        if h < hops:
            w_plus[h + 1] = send(two(-h), two(-h - 1), up)
            w_minus[h].wait_recv()
            if h + 1 < hops:
                w_minus[h + 1] = send(two(h), two(h + 1), down)

    def take(h, p):
        for k, (dz, got, onward) in enumerate(((-h, z_plus, up), (h, z_minus, down))):
            got[h, p].wait_recv()
            if h + 2 == hops and p == 2:
                continue
            if h + 1 < hops:
                got[h + 1, p] = send(piece(dz, p), piece(-h - 1 if k == 0 else h + 1, p), onward)
            elif h + 1 == hops:
                got[hops, p] = send(piece(dz, p, k * quarter, quarter), piece(hops, p, k * quarter, quarter), onward)
        if h + 1 == hops and p == 0:
            z_plus[h, 2] = send(piece(1 - h, 2), piece(-h, 2), up)
            z_minus[h, 2] = send(piece(h - 1, 2), piece(h, 2), down)
        if p == 0:
            for dz in (-h, h)[: 1 if h == hops else 2]:
                post[dz] = send(s_raw.at[rel(dz, 0), hi], s_raw.at[rel(dz, 1), hi], mate)

    def take_post(h):
        for dz in (-h, h)[: 1 if h == hops else 2]:
            post[dz].wait_recv()

    def lines_of(dist):
        return (0, 1) if dist == 0 else (2 * dist - 1, 2)

    def bring(dist):
        first, places = lines_of(dist)
        compact(dist)
        norm_lines(2 * first, places)
        table_copy(dist).start()
        norm_lines(2 * first + places, places)
        table_copy(dist).wait()

    for h in range(1, hops):
        take_tables(h)
        take(h, 0)
        take(h, 1)
        bring(h - 1)
        builds(*lines_of(h - 1), (0, 2), True, False)
        if h == 2:
            w_far.wait_recv()
            far_table = pltpu.make_async_copy(tabf, tabf_sm, loc.at[3])
            far_table.start()
            f_far.wait_recv()

            def far_unit(i, _):
                for w in range(sb):
                    f_hi[w], f_lo[w] = unit(f_raw[w], True)
                return 0

            lax.fori_loop(0, 1, far_unit, 0)
            far_table.wait()
            rf0[...] = lax.fori_loop(0, sb // 4, far_tiles, jnp.zeros((8, N), F32))
            mass_pair.wait_recv()
            mass_diagonal = send(tmass.at[1], tmass.at[3], partner)
        if h < hops - 1:
            take(h, 2)
            take_post(h)
    t_pair.wait_recv()
    t_diagonal = send(t_raw.at[1], t_raw.at[3], partner)
    norm_t(1)
    take_tables(hops)
    take(hops, 0)
    t_diagonal.wait_recv()
    norm_t(3)
    builds(0, 2 * hops - 3, (1, 3), False, True)
    take(hops - 1, 2)
    take_post(hops - 1)
    bring(hops - 1)
    compact(hops)
    builds(*lines_of(hops - 1), range(TARGETS), True, True)
    table_copy(hops).start()
    take(hops, 1)
    table_copy(hops).wait()
    norm_lines(2 * (nz - 1), 1)
    last_build(0)
    take(hops, 2)
    take_post(hops)
    norm_lines(2 * nz - 1, 1)
    last_build(1)

    others = [(dz, bx) for dz in range(nz) for bx in range(2) if (dz, bx) != (0, 0)]
    others.sort(key=lambda o: -min(o[0], nz - o[0]))

    def exchange(src, dst, k, to_dev):
        return pltpu.make_async_remote_copy(
            src_ref=src, dst_ref=dst, send_sem=ex_snd.at[k], recv_sem=ex_rcv.at[k],
            device_id=to_dev, device_id_type=MESH)

    def group(j):
        return (lax.rem(nz - j, nz), j), (j + 1, j + 1)

    def spread(v, r):
        h, l = halves(v)
        return jnp.where(sub16 == r, h, jnp.where(sub16 == r + 8, l, 0.0)).astype(BF16)

    def product(lhs, tiles):
        o = nn(jnp.concatenate([v for v in lhs for _ in range(2)], axis=1), tiles)
        return o[:8] + o[8:]

    def rows_pass(rp, rpi, rf):
        def body(r0, _):
            j = hops - 1 - r0
            for dz, dist in group(j):
                for bx in range(2):
                    r = dz * 2 + bx
                    lhs = []
                    for t in range(TARGETS):
                        for u in range(CAP):
                            b, q = tabs_sm[dist, u, lane_of(r, t)], tabs_sm[dist, CAP + u, lane_of(r, t)]
                            lhs.append(spread(ts[t, pl.ds(jnp.maximum(q, 0), 1), :], b))
                    rp[r] = product(lhs, k_row[r])
            for dz, _ in group(j):
                send_rows(rp, rpi, dz)
            return 0

        lax.fori_loop(0, hops, body, 0)
        lhs = [spread(ts[0, pl.ds(tabf_sm[2 * CAP, f], 1), :], f) for f in range(sb)]
        rf[...] = product(lhs, kf_row[...])

    def cols_pass(so, ss, sf, far_copy):
        def body(j, accs):
            accs = list(accs)
            slots = [(t, u) for t in range(TARGETS) for u in range(CAP)]
            for dz, dist in group(j):
                for bx in range(2):
                    copy = from_line(so, ss, ag_snd, ag_rcv, dz, bx, True)
                    if bx == 0:
                        pl.when(dz > 0)(copy.wait_recv)
                    else:
                        copy.wait_recv()
                for bx in range(2):
                    ssl[dz * 2 + bx] = ss[dz * 2 + bx]
                for bx in range(2):
                    r = dz * 2 + bx
                    lhs = []
                    for k, (t, u) in enumerate(slots):
                        b = tabs_sm[dist, u, lane_of(r, t)]
                        lhs.append(spread(ssl[r, pl.ds(jnp.maximum(b, 0), 1), :], k))
                    o = product(lhs, k_col[r])
                    for k, (t, u) in enumerate(slots):
                        q = tabs_sm[dist, CAP + u, lane_of(r, t)]
                        accs[t] = accs[t] + jnp.where(sub32 == q, o[k : k + 1], 0.0)
            return tuple(accs)

        zero = jnp.zeros((tb_dev, N), F32)
        first = zero
        far_copy.wait_recv()
        lhs = [spread(sf[f : f + 1, :], f) for f in range(sb)]
        o = product(lhs, kf_col[...])
        for f in range(sb):
            first = first + jnp.where(sub32 == tabf_sm[2 * CAP, f], o[f : f + 1], 0.0)
        return list(lax.fori_loop(0, hops, body, (first,) + (zero,) * (TARGETS - 1)))

    mass_core.wait_recv()
    mass_diagonal.wait_recv()
    for it, (rp, rpi, rf, rfi, so, ss, sf, co, ci, wo, wi) in enumerate((
        (rp0, rpi0, rf0, rfi0, so0, ss0, sf0, co0, ci0, wo0, wi0),
        (rp1, rpi1, rf1, rfi1, so1, ss1, sf1, co1, ci1, wo1, wi1),
    )):
        last = it == ITERS - 1
        far_rows = exchange(rf, rfi, 0, behind)
        far_scale = exchange(so, sf, 1, ahead)
        if it > 0:
            rows_pass(rp, rpi, rf)
        far_rows.start()
        total = rp[0]
        for o in others[::-1]:
            from_line(rp, rpi, rs_snd, rs_rcv, *o).wait_recv()
        far_rows.wait_recv()
        total = total + rfi[...]
        for o in others:
            total = total + rpi[rel(*o)]
        scale = smass[...] / (DUSTBIN + total)
        so[...] = scale
        ss[0] = scale
        if last:
            out[:sb] = scale
        for o in others:
            to_line(so, ss, ag_snd, ag_rcv, *o, True).start()
        far_scale.start()
        accs = cols_pass(so, ss, sf, far_scale)
        theirs = pl.ds(2, 2) if last else pl.ds(0, TARGETS)
        for t in range(2 if last else 0, TARGETS):
            co[t] = accs[t]
        cores = exchange(co.at[theirs], ci.at[theirs], 2 + 2 * it, partner)
        cores.start()
        for left, sem in ((rp, rs_snd), (ss, ag_snd)):
            pltpu.make_async_copy(left.at[pl.ds(1, nr - 1)], left.at[pl.ds(1, nr - 1)], sem.at[0]).wait()
        far_rows.wait_send()
        far_scale.wait_send()
        cores.wait_recv()
        sums = [accs[t] + ci[t ^ 2] for t in range(2 if last else TARGETS)]
        moving = pl.ds(1, 1) if last else pl.ds(0, TARGETS)
        for t in (1,) if last else range(TARGETS):
            wo[t] = sums[t]
        swap = exchange(wo.at[moving], wi.at[moving], 3 + 2 * it, pair)
        swap.start()
        swap.wait_recv()
        if last:
            out[sb:] = tmass[0] / (DUSTBIN + (sums[0] + wi[1]))
        else:
            for t in range(TARGETS):
                ts[t] = tmass[t] / (DUSTBIN + (sums[t] + wi[t ^ 1]))
        cores.wait_send()
        swap.wait_send()
    others_part = pl.ds(1, TARGETS - 1)
    for k, left in enumerate((s_raw, t_raw.at[others_part], tabs, tmass.at[others_part])):
        pltpu.make_async_copy(left, left, snd.at[k]).wait()
    assert count[0] == COPIES


def local(ng, nz, semb, temb, smass, tmass, cdev, cblk):
    sb, tb = semb.shape[0], temb.shape[0]
    nr = 2 * nz
    slots = TARGETS * CAP * 2 * N
    vm = pltpu.VMEM
    dma = pltpu.SemaphoreType.DMA
    tile = (N, N)
    blocks = vm((nr, sb, N), F32)
    source, targets = vm((sb, N), F32), vm((TARGETS, tb, N), F32)
    scratch = [
        vm((nr, sb) + tile, F32), vm((TARGETS, tb) + tile, F32), vm((sb,) + tile, F32),
        vm((nr * sb,) + tile, BF16), vm((nr * sb,) + tile, BF16),
        vm((TARGETS, tb) + tile, BF16), vm((TARGETS, tb) + tile, BF16),
        vm((sb,) + tile, BF16), vm((sb,) + tile, BF16),
        vm((nr, slots, N), BF16), vm((nr, slots, N), BF16),
        vm((sb * 2 * N, N), BF16), vm((sb * 2 * N, N), BF16),
        vm((8, N), I32), vm((nr, 8, N), I32), vm((8, N), I32), vm((nz // 2 + 1, 8, N), I32),
        pltpu.SMEM((nz // 2 + 1, 8, N), I32), pltpu.SMEM((8, N), I32),
    ]
    scratch += [blocks] * 7 + [source] * 8 + [targets] * 9
    scratch += [vm(a.shape, a.dtype) for a in (smass, cdev, cblk)] + [targets]
    scratch += [dma((4,)), dma((COPIES,)), dma((1,)), dma((nr,)), dma((1,)), dma((nr,))] + [dma((6,))] * 2 + [dma((8,))]
    any_, vmem = pl.BlockSpec(memory_space=pl.ANY), pl.BlockSpec(memory_space=pltpu.VMEM)
    both = pl.pallas_call(
        functools.partial(kernel, ng, nz, sb, tb),
        out_shape=jax.ShapeDtypeStruct((sb + tb, N), F32),
        in_specs=[any_] * 6,
        out_specs=vmem,
        scratch_shapes=scratch,
        compiler_params=pltpu.CompilerParams(
            collective_id=0, has_side_effects=True, vmem_limit_bytes=VMEM_BYTES),
        name="sinkhorn",
    )(semb, temb, smass, tmass, cdev, cblk)

    def split(both_ref, src_ref, tgt_ref):
        src_ref[...] = both_ref[:sb]
        tgt_ref[...] = both_ref[sb:]

    return pl.pallas_call(
        split,
        out_shape=(jax.ShapeDtypeStruct(smass.shape, F32), jax.ShapeDtypeStruct(tmass.shape, F32)),
        in_specs=[vmem],
        out_specs=(vmem, vmem),
        name="split",
    )(both)


def solution(mesh):
    placed = (
        P(("group", "dev"), None, None),
        P(("group", "dev"), None, None),
        P(("group", "dev"), None),
        P(("group", "dev"), None),
        P(("group", "dev"), None),
        P(("group", "dev"), None),
    )
    ng, nz = mesh.shape["group"], mesh.shape["dev"] // (2 * NX)
    return jax.shard_map(
        functools.partial(local, ng, nz),
        mesh=mesh,
        in_specs=placed,
        out_specs=(P(("group", "dev"), None), P(("group", "dev"), None)),
        check_vma=False,
    )
```
